256 devices in a mesh: dp: 4 (over y_hi, core), seq: 8 (over z), head: 8 (over x, y_lo).
Axes of the slice: x: 4, y: 4 (y_hi: 2, y_lo: 2; y = y_hi * 2 + y_lo), z: 8, core: 2. Of those that a mesh axis runs over, the one named last changes fastest.
Arguments:
- tokens: bfloat16 [4, 8192, 512], P('dp', ('seq', 'head')), may hold values from -800 to 800
- bin_ids: int32 [4, 8192], P('dp'), may hold values from 0 to 127, never falling along the last dimension, each value on 1 to 256 neighbouring positions
- pattern: int32 [4, 64, 9], P('dp'), may hold values from 0 to 63, as said below
- w_qkv: bfloat16 [512, 1536], replicated, may hold values from -3.2 to 3.2
- w_out: bfloat16 [512, 512], replicated, may hold values from -5 to 5
- head_bias: float32 [8], replicated, may hold values from -3 to 400
- grad_output: bfloat16 [4, 8192, 512], P('dp', ('seq', 'head')), may hold values from -6 to 6
Outputs:
- output: bfloat16 [4, 8192, 512], P('dp', ('seq', 'head'))
- grad_tokens: bfloat16 [4, 8192, 512], P('dp', ('seq', 'head'))
- grad_w_qkv: float32 [512, 1536], P(None, 'head')
- grad_w_out: float32 [512, 512], P('head')
The draws below stay inside these ranges and needn't reach their ends.
Inputs may be any that keep to these rules, and one draw needn't show every extreme that they name: `pattern`: row i of sequence b lists (i + o) mod 64 for the 9 offsets o of sequence b, in the same order in every row: 0, 1, -1, then distinct a from 2 to 31, then their negatives. So block J is in row I exactly when I is in row J. `bin_ids`: bin numbers never fall along a sequence.
All inputs are finite; a program needn't handle non-finite values.
Results may differ from the reference program's by a relative error of at most 0.01.
Values may be sent and summed in bfloat16 or wider, within the bound.
A program may use at most 64 MiB of HBM per device.

```python
import math
import jax
import jax.numpy as jnp
import numpy as np
from jax import lax

D = 512
HEADS = 8
HD = 64
BLK = 128
NNZ = 9
SEQLEN = 8192
NB = 64
BATCH = 4
BIN_COUNT = 128
BIN_MOST = 256


def draw_tokens(key, part):
    key_base, key_rows, key_cols = jax.random.split(key, 3)
    base_values = jnp.clip(jax.random.normal(key_base, (BATCH, SEQLEN, D), jnp.float32), -5.0, 5.0)
    row_scale = jnp.exp(jax.random.uniform(key_rows, (BATCH, SEQLEN, 1), jnp.float32, 0.0, 2.3026))
    col_scale = jnp.exp(jax.random.uniform(key_cols, (1, 1, D), jnp.float32, 0.0, 2.3026))
    return (base_values * row_scale * col_scale).astype(jnp.bfloat16)


def draw_w_qkv(key, part):
    key_main = jax.random.fold_in(key, 0)
    main_part = jnp.clip(jax.random.normal(key_main, (D, 3 * D), jnp.float32), -4.0, 4.0)
    return (main_part / jnp.sqrt(float(D))).astype(jnp.bfloat16)


def draw_head_bias(key, part):
    key_small = jax.random.fold_in(key, 1)
    small_values = jax.random.uniform(key_small, (HEADS,), jnp.float32, -3.0, 3.0)
    return small_values


def draw_pattern(key, part):
    extra_pairs = (NNZ - 3) // 2

    def one_sequence(seq_key):
        chosen_gaps = jax.random.permutation(seq_key, jnp.arange(2, NB // 2, dtype=jnp.int32))[:extra_pairs]
        offsets = jnp.concatenate([jnp.array([0, 1, -1], jnp.int32), chosen_gaps, -chosen_gaps])
        row_index = jnp.arange(NB, dtype=jnp.int32)
        return (row_index[:, None] + offsets[None, :]) % NB
    return jax.vmap(one_sequence)(jax.random.split(key, BATCH))


def levels(stream_key, dims, pieces, low, high):
    gain, own = 1.0, jax.random.fold_in(stream_key, 6)
    for position, shards_of in pieces:
        heights = jnp.exp(jax.random.uniform(jax.random.fold_in(own, position), (shards_of,), jnp.float32, low / len(pieces), high / len(pieces)))
        gain = gain * jnp.repeat(heights, dims[position] // shards_of).reshape([-1 if axis == position else 1 for axis in range(len(dims))])
    return gain


def profile(count, total, reach, lean):
    weights = [(1 << 20) // math.isqrt(rank ** lean) + 1 for rank in range(2, count + 1)]
    rest, holding = total - reach - (count - 1), [1] * (count - 1)
    while rest > 0:
        candidates = [i for i in range(count - 1) if holding[i] < reach]
        pool, remaining = sum([weights[i] for i in candidates]), rest
        for i in candidates:
            more = min(reach - holding[i], max(1, remaining * weights[i] // pool), rest)
            holding[i] = holding[i] + more
            rest = rest - more
    return np.array([reach] + holding)


def uneven(stream_key, amount, total, limit, skew):
    if amount == 2:
        one = jax.random.randint(stream_key, (), max(1, total - limit), min(limit, total - 1) + 1)
        return jnp.stack([one, total - one])
    tallies = jnp.asarray(profile(amount, total, limit, skew), jnp.int32)
    twos = (amount - 1) // 2
    source_of, sink = tallies[1:1 + 2 * twos:2], tallies[2:2 + 2 * twos:2]
    margin = jnp.minimum(source_of - 1, limit - sink)
    shifted = jax.random.randint(jax.random.fold_in(stream_key, 1), (twos,), 0, 1 << 20) % (margin + 1)
    tallies = tallies.at[1:1 + 2 * twos:2].set(source_of - shifted).at[2:2 + 2 * twos:2].set(sink + shifted)
    return tallies[jax.random.permutation(jax.random.fold_in(stream_key, 2), amount)]


def gaussian(stream_key, shape, scale, limit, pieces=(), kind=jnp.bfloat16):
    factor_of = levels(stream_key, shape, pieces, -0.22, 0.18) if pieces else 1.0
    result = jax.random.normal(stream_key, shape, jnp.float32) * scale * factor_of
    return jnp.minimum(jnp.maximum(result, -limit), limit).astype(kind)


def setup_inputs(seed: int = 0) -> dict:
    key_list = jax.random.split(jax.random.key(seed), 8)
    return {
        "tokens": draw_tokens(jax.random.fold_in(key_list[7], 71), 0),
        "bin_ids": jax.vmap(lambda own: jnp.searchsorted(jnp.cumsum(uneven(own, BIN_COUNT, SEQLEN, BIN_MOST, 2)), jnp.arange(SEQLEN), side="right"))(jax.random.split(key_list[1], BATCH)).reshape((BATCH, SEQLEN)).astype(jnp.int32),
        "pattern": draw_pattern(jax.random.fold_in(key_list[7], 71), 0),
        "w_qkv": draw_w_qkv(jax.random.fold_in(key_list[7], 71), 0),
        "w_out": gaussian(key_list[4], (D, D), 1.0, 5.0),
        "head_bias": draw_head_bias(jax.random.fold_in(key_list[7], 71), 0),
        "grad_output": gaussian(key_list[6], (BATCH, SEQLEN, D), 1.0, 6.0, ((0, 4), (1, 64))),
    }


EPSILON = 1e-05

def normalize(token_rows):
    widened = token_rows.astype(jnp.float32)
    spread = jnp.sqrt(lax.optimization_barrier(jnp.mean(widened * widened, axis=-1, keepdims=True)) + EPSILON)
    return (widened / spread, spread)

def rounded(values):
    return lax.optimization_barrier(values.astype(jnp.bfloat16)).astype(jnp.float32)

def query_scores(query_blk, key_blk, bin_query, bin_key, bias_local, factor):
    raw_scores = jnp.einsum('gqhe,gnkhe->ghqnk', query_blk, key_blk)
    same_bin = (bin_query[:, None, :, None, None] == bin_key[:, None, None, :, :]).astype(jnp.float32)
    scores = raw_scores * factor + bias_local[None, :, None, None, None] * same_bin
    return scores.reshape(scores.shape[0], scores.shape[1], scores.shape[2], -1)

def key_side_scores(query_blk, key_blk, bin_query, bin_key, bias_local, factor):
    raw_scores = jnp.einsum('gnqhe,gkhe->ghnqk', query_blk, key_blk)
    same_bin = (bin_query[:, None, :, :, None] == bin_key[:, None, None, None, :]).astype(jnp.float32)
    return raw_scores * factor + bias_local[None, :, None, None, None] * same_bin

def reference(tokens, bin_ids, pattern, w_qkv, w_out, head_bias, grad_output):
    factor = 1.0 / math.sqrt(HD)
    group_size = math.gcd(NB, 4)
    group_count = NB // group_size
    bias_all = head_bias.astype(jnp.float32)

    def grouped(array):
        return array.reshape((group_count, group_size) + array.shape[1:])
    grad_qkv = jnp.zeros((D, 3 * D), jnp.float32)
    grad_out = jnp.zeros((D, D), jnp.float32)
    results = []
    input_grads = []
    for sequence in range(BATCH):
        normed, spread = normalize(tokens[sequence])
        hidden = normed.astype(jnp.bfloat16)
        packed = jnp.dot(hidden, w_qkv, preferred_element_type=jnp.float32).astype(jnp.bfloat16)
        packed = packed.reshape(NB, BLK, HEADS, 3 * HD)
        query_tab = packed[..., :HD]
        key_tab = packed[..., HD:2 * HD]
        value_tab = packed[..., 2 * HD:]
        bin_tab = bin_ids[sequence].reshape(NB, BLK)
        key_lists = pattern[sequence]

        def forward_group(entries):
            query_blk, key_rows, bin_query = entries
            key_blk = jnp.take(key_tab, key_rows, axis=0).astype(jnp.float32)
            value_blk = jnp.take(value_tab, key_rows, axis=0).astype(jnp.float32)
            value_blk = value_blk.reshape(group_size, NNZ * BLK, HEADS, HD)
            bin_key = jnp.take(bin_tab, key_rows, axis=0)
            scores = query_scores(query_blk.astype(jnp.float32), key_blk, bin_query, bin_key, bias_all, factor)
            row_max = lax.optimization_barrier(jnp.max(scores, axis=-1, keepdims=True))
            log_total = row_max + jnp.log(lax.optimization_barrier(jnp.sum(jnp.exp(scores - row_max), axis=-1, keepdims=True)))
            probs = rounded(jnp.exp(scores - log_total))
            attended = jnp.einsum('ghqm,gmhe->gqhe', probs, value_blk).astype(jnp.bfloat16)
            return (attended, log_total[..., 0])
        attended, log_blocks = lax.map(forward_group, (grouped(query_tab), grouped(key_lists), grouped(bin_tab)))
        attended = attended.reshape(SEQLEN, D)
        log_blocks = log_blocks.reshape(NB, HEADS, BLK)
        results.append(jnp.dot(attended, w_out, preferred_element_type=jnp.float32).astype(jnp.bfloat16))
        grad_rows = grad_output[sequence]
        grad_att = jnp.dot(grad_rows, w_out.T, preferred_element_type=jnp.float32).astype(jnp.bfloat16)
        grad_out = grad_out + jnp.dot(attended.T, grad_rows, preferred_element_type=jnp.float32)
        delta_rows = lax.optimization_barrier(jnp.sum((grad_att.astype(jnp.float32) * attended.astype(jnp.float32)).reshape(SEQLEN, HEADS, HD), axis=-1))
        delta_blocks = delta_rows.reshape(NB, BLK, HEADS).swapaxes(1, 2)
        grad_tab = grad_att.reshape(NB, BLK, HEADS, HD)

        def query_group(entries):
            query_blk, grad_blk, log_blk, delta_blk, key_rows, bin_query = entries
            key_blk = jnp.take(key_tab, key_rows, axis=0).astype(jnp.float32)
            value_blk = jnp.take(value_tab, key_rows, axis=0).astype(jnp.float32)
            bin_key = jnp.take(bin_tab, key_rows, axis=0)
            scores = query_scores(query_blk.astype(jnp.float32), key_blk, bin_query, bin_key, bias_all, factor)
            probs = jnp.exp(scores - log_blk[..., None])
            value_flat = value_blk.reshape(group_size, NNZ * BLK, HEADS, HD)
            key_flat = key_blk.reshape(group_size, NNZ * BLK, HEADS, HD)
            grad_prob = jnp.einsum('gqhe,gmhe->ghqm', grad_blk.astype(jnp.float32), value_flat)
            grad_score = rounded(probs * (grad_prob - delta_blk[..., None]) * factor)
            return jnp.einsum('ghqm,gmhe->gqhe', grad_score, key_flat).astype(jnp.bfloat16)
        grad_query = lax.map(query_group, (grouped(query_tab), grouped(grad_tab), grouped(log_blocks), grouped(delta_blocks), grouped(key_lists), grouped(bin_tab)))

        def key_group(entries):
            key_blk, value_blk, key_rows, bin_key = entries
            query_blk = jnp.take(query_tab, key_rows, axis=0).astype(jnp.float32)
            grad_blk = jnp.take(grad_tab, key_rows, axis=0).astype(jnp.float32)
            log_blk = jnp.take(log_blocks, key_rows, axis=0).swapaxes(1, 2)
            delta_blk = jnp.take(delta_blocks, key_rows, axis=0).swapaxes(1, 2)
            bin_query = jnp.take(bin_tab, key_rows, axis=0)
            scores = key_side_scores(query_blk, key_blk.astype(jnp.float32), bin_query, bin_key, bias_all, factor)
            probs = jnp.exp(scores - log_blk[..., None])
            grad_prob = jnp.einsum('gnqhe,gkhe->ghnqk', grad_blk, value_blk.astype(jnp.float32))
            grad_score = rounded(probs * (grad_prob - delta_blk[..., None]) * factor)
            grad_key = jnp.einsum('ghnqk,gnqhe->gkhe', grad_score, query_blk).astype(jnp.bfloat16)
            grad_value = jnp.einsum('ghnqk,gnqhe->gkhe', rounded(probs), grad_blk).astype(jnp.bfloat16)
            return jnp.concatenate([grad_key, grad_value], axis=-1)
        grad_pairs = lax.map(key_group, (grouped(key_tab), grouped(value_tab), grouped(key_lists), grouped(bin_tab)))
        grad_packed = jnp.concatenate([grad_query.reshape(SEQLEN, HEADS, HD), grad_pairs.reshape(SEQLEN, HEADS, 2 * HD)], axis=-1)
        grad_packed = grad_packed.reshape(SEQLEN, 3 * D)
        grad_qkv = grad_qkv + jnp.dot(hidden.T, grad_packed, preferred_element_type=jnp.float32)
        grad_hidden = jnp.dot(grad_packed, w_qkv.T, preferred_element_type=jnp.float32)
        inner = lax.optimization_barrier(jnp.mean(grad_hidden * normed, axis=-1, keepdims=True))
        input_grads.append(((grad_hidden - normed * inner) / spread).astype(jnp.bfloat16))
    return (jnp.stack(results), jnp.stack(input_grads), grad_qkv, grad_out)
```

```python
import functools
import math

import jax
import jax.numpy as jnp
from jax import lax
from jax.experimental import pallas as pl
from jax.experimental.pallas import tpu as pltpu
from jax.sharding import PartitionSpec as P

D = 512
HEADS = 8
HD = 64
BLK = 128
NNZ = 9
SPANS = 8
PER = 8
NB = SPANS * PER
EPSILON = 1e-05
LOG2E = math.log2(math.e)
MESH = pl.DeviceIdType.MESH
F32 = jnp.float32
BF16 = jnp.bfloat16


def dot_nn(a, b):
    return lax.dot_general(a, b, (((1,), (0,)), ((), ())), preferred_element_type=F32)


def dot_nt(a, b):
    return lax.dot_general(a, b, (((1,), (1,)), ((), ())), preferred_element_type=F32)


A_KV, A_QD, A_HID, A_GO, A_BQO, A_BKV, A_ST, A_RS0, A_RS1, A_AG0, A_AG1 = range(11)


def kernel(
    pat_ref, bias_ref, tok_ref, gout_ref, wqkv_ref, wout_ref, bins_ref,
    out_ref, gtok_ref, gqkv_ref, gwo_ref,
    gkv, gqd, hid, gog, skv, sqd, normed_ref, spread_ref,
    ycat, a2, sd, pd, stcol, strow, stg, binsf, binst,
    bqo, bkv, rqo, rkv, dtqo, dtkv,
    wpart, ars, arr, dpx, fin, att, gp,
    ss, rr, dps, dpr, zs, zr,
):
    dp = lax.axis_index("dp")
    s = lax.axis_index("seq")
    h = lax.axis_index("head")
    factor = 1.0 / math.sqrt(HD)
    c2 = factor * LOG2E

    def mod8(v):
        return lax.rem(v + 16, 8)

    def send(kind, d, axis, src, dst):
        peer = mod8((h if axis == "head" else s) + d)
        return pltpu.make_async_remote_copy(
            src_ref=src,
            dst_ref=dst,
            send_sem=ss.at[kind, d],
            recv_sem=rr.at[kind, d],
            device_id={axis: peer},
            device_id_type=MESH,
        )

    pending = []

    def start(copy):
        copy.start()
        pending.append(copy)
        return copy

    barrier = pltpu.get_barrier_semaphore()
    for d in range(1, 8):
        pl.semaphore_signal(barrier, inc=1, device_id={"head": mod8(h + d)}, device_id_type=MESH)
        pl.semaphore_signal(barrier, inc=1, device_id={"seq": mod8(s + d)}, device_id_type=MESH)
    for d in range(1, 4):
        pl.semaphore_signal(
            barrier, inc=1, device_id={"dp": lax.rem(dp + d, 4)}, device_id_type=MESH
        )

    lane = lax.broadcasted_iota(jnp.int32, (BLK, 2 * HD), 1)
    low = lane < HD

    def swap(x):
        return pltpu.roll(x, HD, 1)

    x = tok_ref[...].astype(F32)
    spread = jnp.sqrt(jnp.mean(x * x, axis=-1, keepdims=True) + EPSILON)
    normed = x / spread
    normed_ref[...] = normed
    spread_ref[...] = spread
    hidden = normed.astype(BF16)
    hid[h] = hidden
    gout = gout_ref[...]
    gog[h] = gout
    for g in range(HEADS // 2):
        t = dot_nn(hidden, wqkv_ref[:, g * 384 : (g + 1) * 384])
        u = dot_nt(gout, wout_ref[g * 128 : (g + 1) * 128, :])
        t0, t1, t2 = t[:, 0:128], t[:, 128:256], t[:, 256:384]
        st1 = swap(t1)
        skv[2 * g] = jnp.where(low, swap(t0), st1).astype(BF16)
        skv[2 * g + 1] = t2.astype(BF16)
        sqd[2 * g] = jnp.where(low, t0, swap(u)).astype(BF16)
        sqd[2 * g + 1] = jnp.where(low, st1, u).astype(BF16)
    gkv[PER * s + h] = skv[h]
    gqd[PER * s + h] = sqd[h]

    pl.semaphore_wait(barrier, 17)

    def a2a(kind, src_of, dst):
        return [start(send(kind, d, "head", src_of(mod8(h + d)), dst)) for d in range(1, 8)]

    c_kv = a2a(A_KV, lambda p: skv.at[p], gkv.at[PER * s + h])
    c_qd = a2a(A_QD, lambda p: sqd.at[p], gqd.at[PER * s + h])
    c_hid = a2a(A_HID, lambda p: hid.at[h], hid.at[h])
    c_go = a2a(A_GO, lambda p: gog.at[h], gog.at[h])

    binsf[...] = bins_ref[...].astype(F32)
    binst[...] = jnp.concatenate([binsf[...], jnp.zeros((BLK - NB, BLK), F32)], axis=0).T

    right, left = mod8(s + 1), mod8(s - 1)

    def hop(which, buf, way, t, c):
        span = mod8(s - t + 1) if way == 0 else mod8(s + t - 1)
        part = buf.at[pl.ds(PER * span + 4 * c, 4)]
        return pltpu.make_async_remote_copy(
            src_ref=part,
            dst_ref=part,
            send_sem=zs.at[which, way, t, c],
            recv_sem=zr.at[which, way, t, c],
            device_id={"seq": right if way == 0 else left},
            device_id_type=MESH,
        )

    def used(way, t, c):
        return t < 4 or c == way

    def first_hop(which, buf):
        return {(w, 1, c): start(hop(which, buf, w, 1, c)) for c in (0, 1) for w in (0, 1)}

    def next_hop(which, buf, table, t):
        for c in (0, 1):
            for w in (0, 1):
                table[w, t, c].wait_recv()
                if used(w, t + 1, c):
                    table[w, t + 1, c] = start(hop(which, buf, w, t + 1, c))

    def last_hop(table):
        for w in (0, 1):
            table[w, 4, w].wait_recv()

    for copy in c_kv:
        copy.wait_recv()
    z_kv = first_hop(0, gkv)
    for t in (1, 2, 3):
        next_hop(0, gkv, z_kv, t)
    for copy in c_qd:
        copy.wait_recv()
    z_qd = first_hop(1, gqd)
    last_hop(z_kv)

    bias2 = bias_ref[h] * LOG2E

    def gather(buf, row):
        for n in range(NNZ):
            ycat[n * BLK : (n + 1) * BLK, :] = buf[pat_ref[row, n]]

    def stack_halves(block):
        zero = jnp.zeros((BLK, 2 * HD), BF16)
        a2[0:BLK, :] = jnp.where(low, block, zero)
        a2[BLK : 2 * BLK, :] = jnp.where(low, zero, block)

    def own_bins(row):
        return jnp.sum(jnp.where(lane == row, binst[...], 0.0), axis=1, keepdims=True)

    def tile(n):
        return slice(n * BLK, (n + 1) * BLK)

    stcol[...] = jnp.zeros((BLK, BLK), F32)

    def query_block(i, carry):
        row = PER * s + i
        gather(gkv, row)
        stack_halves(gqd[row])
        sd[...] = dot_nt(a2[...], ycat[...])
        bin_col = own_bins(row)
        top = None
        for n in range(NNZ):
            bin_row = binsf[pl.ds(pat_ref[row, n], 1), :]
            v = sd[0:BLK, tile(n)] * c2 + jnp.where(bin_col == bin_row, bias2, 0.0)
            sd[0:BLK, tile(n)] = v
            top = v if top is None else jnp.maximum(top, v)
        m = jnp.max(top, axis=1, keepdims=True)
        total = jnp.zeros((BLK, BLK), F32)
        inner = jnp.zeros((BLK, BLK), F32)
        for n in range(NNZ):
            p = jnp.exp2(sd[0:BLK, tile(n)] - m)
            sd[0:BLK, tile(n)] = p
            total = total + p
            inner = inner + p * sd[BLK : 2 * BLK, tile(n)]
        total = jnp.sum(total, axis=1, keepdims=True)
        delta = jnp.sum(inner, axis=1, keepdims=True) / total
        for n in range(NNZ):
            p = sd[0:BLK, tile(n)]
            pd[0:BLK, tile(n)] = p.astype(BF16)
            pd[BLK : 2 * BLK, tile(n)] = (p * (sd[BLK : 2 * BLK, tile(n)] - delta)).astype(BF16)
        r = dot_nn(pd[...], ycat[...])
        inv = 1.0 / total
        both = jnp.where(low, r[BLK : 2 * BLK] * (inv * factor), r[0:BLK] * inv)
        bqo[i] = both.astype(BF16)
        dtqo[:, pl.ds(pl.multiple_of(i * BLK, BLK), BLK)] = both.T.astype(BF16)
        logs = m + jnp.log2(total)
        stcol[...] = jnp.where(
            lane == 2 * i, logs, jnp.where(lane == 2 * i + 1, delta, stcol[...])
        )
        return carry

    lax.fori_loop(0, PER, query_block, 0)

    strow[...] = stcol[...].T
    stg[pl.ds(pl.multiple_of(2 * PER * s, 16), 16), :] = strow[0:16, :]
    mine = stg.at[pl.ds(pl.multiple_of(2 * PER * s, 16), 16)]
    c_st = [start(send(A_ST, d, "seq", mine, mine)) for d in range(1, 8)]
    next_hop(1, gqd, z_qd, 1)
    rqo[h] = bqo[h]
    c_bqo = a2a(A_BQO, lambda p: bqo.at[p], rqo.at[h])
    next_hop(1, gqd, z_qd, 2)

    for copy in c_hid:
        copy.wait_recv()
    for copy in c_go:
        copy.wait_recv()
    hid_all = hid[...].reshape(PER * BLK, D)
    go_all = gog[...].reshape(PER * BLK, D)

    def reduce_send(k, part):
        wpart[k] = part
        for z in range(SPANS):
            ars[k, z] = part[16 * z : 16 * (z + 1), :].astype(BF16)
        return [
            start(send((A_RS0, A_RS1)[k], d, "seq", ars.at[k, mod8(s + d)], arr.at[k, s]))
            for d in range(1, 8)
        ]

    def reduce_dp(k, copies):
        total = wpart[k, pl.ds(pl.multiple_of(16 * s, 16), 16), :]
        for d, copy in zip(range(1, 8), copies):
            copy.wait_recv()
            total = total + arr[k, mod8(s - d)].astype(F32)
        dpx[k, dp] = total.astype(BF16)
        sent = []
        for d in range(1, 4):
            sent.append(
                start(
                    pltpu.make_async_remote_copy(
                        src_ref=dpx.at[k, dp],
                        dst_ref=dpx.at[k, dp],
                        send_sem=dps.at[k, d],
                        recv_sem=dpr.at[k, d],
                        device_id={"dp": lax.rem(dp + d, 4)},
                        device_id_type=MESH,
                    )
                )
            )
        return sent

    def reduce_gather(k, copies):
        for copy in copies:
            copy.wait_recv()
        total = dpx[k, 0].astype(F32)
        for q in range(1, 4):
            total = total + dpx[k, q].astype(F32)
        fin[k, s] = total.astype(BF16)
        return [
            start(send((A_AG0, A_AG1)[k], d, "seq", fin.at[k, s], fin.at[k, s]))
            for d in range(1, 8)
        ]

    part0 = jnp.concatenate(
        [dot_nn(dtqo[0:HD, :], hid_all), dot_nn(dtqo[HD : 2 * HD, :], go_all)], axis=0
    )
    next_hop(1, gqd, z_qd, 3)
    rs0 = reduce_send(0, part0)
    for copy in c_st:
        copy.wait_recv()
    last_hop(z_qd)

    def key_block(i, carry):
        row = PER * s + i
        gather(gqd, row)
        stack_halves(gkv[row])
        sd[...] = dot_nt(a2[...], ycat[...])
        bin_col = own_bins(row)
        for n in range(NNZ):
            other = pat_ref[row, n]
            bin_row = binsf[pl.ds(other, 1), :]
            log_row = stg[pl.ds(2 * other, 1), :]
            delta_row = stg[pl.ds(2 * other + 1, 1), :]
            v = sd[0:BLK, tile(n)] * c2 + jnp.where(bin_col == bin_row, bias2, 0.0)
            p = jnp.exp2(v - log_row)
            pd[0:BLK, tile(n)] = p.astype(BF16)
            pd[BLK : 2 * BLK, tile(n)] = (p * (sd[BLK : 2 * BLK, tile(n)] - delta_row)).astype(BF16)
        r = dot_nn(pd[...], ycat[...])
        both = jnp.where(low, r[BLK : 2 * BLK] * factor, r[0:BLK])
        bkv[i] = both.astype(BF16)
        dtkv[:, pl.ds(pl.multiple_of(i * BLK, BLK), BLK)] = both.T.astype(BF16)
        return carry

    lax.fori_loop(0, PER, key_block, 0)

    rkv[h] = bkv[h]
    c_bkv = a2a(A_BKV, lambda p: bkv.at[p], rkv.at[h])
    part1 = dot_nn(dtkv[...], hid[...].reshape(PER * BLK, D))
    rs1 = reduce_send(1, part1)
    dp0 = reduce_dp(0, rs0)

    for copy in c_bqo:
        copy.wait_recv()
    for g in range(HEADS // 2):
        even, odd = rqo[2 * g].astype(F32), rqo[2 * g + 1].astype(F32)
        att[:, g * 128 : (g + 1) * 128] = jnp.where(low, swap(even), odd).astype(BF16)
    out_ref[...] = dot_nn(att[...], wout_ref[...]).astype(BF16)
    dp1 = reduce_dp(1, rs1)
    ag0 = reduce_gather(0, dp0)

    for copy in c_bkv:
        copy.wait_recv()
    for g in range(HEADS // 2):
        qo_even, qo_odd = rqo[2 * g].astype(F32), rqo[2 * g + 1].astype(F32)
        kv_even = swap(rkv[2 * g].astype(F32))
        gp[:, g * 384 : g * 384 + 128] = jnp.where(low, qo_even, kv_even).astype(BF16)
        gp[:, g * 384 + 128 : g * 384 + 256] = jnp.where(low, kv_even, swap(qo_odd)).astype(BF16)
        gp[:, g * 384 + 256 : g * 384 + 384] = rkv[2 * g + 1]
    ag1 = reduce_gather(1, dp1)
    grad_hidden = dot_nt(gp[...], wqkv_ref[...])
    normed = normed_ref[...]
    inner = jnp.mean(grad_hidden * normed, axis=-1, keepdims=True)
    gtok_ref[...] = ((grad_hidden - normed * inner) / spread_ref[...]).astype(BF16)

    for copy in ag0 + ag1:
        copy.wait_recv()
    first = fin[0].reshape(BLK, D).astype(F32)
    second = fin[1].reshape(BLK, D).astype(F32)
    gwo_ref[...] = first[HD : 2 * HD, :]
    rows = jnp.concatenate([first[0:HD, :], second, jnp.zeros((HD, D), F32)], axis=0)
    gqkv_ref[...] = rows.T[:, 0 : 3 * HD]

    for copy in pending:
        copy.wait_send()


def body(tokens, bin_ids, pattern, w_qkv, w_out, head_bias, grad_output):
    vmem = pl.BlockSpec(memory_space=pltpu.VMEM)
    smem = pl.BlockSpec(memory_space=pltpu.SMEM)
    dma = pltpu.SemaphoreType.DMA
    blocks = functools.partial(pltpu.VMEM, dtype=BF16)
    scratch = [
        blocks((NB, BLK, 128)),
        blocks((NB, BLK, 128)),
        blocks((8, BLK, D)),
        blocks((8, BLK, D)),
        blocks((8, BLK, 128)),
        blocks((8, BLK, 128)),
        pltpu.VMEM((BLK, D), F32),
        pltpu.VMEM((BLK, 1), F32),
        blocks((NNZ * BLK, 128)),
        blocks((2 * BLK, 128)),
        pltpu.VMEM((2 * BLK, NNZ * BLK), F32),
        blocks((2 * BLK, NNZ * BLK)),
        pltpu.VMEM((BLK, BLK), F32),
        pltpu.VMEM((BLK, BLK), F32),
        pltpu.VMEM((2 * NB, BLK), F32),
        pltpu.VMEM((NB, BLK), F32),
        pltpu.VMEM((BLK, BLK), F32),
        blocks((8, BLK, 128)),
        blocks((8, BLK, 128)),
        blocks((8, BLK, 128)),
        blocks((8, BLK, 128)),
        blocks((BLK, PER * BLK)),
        blocks((BLK, PER * BLK)),
        pltpu.VMEM((2, BLK, D), F32),
        blocks((2, 8, 16, D)),
        blocks((2, 8, 16, D)),
        blocks((2, 4, 16, D)),
        blocks((2, 8, 16, D)),
        blocks((BLK, D)),
        blocks((BLK, 3 * D)),
        dma((11, 8)),
        dma((11, 8)),
        dma((2, 4)),
        dma((2, 4)),
        dma((2, 2, 5, 2)),
        dma((2, 2, 5, 2)),
    ]
    result, grad_input, own_qkv, own_out = pl.pallas_call(
        kernel,
        out_shape=(
            jax.ShapeDtypeStruct((BLK, D), BF16),
            jax.ShapeDtypeStruct((BLK, D), BF16),
            jax.ShapeDtypeStruct((D, 3 * HD), F32),
            jax.ShapeDtypeStruct((HD, D), F32),
        ),
        in_specs=[smem, smem, vmem, vmem, vmem, vmem, vmem],
        out_specs=(vmem, vmem, vmem, vmem),
        scratch_shapes=scratch,
        compiler_params=pltpu.CompilerParams(
            collective_id=0, has_side_effects=True, vmem_limit_bytes=48 * 1024 * 1024
        ),
        name="layer",
    )(
        pattern[0],
        head_bias,
        tokens[0],
        grad_output[0],
        w_qkv,
        w_out,
        bin_ids[0].reshape(NB, BLK),
    )
    return (result[None], grad_input[None], own_qkv, own_out)


def solution(mesh):
    return jax.shard_map(
        body,
        mesh=mesh,
        in_specs=(
            P("dp", ("seq", "head"), None),
            P("dp", None),
            P("dp", None, None),
            P(),
            P(),
            P(),
            P("dp", ("seq", "head"), None),
        ),
        out_specs=(
            P("dp", ("seq", "head"), None),
            P("dp", ("seq", "head"), None),
            P(None, "head"),
            P("head", None),
        ),
        check_vma=False,
    )
```

```python
import functools
import math

import jax
import jax.numpy as jnp
from jax import lax
from jax.experimental import pallas as pl
from jax.experimental.pallas import tpu as pltpu
from jax.sharding import PartitionSpec as P

D = 512
HEADS = 8
HD = 64
BLK = 128
NNZ = 9
PER = 8
NB = 64
EPSILON = 1e-05
LOG2E = math.log2(math.e)
MESH = pl.DeviceIdType.MESH
F32 = jnp.float32
BF16 = jnp.bfloat16
CAT = NNZ * BLK

BATCHES = ((0, 1), (1, 2), (3, 2), (5, 2), (7, 1))

(
    Z_BQO, Z_BKV, Z_S3A, Z_S3B, G_ST, G_S1A, G_S1B, G_S4A, G_S4B,
) = range(9)


def dot_nn(a, b):
    return lax.dot_general(a, b, (((1,), (0,)), ((), ())), preferred_element_type=F32)


def dot_nt(a, b):
    return lax.dot_general(a, b, (((1,), (1,)), ((), ())), preferred_element_type=F32)


def place(rel):
    return jnp.where(rel == 0, 0, jnp.where(rel <= 4, 2 * rel - 1, 16 - 2 * rel))


def tile(n):
    return slice(n * BLK, (n + 1) * BLK)


def kernel(
    bias_ref, tok_hbm, gout_hbm, wqkv_hbm, wout_hbm, aux_hbm,
    out_hbm, gtok_hbm, gqkv_ref, gwo_ref,
    gkv, gqd, hid, gog, tok, wqkv, wout, aux, pat, wcat, wo2, normed_ref, spread_ref,
    ycats, ycat, probs, sd, pd, a2, stcol, strow, stg, deltas, invs, binsf, binst,
    obuf, bqo, bkv, rqo, rkv, dtqo, dtkv,
    wpart, ars, arr, dpx, zbc, fin, att, gp, res, gres,
    ss, rr, ys, yr, zs, zr, xs, xr, ins, sws, swr,
):
    dp = lax.axis_index("dp")
    z = lax.axis_index("seq")
    head = lax.axis_index("head")
    yhi, c = dp // 2, lax.rem(dp, 2)
    x, ylo = head // 2, lax.rem(head, 2)
    r = 2 * x + c
    seqno = 2 * yhi + ylo
    moved = c != ylo
    odd = lax.rem(z, 2) == 1
    factor = 1.0 / math.sqrt(HD)
    c2 = factor * LOG2E

    def mod8(v):
        return lax.rem(v + 16, 8)

    def device(xx, cc):
        return {"dp": 2 * yhi + cc, "head": 2 * xx + ylo}

    partner = {"dp": 2 * yhi + ylo, "head": 2 * x + c}
    sibling = {"dp": 2 * yhi + (1 - c)}

    def member(d):
        dx, dc = d // 2, d % 2
        xx = lax.rem(x + dx, 4)
        cc = c if dc == 0 else 1 - c
        return xx, cc

    def giver(d):
        dx, dc = d // 2, d % 2
        xx = lax.rem(x + 4 - dx, 4)
        cc = c if dc == 0 else 1 - c
        return 2 * xx + cc

    def remote(src, dst, ssem, rsem, dev):
        return pltpu.make_async_remote_copy(
            src_ref=src, dst_ref=dst, send_sem=ssem, recv_sem=rsem,
            device_id=dev, device_id_type=MESH,
        )

    pending = []

    def start(copy):
        copy.start()
        pending.append(copy)
        return copy

    def when(cond, fn):
        pl.when(cond)(fn)

    barrier = pltpu.get_barrier_semaphore()

    def greet(dev):
        pl.semaphore_signal(barrier, inc=1, device_id=dev, device_id_type=MESH)

    for d in range(1, 8):
        greet({"seq": mod8(z + d)})
        greet(device(*member(d)))
    others = []
    for e in range(1, 4):
        yh = yhi if e // 2 == 0 else 1 - yhi
        yl = ylo if e % 2 == 0 else 1 - ylo
        others.append({"dp": 2 * yh + c, "head": 2 * x + yl})
        greet(others[-1])
    when(moved, lambda: greet(partner))

    weights = [
        pltpu.make_async_copy(wqkv_hbm, wqkv, ins.at[0]),
        pltpu.make_async_copy(wout_hbm, wout, ins.at[1]),
    ]
    stay = [
        pltpu.make_async_copy(tok_hbm, tok, ins.at[2]),
        pltpu.make_async_copy(gout_hbm, gog.at[0], ins.at[3]),
        pltpu.make_async_copy(aux_hbm, aux, ins.at[4]),
    ]
    go = [
        remote(tok_hbm, tok, sws.at[0], swr.at[0], partner),
        remote(gout_hbm, gog.at[0], sws.at[1], swr.at[1], partner),
    ]
    share = remote(aux_hbm, aux, sws.at[2], swr.at[2], sibling)
    for copy in weights:
        copy.start()
    when(jnp.logical_not(moved), lambda: [copy.start() for copy in stay] and None)

    lane = lax.broadcasted_iota(jnp.int32, (BLK, 2 * HD), 1)
    low = lane < HD

    def swap(v):
        return pltpu.roll(v, HD, 1)

    for copy in weights:
        copy.wait()
    pair = pl.multiple_of((z // 2) * 384, 128)
    for q in range(4):
        rows = slice(128 * q, 128 * (q + 1))
        w0 = wqkv[rows, pl.ds(pair, 128)].astype(F32)
        w1 = wqkv[rows, pl.ds(pair + 128, 128)].astype(F32)
        w2 = wqkv[rows, pl.ds(pair + 256, 128)].astype(F32)
        s1 = swap(w1)
        wcat[rows, 0:128] = jnp.where(odd, w2, jnp.where(low, swap(w0), s1)).astype(BF16)
        wcat[rows, 128:256] = jnp.where(low, jnp.where(odd, s1, w0), 0.0).astype(BF16)
    wo_pair = wout[pl.ds(pl.multiple_of((z // 2) * 128, 128), 128), :]
    wo2[0:HD, :] = jnp.zeros((HD, D), BF16)
    wo2[HD:BLK, :] = jnp.where(odd, wo_pair[HD:BLK, :], wo_pair[0:HD, :])

    pl.semaphore_wait(barrier, 17 + jnp.where(moved, 1, 0))
    when(moved, lambda: [copy.start() for copy in go] and None)
    when(jnp.logical_not(moved), lambda: share.start())

    when(moved, lambda: go[0].wait_recv())
    when(jnp.logical_not(moved), lambda: stay[0].wait())

    tokens = tok[...].astype(F32)
    spread = jnp.sqrt(jnp.mean(tokens * tokens, axis=-1, keepdims=True) + EPSILON)
    normed = tokens / spread
    normed_ref[...] = normed
    spread_ref[...] = spread
    hid[0] = normed.astype(BF16)

    rings = (hid, gog)
    table = {}

    def hop(k, way, t, part):
        if way == 0:
            src, dst = (0 if t == 1 else 2 * (t - 1)), (2 * t if t < 4 else 7)
        else:
            src, dst = (0 if t == 1 else 2 * (t - 1) - 1), 2 * t - 1
        rows = pl.ds(64 * part, 64)
        return remote(
            rings[k].at[src, rows], rings[k].at[dst, rows],
            zs.at[k, way, t, part], zr.at[k, way, t, part],
            {"seq": mod8(z + 1) if way == 0 else mod8(z - 1)},
        )

    def first_hop(k):
        for part in (0, 1):
            for way in (0, 1):
                table[k, way, 1, part] = start(hop(k, way, 1, part))

    def next_hop(k, t):
        for part in (0, 1):
            for way in (0, 1):
                table[k, way, t, part].wait_recv()
                if t + 1 < 4 or (t + 1 == 4 and part == way):
                    table[k, way, t + 1, part] = start(hop(k, way, t + 1, part))

    def last_hop(k):
        for way in (0, 1):
            table[k, way, 4, way].wait_recv()

    pools = (gkv, gqd)
    ring_x = {}
    x_right, x_left = lax.rem(x + 1, 4), lax.rem(x + 3, 4)
    x_far = lax.rem(x + 2, 4)

    def xcopy(k, b, kind, owner, dev):
        first, count = BATCHES[b]
        part = pools[k].at[owner, pl.ds(first, count)]
        ring_x[k, b, kind] = start(
            remote(part, part, xs.at[k, b, kind], xr.at[k, b, kind], dev)
        )

    def x_own(k, b):
        xcopy(k, b, 0, r, device(x_right, c))
        xcopy(k, b, 1, r, device(x_left, c))
        xcopy(k, b, 2, r, sibling)

    def x_pass(k, b):
        ring_x[k, b, 0].wait_recv()
        if b in (0, 1, 4):
            xcopy(k, b, 5, 2 * x_left + c, device(x_right, c))
        xcopy(k, b, 3, 2 * x_left + c, sibling)
        ring_x[k, b, 1].wait_recv()
        if b in (2, 3):
            xcopy(k, b, 5, 2 * x_right + c, device(x_left, c))
        xcopy(k, b, 4, 2 * x_right + c, sibling)

    def x_far_pass(k, b):
        ring_x[k, b, 5].wait_recv()
        xcopy(k, b, 6, 2 * x_far + c, sibling)

    def x_end(k):
        for b in range(5):
            for kind in (2, 3, 4, 6):
                ring_x[k, b, kind].wait_recv()

    def project(b):
        first, count = BATCHES[b]
        for p in range(first, first + count):
            t = dot_nn(hid[p], wcat[...]).astype(BF16)
            gkv[r, p] = t[:, 0:128]
            gqd[r, p] = t[:, 128:256]
        x_own(0, b)

    def project_grad(b):
        first, count = BATCHES[b]
        for p in range(first, first + count):
            u = dot_nt(gog[p], wo2[...])
            gqd[r, p] = jnp.where(low, gqd[r, p], u.astype(BF16))
        x_own(1, b)

    first_hop(0)
    project(0)
    when(moved, lambda: go[1].wait_recv())
    when(jnp.logical_not(moved), lambda: stay[1].wait())
    next_hop(0, 1)
    first_hop(1)
    project(1)
    project_grad(0)
    x_pass(0, 0)
    next_hop(0, 2)
    project(2)
    x_pass(0, 1)
    x_far_pass(0, 0)
    next_hop(1, 1)
    project_grad(1)
    next_hop(0, 3)
    project(3)
    x_pass(0, 2)
    x_far_pass(0, 1)
    x_pass(1, 0)
    next_hop(1, 2)
    project_grad(2)
    last_hop(0)
    project(4)
    x_pass(0, 3)
    x_far_pass(0, 2)
    x_pass(1, 1)
    x_far_pass(1, 0)

    when(moved, lambda: share.wait_recv())
    when(jnp.logical_not(moved), lambda: stay[2].wait())
    to_scalars = pltpu.make_async_copy(aux.at[pl.ds(NB, 8)], pat, ins.at[5])
    to_scalars.start()
    binsf[...] = aux[0:NB, :].astype(F32)
    binst[...] = jnp.concatenate([binsf[...], jnp.zeros((BLK - NB, BLK), F32)], axis=0).T
    to_scalars.wait()

    x_pass(0, 4)
    x_far_pass(0, 3)
    next_hop(1, 3)
    project_grad(3)
    x_far_pass(0, 4)
    x_pass(1, 2)
    x_far_pass(1, 1)
    x_end(0)

    bias2 = bias_ref[z] * LOG2E

    def own_block(p):
        t = (p + 1) // 2
        rel = jnp.where(lax.rem(p, 2) == 1, t, -t)
        return 8 * mod8(z + rel) + r

    def used_block(row, n):
        other = lax.rem(row + pat[0, n], NB)
        return other, lax.rem(other, 8), place(mod8(other // 8 - z))

    def own_bins(row):
        return jnp.sum(jnp.where(lane == row, binst[...], 0.0), axis=1, keepdims=True)

    stcol[...] = jnp.zeros((BLK, BLK), F32)

    def forward_block(p, carry):
        row = own_block(p)
        for n in range(NNZ):
            _, rn, pn = used_block(row, n)
            ycats[p, tile(n), :] = gkv[rn, pn]
        query = gqd[r, p]
        sd[0:BLK, :] = dot_nt(jnp.where(low, query, jnp.zeros_like(query)), ycats[p])
        bin_col = own_bins(row)
        top = None
        for n in range(NNZ):
            other, _, _ = used_block(row, n)
            bin_row = binsf[pl.ds(other, 1), :]
            v = sd[0:BLK, tile(n)] * c2 + jnp.where(bin_col == bin_row, bias2, 0.0)
            sd[0:BLK, tile(n)] = v
            top = v if top is None else jnp.maximum(top, v)
        m = jnp.max(top, axis=1, keepdims=True)
        total = jnp.zeros((BLK, BLK), F32)
        for n in range(NNZ):
            e = jnp.exp2(sd[0:BLK, tile(n)] - m)
            probs[p, :, tile(n)] = e
            pd[0:BLK, tile(n)] = e.astype(BF16)
            total = total + e
        total = jnp.sum(total, axis=1, keepdims=True)
        inv = 1.0 / total
        obuf[p] = (dot_nn(pd[0:BLK, :], ycats[p]) * inv).astype(BF16)
        invs[p] = inv
        stcol[...] = jnp.where(lane == 2 * p, m + jnp.log2(total), stcol[...])
        return carry

    lax.fori_loop(0, PER, forward_block, 0)

    x_pass(1, 3)
    x_far_pass(1, 2)
    last_hop(1)
    project_grad(4)

    for p in range(PER):
        both = gqd[r, p].astype(F32) * obuf[p].astype(F32)
        delta = jnp.sum(jnp.where(low, 0.0, both), axis=1, keepdims=True)
        deltas[p] = delta
        stcol[...] = jnp.where(lane == 2 * p + 1, delta, stcol[...])
    strow[...] = stcol[...].T
    mine = stg.at[pl.ds(pl.multiple_of(2 * PER * r, 16), 16)]
    stg[pl.ds(pl.multiple_of(2 * PER * r, 16), 16), :] = strow[0:16, :]

    def group(kind, d, src, dst):
        return start(remote(src, dst, ss.at[kind, d], rr.at[kind, d], device(*member(d))))

    def along(kind, d, src, dst):
        return start(remote(src, dst, ss.at[kind, d], rr.at[kind, d], {"seq": mod8(z + d)}))

    c_st = [group(G_ST, d, mine, mine) for d in range(1, 8)]
    x_pass(1, 4)
    x_far_pass(1, 3)

    def query_block(p, carry):
        block = gqd[r, p]
        sd[0:BLK, :] = dot_nt(jnp.where(low, jnp.zeros_like(block), block), ycats[p])
        delta = deltas[p]
        for n in range(NNZ):
            pd[0:BLK, tile(n)] = (
                probs[p, :, tile(n)] * (sd[0:BLK, tile(n)] - delta)
            ).astype(BF16)
        grad = dot_nn(pd[0:BLK, :], ycats[p]) * (invs[p] * factor)
        both = jnp.where(low, grad, obuf[p].astype(F32))
        bqo[p] = both.astype(BF16)
        dtqo[:, pl.ds(pl.multiple_of(p * BLK, BLK), BLK)] = both.T.astype(BF16)
        return carry

    lax.fori_loop(0, PER, query_block, 0)

    far = (0, 1, 3, 5, 7, 6, 4, 2)
    rqo[z] = bqo[0]
    c_bqo = [along(Z_BQO, d, bqo.at[far[d]], rqo.at[z]) for d in range(1, 8)]
    x_far_pass(1, 4)

    def stage1(k, part):
        wpart[k] = part
        for q in range(8):
            ars[k, q] = part[16 * q : 16 * (q + 1), :].astype(BF16)
        sent = []
        for d in range(1, 8):
            xx, cc = member(d)
            sent.append(group((G_S1A, G_S1B)[k], d, ars.at[k, 2 * xx + cc], arr.at[k, r]))
        return sent

    def stage2(k, copies):
        total = wpart[k, pl.ds(pl.multiple_of(16 * r, 16), 16), :]
        for d, copy in zip(range(1, 8), copies):
            copy.wait_recv()
            total = total + arr[k, giver(d)].astype(F32)
        dpx[k, seqno] = total.astype(BF16)
        slot = dpx.at[k, seqno]
        return [
            start(remote(slot, slot, ys.at[k, e], yr.at[k, e], others[e - 1]))
            for e in range(1, 4)
        ]

    mine_here = lax.rem(z, 2) == ylo

    def stage3(k, copies):
        for copy in copies:
            copy.wait_recv()
        total = dpx[k, 0].astype(F32)
        for q in range(1, 4):
            total = total + dpx[k, q].astype(F32)

        def spread_out():
            zbc[k, z // 2] = total.astype(BF16)

        slot = zbc.at[k, z // 2]
        kind = (Z_S3A, Z_S3B)[k]
        sent = [
            remote(slot, slot, ss.at[kind, d], rr.at[kind, d], {"seq": mod8(z + d)})
            for d in range(1, 8)
        ]
        when(mine_here, spread_out)
        when(mine_here, lambda: [copy.start() for copy in sent] and None)
        return sent

    def stage4(k, copies):
        for d, copy in zip(range(1, 8), copies):
            when(lax.rem(z + 8 - d, 2) == ylo, lambda: copy.wait_recv())
        fin[k, r] = zbc[k, x]
        sent = []
        for d in range(1, 8):
            xx, _ = member(d)
            sent.append(group((G_S4A, G_S4B)[k], d, zbc.at[k, xx], fin.at[k, r]))
        when(mine_here, lambda: [copy.wait_send() for copy in copies] and None)
        return sent

    hid_all = hid[...].reshape(PER * BLK, D)
    go_all = gog[...].reshape(PER * BLK, D)
    part0 = jnp.concatenate(
        [dot_nn(dtqo[0:HD, :], hid_all), dot_nn(dtqo[HD : 2 * HD, :], go_all)], axis=0
    )
    s1a = stage1(0, part0)
    for copy in c_st:
        copy.wait_recv()
    x_end(1)

    def key_block(p, carry):
        row = own_block(p)
        for n in range(NNZ):
            _, rn, pn = used_block(row, n)
            ycat[tile(n), :] = gqd[rn, pn]
        block = gkv[r, p]
        zero = jnp.zeros_like(block)
        a2[0:BLK, :] = jnp.where(low, block, zero)
        a2[BLK : 2 * BLK, :] = jnp.where(low, zero, block)
        sd[...] = dot_nt(a2[...], ycat[...])
        bin_col = own_bins(row)
        for n in range(NNZ):
            other, rn, pn = used_block(row, n)
            bin_row = binsf[pl.ds(other, 1), :]
            log_row = stg[pl.ds(16 * rn + 2 * pn, 1), :]
            delta_row = stg[pl.ds(16 * rn + 2 * pn + 1, 1), :]
            v = sd[0:BLK, tile(n)] * c2 + jnp.where(bin_col == bin_row, bias2, 0.0)
            e = jnp.exp2(v - log_row)
            pd[0:BLK, tile(n)] = e.astype(BF16)
            pd[BLK : 2 * BLK, tile(n)] = (e * (sd[BLK : 2 * BLK, tile(n)] - delta_row)).astype(BF16)
        g = dot_nn(pd[...], ycat[...])
        both = jnp.where(low, g[BLK : 2 * BLK] * factor, g[0:BLK])
        bkv[p] = both.astype(BF16)
        dtkv[:, pl.ds(pl.multiple_of(p * BLK, BLK), BLK)] = both.T.astype(BF16)
        return carry

    lax.fori_loop(0, PER, key_block, 0)

    rkv[z] = bkv[0]
    c_bkv = [along(Z_BKV, d, bkv.at[far[d]], rkv.at[z]) for d in range(1, 8)]
    s1b = stage1(1, dot_nn(dtkv[...], hid[...].reshape(PER * BLK, D)))
    s2a = stage2(0, s1a)

    def deliver(src, dst, k):
        here = pltpu.make_async_copy(src, dst, ins.at[6 + k])
        there = remote(src, dst, sws.at[3 + k], swr.at[3 + k], partner)
        when(jnp.logical_not(moved), lambda: here.start())
        when(moved, lambda: there.start())
        return here, there

    for copy in c_bqo:
        copy.wait_recv()
    for g in range(HEADS // 2):
        even, uneven = rqo[2 * g].astype(F32), rqo[2 * g + 1].astype(F32)
        att[:, tile(g)] = jnp.where(low, swap(even), uneven).astype(BF16)
    res[...] = dot_nn(att[...], wout[...]).astype(BF16)
    d_out = deliver(res, out_hbm, 0)
    s3a = stage3(0, s2a)
    s2b = stage2(1, s1b)
    s4a = stage4(0, s3a)
    s3b = stage3(1, s2b)

    for copy in c_bkv:
        copy.wait_recv()
    for g in range(HEADS // 2):
        qo_even, qo_odd = rqo[2 * g].astype(F32), rqo[2 * g + 1].astype(F32)
        kv_even = swap(rkv[2 * g].astype(F32))
        gp[:, tile(3 * g)] = jnp.where(low, qo_even, kv_even).astype(BF16)
        gp[:, tile(3 * g + 1)] = jnp.where(low, kv_even, swap(qo_odd)).astype(BF16)
        gp[:, tile(3 * g + 2)] = rkv[2 * g + 1]
    grad_hidden = dot_nt(gp[...], wqkv[...])
    s4b = stage4(1, s3b)
    normed = normed_ref[...]
    inner = jnp.mean(grad_hidden * normed, axis=-1, keepdims=True)
    gres[...] = ((grad_hidden - normed * inner) / spread_ref[...]).astype(BF16)
    d_gtok = deliver(gres, gtok_hbm, 1)

    for copy in s4a + s4b:
        copy.wait_recv()
    first = fin[0].reshape(BLK, D).astype(F32)
    second = fin[1].reshape(BLK, D).astype(F32)
    gwo_ref[...] = first[HD : 2 * HD, :]
    rows = jnp.concatenate([first[0:HD, :], second, jnp.zeros((HD, D), F32)], axis=0)
    gqkv_ref[...] = rows.T[:, 0 : 3 * HD]

    for copy in pending:
        copy.wait_send()
    when(moved, lambda: [copy.wait_send() for copy in go] and None)
    when(jnp.logical_not(moved), lambda: share.wait_send())
    for here, there in (d_out, d_gtok):
        when(jnp.logical_not(moved), lambda: here.wait())
        when(moved, lambda: there.wait())


def body(tokens, bin_ids, pattern, w_qkv, w_out, head_bias, grad_output):
    vmem = pl.BlockSpec(memory_space=pltpu.VMEM)
    smem = pl.BlockSpec(memory_space=pltpu.SMEM)
    hbm = pl.BlockSpec(memory_space=pltpu.HBM)
    dma = pltpu.SemaphoreType.DMA
    half = functools.partial(pltpu.VMEM, dtype=BF16)
    full = functools.partial(pltpu.VMEM, dtype=F32)
    scratch = [
        half((8, 8, BLK, 128)),
        half((8, 8, BLK, 128)),
        half((8, BLK, D)),
        half((8, BLK, D)),
        half((BLK, D)),
        half((D, 3 * D)),
        half((D, D)),
        pltpu.VMEM((NB + 8, BLK), jnp.int32),
        pltpu.SMEM((8, BLK), jnp.int32),
        half((D, 256)),
        half((BLK, D)),
        full((BLK, D)),
        full((BLK, 1)),
        half((PER, CAT, 128)),
        half((CAT, 128)),
        full((PER, BLK, CAT)),
        full((2 * BLK, CAT)),
        half((2 * BLK, CAT)),
        half((2 * BLK, 128)),
        full((BLK, BLK)),
        full((BLK, BLK)),
        full((2 * NB, BLK)),
        full((PER, BLK, 1)),
        full((PER, BLK, 1)),
        full((NB, BLK)),
        full((BLK, BLK)),
        half((8, BLK, 128)),
        half((8, BLK, 128)),
        half((8, BLK, 128)),
        half((8, BLK, 128)),
        half((8, BLK, 128)),
        half((BLK, PER * BLK)),
        half((BLK, PER * BLK)),
        full((2, BLK, D)),
        half((2, 8, 16, D)),
        half((2, 8, 16, D)),
        half((2, 4, 16, D)),
        half((2, 4, 16, D)),
        half((2, 8, 16, D)),
        half((BLK, D)),
        half((BLK, 3 * D)),
        half((BLK, D)),
        half((BLK, D)),
        dma((9, 8)),
        dma((9, 8)),
        dma((2, 4)),
        dma((2, 4)),
        dma((2, 2, 5, 2)),
        dma((2, 2, 5, 2)),
        dma((2, 5, 7)),
        dma((2, 5, 7)),
        dma((8,)),
        dma((5,)),
        dma((5,)),
    ]
    aux = jnp.concatenate(
        [bin_ids[0].reshape(NB, BLK), jnp.pad(pattern[0, 0:1], ((0, 7), (0, BLK - NNZ)))], axis=0
    )
    result, grad_input, own_qkv, own_out = pl.pallas_call(
        kernel,
        out_shape=(
            jax.ShapeDtypeStruct((BLK, D), BF16),
            jax.ShapeDtypeStruct((BLK, D), BF16),
            jax.ShapeDtypeStruct((D, 3 * HD), F32),
            jax.ShapeDtypeStruct((HD, D), F32),
        ),
        in_specs=[smem, hbm, hbm, hbm, hbm, hbm],
        out_specs=(hbm, hbm, vmem, vmem),
        scratch_shapes=scratch,
        compiler_params=pltpu.CompilerParams(
            collective_id=0, has_side_effects=True, vmem_limit_bytes=48 * 1024 * 1024
        ),
        name="layer",
    )(head_bias, tokens[0], grad_output[0], w_qkv, w_out, aux)
    return (result[None], grad_input[None], own_qkv, own_out)


def solution(mesh):
    return jax.shard_map(
        body,
        mesh=mesh,
        in_specs=(
            P("dp", ("seq", "head"), None),
            P("dp", None),
            P("dp", None, None),
            P(),
            P(),
            P(),
            P("dp", ("seq", "head"), None),
        ),
        out_specs=(
            P("dp", ("seq", "head"), None),
            P("dp", ("seq", "head"), None),
            P(None, "head"),
            P("head", None),
        ),
        check_vma=False,
    )
```

```python
import functools
import math

import jax
import jax.numpy as jnp
from jax import lax
from jax.experimental import pallas as pl
from jax.experimental.pallas import tpu as pltpu
from jax.sharding import PartitionSpec as P

D = 512
HEADS = 8
HD = 64
BLK = 128
NNZ = 9
PER = 8
NB = 64
EPSILON = 1e-05
LOG2E = math.log2(math.e)
MESH = pl.DeviceIdType.MESH
F32 = jnp.float32
BF16 = jnp.bfloat16
CAT = NNZ * BLK

BATCHES = ((0, 1), (1, 2), (3, 2), (5, 2), (7, 1))

(
    Z_BQO, Z_BKV, Z_S3A, Z_S3B, G_ST, G_S1A, G_S1B, G_S4A, G_S4B,
) = range(9)


def dot_nn(a, b):
    return lax.dot_general(a, b, (((1,), (0,)), ((), ())), preferred_element_type=F32)


def dot_nt(a, b):
    return lax.dot_general(a, b, (((1,), (1,)), ((), ())), preferred_element_type=F32)


def place(rel):
    return jnp.where(rel == 0, 0, jnp.where(rel <= 4, 2 * rel - 1, 16 - 2 * rel))


def tile(n):
    return slice(n * BLK, (n + 1) * BLK)


def kernel(
    bias_ref, tok_hbm, gout_hbm, wqkv_hbm, wout_hbm, bins_hbm, pat_hbm,
    out_hbm, gtok_hbm, fin,
    gkv, gqd, hid, gog, tok, wqkv, wout, bins, patv, pat, wcat, wo2, normed_ref, spread_ref,
    ycats, ycat, probs, sd, pd, a2, stcol, strow, stg, deltas, invs, binsf, binst,
    obuf, bqo, bkv, rqo, rkv, dtqo, dtkv,
    wpart, ars, arr, dpx, zbc, att, gp, res, gres,
    ss, rr, ys, yr, zs, zr, xs, xr, ins, sws, swr,
):
    dp = lax.axis_index("dp")
    z = lax.axis_index("seq")
    head = lax.axis_index("head")
    yhi, c = dp // 2, lax.rem(dp, 2)
    x, ylo = head // 2, lax.rem(head, 2)
    r = 2 * x + c
    seqno = 2 * yhi + ylo
    moved = c != ylo
    odd = lax.rem(z, 2) == 1
    factor = 1.0 / math.sqrt(HD)
    c2 = factor * LOG2E

    def mod8(v):
        return lax.rem(v + 16, 8)

    def device(xx, cc):
        return {"dp": 2 * yhi + cc, "head": 2 * xx + ylo}

    partner = {"dp": 2 * yhi + ylo, "head": 2 * x + c}
    sibling = {"dp": 2 * yhi + (1 - c)}

    def member(d):
        dx, dc = d // 2, d % 2
        xx = lax.rem(x + dx, 4)
        cc = c if dc == 0 else 1 - c
        return xx, cc

    def giver(d):
        dx, dc = d // 2, d % 2
        xx = lax.rem(x + 4 - dx, 4)
        cc = c if dc == 0 else 1 - c
        return 2 * xx + cc

    def remote(src, dst, ssem, rsem, dev):
        return pltpu.make_async_remote_copy(
            src_ref=src, dst_ref=dst, send_sem=ssem, recv_sem=rsem,
            device_id=dev, device_id_type=MESH,
        )

    pending = []

    def start(copy):
        copy.start()
        pending.append(copy)
        return copy

    def when(cond, fn):
        pl.when(cond)(fn)

    barrier = pltpu.get_barrier_semaphore()

    def greet(dev):
        pl.semaphore_signal(barrier, inc=1, device_id=dev, device_id_type=MESH)

    for d in range(1, 8):
        greet({"seq": mod8(z + d)})
        greet(device(*member(d)))
    others = []
    for e in range(1, 4):
        yh = yhi if e // 2 == 0 else 1 - yhi
        yl = ylo if e % 2 == 0 else 1 - ylo
        others.append({"dp": 2 * yh + c, "head": 2 * x + yl})
        greet(others[-1])
    when(moved, lambda: greet(partner))

    weights = [
        pltpu.make_async_copy(wqkv_hbm, wqkv, ins.at[0]),
        pltpu.make_async_copy(wout_hbm, wout, ins.at[1]),
    ]
    stay = [
        pltpu.make_async_copy(tok_hbm, tok, ins.at[2]),
        pltpu.make_async_copy(gout_hbm, gog.at[0], ins.at[3]),
        pltpu.make_async_copy(bins_hbm, bins, ins.at[4]),
        pltpu.make_async_copy(pat_hbm, patv, ins.at[5]),
    ]
    go = [
        remote(tok_hbm, tok, sws.at[0], swr.at[0], partner),
        remote(gout_hbm, gog.at[0], sws.at[1], swr.at[1], partner),
    ]
    share = [
        remote(bins_hbm, bins, sws.at[2], swr.at[2], sibling),
        remote(pat_hbm, patv, sws.at[5], swr.at[5], sibling),
    ]
    for copy in weights:
        copy.start()
    when(jnp.logical_not(moved), lambda: [copy.start() for copy in stay] and None)

    lane = lax.broadcasted_iota(jnp.int32, (BLK, 2 * HD), 1)
    low = lane < HD

    def swap(v):
        return pltpu.roll(v, HD, 1)

    for copy in weights:
        copy.wait()
    pair = pl.multiple_of((z // 2) * 384, 128)
    for q in range(4):
        rows = slice(128 * q, 128 * (q + 1))
        w0 = wqkv[rows, pl.ds(pair, 128)].astype(F32)
        w1 = wqkv[rows, pl.ds(pair + 128, 128)].astype(F32)
        w2 = wqkv[rows, pl.ds(pair + 256, 128)].astype(F32)
        s1 = swap(w1)
        wcat[rows, 0:128] = jnp.where(odd, w2, jnp.where(low, swap(w0), s1)).astype(BF16)
        wcat[rows, 128:256] = jnp.where(low, jnp.where(odd, s1, w0), 0.0).astype(BF16)
    wo_pair = wout[pl.ds(pl.multiple_of((z // 2) * 128, 128), 128), :]
    wo2[0:HD, :] = jnp.zeros((HD, D), BF16)
    wo2[HD:BLK, :] = jnp.where(odd, wo_pair[HD:BLK, :], wo_pair[0:HD, :])

    pl.semaphore_wait(barrier, 17 + jnp.where(moved, 1, 0))
    when(moved, lambda: [copy.start() for copy in go] and None)
    when(jnp.logical_not(moved), lambda: [copy.start() for copy in share] and None)

    when(moved, lambda: go[0].wait_recv())
    when(jnp.logical_not(moved), lambda: stay[0].wait())

    tokens = tok[...].astype(F32)
    spread = jnp.sqrt(jnp.mean(tokens * tokens, axis=-1, keepdims=True) + EPSILON)
    normed = tokens / spread
    normed_ref[...] = normed
    spread_ref[...] = spread
    hid[0] = normed.astype(BF16)

    rings = (hid, gog)
    table = {}

    def hop(k, way, t, part):
        if way == 0:
            src, dst = (0 if t == 1 else 2 * (t - 1)), (2 * t if t < 4 else 7)
        else:
            src, dst = (0 if t == 1 else 2 * (t - 1) - 1), 2 * t - 1
        rows = pl.ds(64 * part, 64)
        return remote(
            rings[k].at[src, rows], rings[k].at[dst, rows],
            zs.at[k, way, t, part], zr.at[k, way, t, part],
            {"seq": mod8(z + 1) if way == 0 else mod8(z - 1)},
        )

    def first_hop(k):
        for part in (0, 1):
            for way in (0, 1):
                table[k, way, 1, part] = start(hop(k, way, 1, part))

    def next_hop(k, t):
        for part in (0, 1):
            for way in (0, 1):
                table[k, way, t, part].wait_recv()
                if t + 1 < 4 or (t + 1 == 4 and part == way):
                    table[k, way, t + 1, part] = start(hop(k, way, t + 1, part))

    def last_hop(k):
        for way in (0, 1):
            table[k, way, 4, way].wait_recv()

    pools = (gkv, gqd)
    ring_x = {}
    x_right, x_left = lax.rem(x + 1, 4), lax.rem(x + 3, 4)
    x_far = lax.rem(x + 2, 4)

    def xcopy(k, b, kind, owner, dev):
        first, count = BATCHES[b]
        part = pools[k].at[owner, pl.ds(first, count)]
        ring_x[k, b, kind] = start(
            remote(part, part, xs.at[k, b, kind], xr.at[k, b, kind], dev)
        )

    def x_own(k, b):
        xcopy(k, b, 0, r, device(x_right, c))
        xcopy(k, b, 1, r, device(x_left, c))
        xcopy(k, b, 2, r, sibling)

    def x_pass(k, b):
        ring_x[k, b, 0].wait_recv()
        if b in (0, 1, 4):
            xcopy(k, b, 5, 2 * x_left + c, device(x_right, c))
        xcopy(k, b, 3, 2 * x_left + c, sibling)
        ring_x[k, b, 1].wait_recv()
        if b in (2, 3):
            xcopy(k, b, 5, 2 * x_right + c, device(x_left, c))
        xcopy(k, b, 4, 2 * x_right + c, sibling)

    def x_far_pass(k, b):
        ring_x[k, b, 5].wait_recv()
        xcopy(k, b, 6, 2 * x_far + c, sibling)

    def x_end(k):
        for b in range(5):
            for kind in (2, 3, 4, 6):
                ring_x[k, b, kind].wait_recv()

    def project(b):
        first, count = BATCHES[b]
        for p in range(first, first + count):
            t = dot_nn(hid[p], wcat[...]).astype(BF16)
            gkv[r, p] = t[:, 0:128]
            gqd[r, p] = t[:, 128:256]
        x_own(0, b)

    def project_grad(b):
        first, count = BATCHES[b]
        for p in range(first, first + count):
            u = dot_nt(gog[p], wo2[...])
            gqd[r, p] = jnp.where(low, gqd[r, p], u.astype(BF16))
        x_own(1, b)

    first_hop(0)
    project(0)
    when(moved, lambda: go[1].wait_recv())
    when(jnp.logical_not(moved), lambda: stay[1].wait())
    next_hop(0, 1)
    first_hop(1)
    project(1)
    project_grad(0)
    next_hop(0, 2)
    project(2)
    x_pass(0, 0)
    x_pass(0, 1)
    next_hop(1, 1)
    project_grad(1)
    next_hop(0, 3)
    project(3)
    x_far_pass(0, 0)
    x_pass(0, 2)
    x_pass(1, 0)
    last_hop(0)
    project(4)
    next_hop(1, 2)
    project_grad(2)
    x_far_pass(0, 1)
    x_pass(0, 3)
    x_far_pass(0, 2)
    x_pass(0, 4)
    x_pass(1, 1)

    when(moved, lambda: [copy.wait_recv() for copy in share] and None)
    when(jnp.logical_not(moved), lambda: [copy.wait() for copy in stay[2:]] and None)
    to_scalars = pltpu.make_async_copy(patv, pat, ins.at[8])
    to_scalars.start()
    for q in range(NB):
        binsf[q : q + 1, :] = bins[:, tile(q)].astype(F32)
    binst[...] = jnp.concatenate([binsf[...], jnp.zeros((BLK - NB, BLK), F32)], axis=0).T
    to_scalars.wait()

    x_far_pass(0, 3)
    x_far_pass(0, 4)
    next_hop(1, 3)
    project_grad(3)
    x_end(0)

    bias2 = bias_ref[z] * LOG2E

    def distance(p):
        t = (p + 1) // 2
        return jnp.where(lax.rem(p, 2) == 1, t, 8 - t)

    def own_block(p):
        return 8 * mod8(z + distance(p)) + r

    far = (0, 1, 3, 5, 7, 6, 4, 2)

    def back(kind, src, dst, d):
        return remote(src, dst, ss.at[kind, d], rr.at[kind, d], {"seq": mod8(z + d)})

    def leave(kind, buf, dst, p):
        when(p > 0, lambda: back(kind, buf.at[p], dst.at[z], distance(p)).start())

    def left(kind, buf, dst):
        dst[z] = buf[0]
        copies = [back(kind, buf.at[far[d]], dst.at[z], d) for d in range(1, 8)]
        pending.extend(copies)
        return copies

    def used_block(row, n):
        other = lax.rem(row + pat[n, 0, 0], NB)
        return other, lax.rem(other, 8), place(mod8(other // 8 - z))

    def own_bins(row):
        return jnp.sum(jnp.where(lane == row, binst[...], 0.0), axis=1, keepdims=True)

    stcol[...] = jnp.zeros((BLK, BLK), F32)

    def forward_block(p, carry):
        row = own_block(p)
        for n in range(NNZ):
            _, rn, pn = used_block(row, n)
            ycats[p, tile(n), :] = gkv[rn, pn]
        query = gqd[r, p]
        sd[0:BLK, :] = dot_nt(jnp.where(low, query, jnp.zeros_like(query)), ycats[p])
        bin_col = own_bins(row)
        top = None
        for n in range(NNZ):
            other, _, _ = used_block(row, n)
            bin_row = binsf[pl.ds(other, 1), :]
            v = sd[0:BLK, tile(n)] * c2 + jnp.where(bin_col == bin_row, bias2, 0.0)
            sd[0:BLK, tile(n)] = v
            top = v if top is None else jnp.maximum(top, v)
        m = jnp.max(top, axis=1, keepdims=True)
        total = jnp.zeros((BLK, BLK), F32)
        for n in range(NNZ):
            e = jnp.exp2(sd[0:BLK, tile(n)] - m)
            probs[p, :, tile(n)] = e
            pd[0:BLK, tile(n)] = e.astype(BF16)
            total = total + e
        total = jnp.sum(total, axis=1, keepdims=True)
        inv = 1.0 / total
        obuf[p] = (dot_nn(pd[0:BLK, :], ycats[p]) * inv).astype(BF16)
        invs[p] = inv
        stcol[...] = jnp.where(lane == 2 * p, m + jnp.log2(total), stcol[...])
        return carry

    lax.fori_loop(0, PER, forward_block, 0)

    last_hop(1)
    project_grad(4)

    for p in range(PER):
        both = gqd[r, p].astype(F32) * obuf[p].astype(F32)
        delta = jnp.sum(jnp.where(low, 0.0, both), axis=1, keepdims=True)
        deltas[p] = delta
        stcol[...] = jnp.where(lane == 2 * p + 1, delta, stcol[...])
    strow[...] = stcol[...].T
    mine = stg.at[pl.ds(pl.multiple_of(2 * PER * r, 16), 16)]
    stg[pl.ds(pl.multiple_of(2 * PER * r, 16), 16), :] = strow[0:16, :]

    def group(kind, d, src, dst):
        return start(remote(src, dst, ss.at[kind, d], rr.at[kind, d], device(*member(d))))

    c_st = [group(G_ST, d, mine, mine) for d in range(1, 8)]
    x_far_pass(1, 0)
    x_far_pass(1, 1)
    x_pass(1, 2)
    x_pass(1, 3)
    x_pass(1, 4)

    def query_block(p, carry):
        block = gqd[r, p]
        sd[0:BLK, :] = dot_nt(jnp.where(low, jnp.zeros_like(block), block), ycats[p])
        delta = deltas[p]
        for n in range(NNZ):
            pd[0:BLK, tile(n)] = (
                probs[p, :, tile(n)] * (sd[0:BLK, tile(n)] - delta)
            ).astype(BF16)
        grad = dot_nn(pd[0:BLK, :], ycats[p]) * (invs[p] * factor)
        both = jnp.where(low, grad, obuf[p].astype(F32))
        bqo[p] = both.astype(BF16)
        leave(Z_BQO, bqo, rqo, p)
        dtqo[:, pl.ds(pl.multiple_of(p * BLK, BLK), BLK)] = both.T.astype(BF16)
        return carry

    lax.fori_loop(0, PER, query_block, 0)

    c_bqo = left(Z_BQO, bqo, rqo)
    x_far_pass(1, 2)
    x_far_pass(1, 3)
    x_far_pass(1, 4)

    def stage1(k, part):
        wpart[k] = part
        for q in range(8):
            ars[k, q] = part[16 * q : 16 * (q + 1), :].astype(BF16)
        sent = []
        for d in range(1, 8):
            xx, cc = member(d)
            sent.append(group((G_S1A, G_S1B)[k], d, ars.at[k, 2 * xx + cc], arr.at[k, r]))
        return sent

    def stage2(k, copies):
        total = wpart[k, pl.ds(pl.multiple_of(16 * r, 16), 16), :]
        for d, copy in zip(range(1, 8), copies):
            copy.wait_recv()
            total = total + arr[k, giver(d)].astype(F32)
        dpx[k, seqno] = total.astype(BF16)
        slot = dpx.at[k, seqno]
        return [
            start(remote(slot, slot, ys.at[k, e], yr.at[k, e], others[e - 1]))
            for e in range(1, 4)
        ]

    mine_here = lax.rem(z, 2) == ylo

    def stage3(k, copies):
        for copy in copies:
            copy.wait_recv()
        total = dpx[k, 0].astype(F32)
        for q in range(1, 4):
            total = total + dpx[k, q].astype(F32)

        def spread_out():
            zbc[k, z // 2] = total.astype(BF16)

        slot = zbc.at[k, z // 2]
        kind = (Z_S3A, Z_S3B)[k]
        sent = [
            remote(slot, slot, ss.at[kind, d], rr.at[kind, d], {"seq": mod8(z + d)})
            for d in range(1, 8)
        ]
        when(mine_here, spread_out)
        when(mine_here, lambda: [copy.start() for copy in sent] and None)
        return sent

    def stage4(k, copies):
        for d, copy in zip(range(1, 8), copies):
            when(lax.rem(z + 8 - d, 2) == ylo, lambda: copy.wait_recv())
        fin[k, r] = zbc[k, x]
        sent = []
        for d in range(1, 8):
            xx, _ = member(d)
            sent.append(group((G_S4A, G_S4B)[k], d, zbc.at[k, xx], fin.at[k, r]))
        when(mine_here, lambda: [copy.wait_send() for copy in copies] and None)
        return sent

    hid_all = hid[...].reshape(PER * BLK, D)
    go_all = gog[...].reshape(PER * BLK, D)
    part0 = jnp.concatenate(
        [dot_nn(dtqo[0:HD, :], hid_all), dot_nn(dtqo[HD : 2 * HD, :], go_all)], axis=0
    )
    s1a = stage1(0, part0)
    for copy in c_st:
        copy.wait_recv()
    x_end(1)

    def key_block(p, carry):
        row = own_block(p)
        for n in range(NNZ):
            _, rn, pn = used_block(row, n)
            ycat[tile(n), :] = gqd[rn, pn]
        block = gkv[r, p]
        zero = jnp.zeros_like(block)
        a2[0:BLK, :] = jnp.where(low, block, zero)
        a2[BLK : 2 * BLK, :] = jnp.where(low, zero, block)
        sd[...] = dot_nt(a2[...], ycat[...])
        bin_col = own_bins(row)
        for n in range(NNZ):
            other, rn, pn = used_block(row, n)
            bin_row = binsf[pl.ds(other, 1), :]
            log_row = stg[pl.ds(16 * rn + 2 * pn, 1), :]
            delta_row = stg[pl.ds(16 * rn + 2 * pn + 1, 1), :]
            v = sd[0:BLK, tile(n)] * c2 + jnp.where(bin_col == bin_row, bias2, 0.0)
            e = jnp.exp2(v - log_row)
            pd[0:BLK, tile(n)] = e.astype(BF16)
            pd[BLK : 2 * BLK, tile(n)] = (e * (sd[BLK : 2 * BLK, tile(n)] - delta_row)).astype(BF16)
        g = dot_nn(pd[...], ycat[...])
        both = jnp.where(low, g[BLK : 2 * BLK] * factor, g[0:BLK])
        bkv[p] = both.astype(BF16)
        leave(Z_BKV, bkv, rkv, p)
        dtkv[:, pl.ds(pl.multiple_of(p * BLK, BLK), BLK)] = both.T.astype(BF16)
        return carry

    lax.fori_loop(0, PER, key_block, 0)

    c_bkv = left(Z_BKV, bkv, rkv)
    s1b = stage1(1, dot_nn(dtkv[...], hid[...].reshape(PER * BLK, D)))
    s2a = stage2(0, s1a)

    def deliver(src, dst, k):
        here = pltpu.make_async_copy(src, dst, ins.at[6 + k])
        there = remote(src, dst, sws.at[3 + k], swr.at[3 + k], partner)
        when(jnp.logical_not(moved), lambda: here.start())
        when(moved, lambda: there.start())
        return here, there

    for copy in c_bqo:
        copy.wait_recv()
    for g in range(HEADS // 2):
        even, uneven = rqo[2 * g].astype(F32), rqo[2 * g + 1].astype(F32)
        att[:, tile(g)] = jnp.where(low, swap(even), uneven).astype(BF16)
    res[...] = dot_nn(att[...], wout[...]).astype(BF16)
    d_out = deliver(res, out_hbm, 0)
    s3a = stage3(0, s2a)
    s2b = stage2(1, s1b)
    s4a = stage4(0, s3a)
    s3b = stage3(1, s2b)

    for copy in c_bkv:
        copy.wait_recv()
    for g in range(HEADS // 2):
        qo_even, qo_odd = rqo[2 * g].astype(F32), rqo[2 * g + 1].astype(F32)
        kv_even = swap(rkv[2 * g].astype(F32))
        gp[:, tile(3 * g)] = jnp.where(low, qo_even, kv_even).astype(BF16)
        gp[:, tile(3 * g + 1)] = jnp.where(low, kv_even, swap(qo_odd)).astype(BF16)
        gp[:, tile(3 * g + 2)] = rkv[2 * g + 1]
    s4b = stage4(1, s3b)
    grad_hidden = dot_nt(gp[...], wqkv[...])
    normed = normed_ref[...]
    inner = jnp.mean(grad_hidden * normed, axis=-1, keepdims=True)
    gres[...] = ((grad_hidden - normed * inner) / spread_ref[...]).astype(BF16)
    d_gtok = deliver(gres, gtok_hbm, 1)

    for copy in s4a + s4b:
        copy.wait_recv()
    for copy in pending:
        copy.wait_send()
    when(moved, lambda: [copy.wait_send() for copy in go] and None)
    when(jnp.logical_not(moved), lambda: [copy.wait_send() for copy in share] and None)
    for here, there in (d_out, d_gtok):
        when(jnp.logical_not(moved), lambda: here.wait())
        when(moved, lambda: there.wait())


def finish(out_in, gtok_in, fin_ref, out_hbm, gtok_hbm, gqkv_ref, gwo_ref, sems):
    copies = [
        pltpu.make_async_copy(out_in, out_hbm, sems.at[0]),
        pltpu.make_async_copy(gtok_in, gtok_hbm, sems.at[1]),
    ]
    for copy in copies:
        copy.start()
    first = fin_ref[0].reshape(BLK, D).astype(F32)
    second = fin_ref[1].reshape(BLK, D).astype(F32)
    gwo_ref[...] = first[HD : 2 * HD, :]
    gqkv_ref[0:HD, :] = first[0:HD, :]
    gqkv_ref[HD : 3 * HD, :] = second
    for copy in copies:
        copy.wait()


def body(tokens, bin_ids, pattern, w_qkv, w_out, head_bias, grad_output):
    vmem = pl.BlockSpec(memory_space=pltpu.VMEM)
    smem = pl.BlockSpec(memory_space=pltpu.SMEM)
    hbm = pl.BlockSpec(memory_space=pltpu.HBM)
    dma = pltpu.SemaphoreType.DMA
    half = functools.partial(pltpu.VMEM, dtype=BF16)
    full = functools.partial(pltpu.VMEM, dtype=F32)
    scratch = [
        half((8, 8, BLK, 128)),
        half((8, 8, BLK, 128)),
        half((8, BLK, D)),
        half((8, BLK, D)),
        half((BLK, D)),
        half((D, 3 * D)),
        half((D, D)),
        pltpu.VMEM((1, NB * BLK), jnp.int32),
        pltpu.VMEM((NNZ, 1, NB), jnp.int32),
        pltpu.SMEM((NNZ, 1, NB), jnp.int32),
        half((D, 256)),
        half((BLK, D)),
        full((BLK, D)),
        full((BLK, 1)),
        half((PER, CAT, 128)),
        half((CAT, 128)),
        full((PER, BLK, CAT)),
        full((2 * BLK, CAT)),
        half((2 * BLK, CAT)),
        half((2 * BLK, 128)),
        full((BLK, BLK)),
        full((BLK, BLK)),
        full((2 * NB, BLK)),
        full((PER, BLK, 1)),
        full((PER, BLK, 1)),
        full((NB, BLK)),
        full((BLK, BLK)),
        half((8, BLK, 128)),
        half((8, BLK, 128)),
        half((8, BLK, 128)),
        half((8, BLK, 128)),
        half((8, BLK, 128)),
        half((BLK, PER * BLK)),
        half((BLK, PER * BLK)),
        full((2, BLK, D)),
        half((2, 8, 16, D)),
        half((2, 8, 16, D)),
        half((2, 4, 16, D)),
        half((2, 4, 16, D)),
        half((BLK, D)),
        half((BLK, 3 * D)),
        half((BLK, D)),
        half((BLK, D)),
        dma((9, 8)),
        dma((9, 8)),
        dma((2, 4)),
        dma((2, 4)),
        dma((2, 2, 5, 2)),
        dma((2, 2, 5, 2)),
        dma((2, 5, 7)),
        dma((2, 5, 7)),
        dma((9,)),
        dma((6,)),
        dma((6,)),
    ]
    shapes = (
        jax.ShapeDtypeStruct((BLK, D), BF16),
        jax.ShapeDtypeStruct((BLK, D), BF16),
    )
    parts = pl.pallas_call(
        kernel,
        out_shape=shapes + (jax.ShapeDtypeStruct((2, 8, 16, D), BF16),),
        in_specs=[smem, hbm, hbm, hbm, hbm, hbm, hbm],
        out_specs=(hbm, hbm, vmem),
        scratch_shapes=scratch,
        compiler_params=pltpu.CompilerParams(
            collective_id=0, has_side_effects=True, vmem_limit_bytes=62 * 1024 * 1024
        ),
        name="layer",
    )(head_bias, tokens[0], grad_output[0], w_qkv, w_out, bin_ids, pattern.transpose(2, 0, 1))
    result, grad_input, own_qkv, own_out = pl.pallas_call(
        finish,
        out_shape=shapes
        + (
            jax.ShapeDtypeStruct((3 * HD, D), F32),
            jax.ShapeDtypeStruct((HD, D), F32),
        ),
        in_specs=[hbm, hbm, vmem],
        out_specs=(hbm, hbm, vmem, vmem),
        scratch_shapes=[dma((2,))],
        name="finish",
    )(*parts)
    return (result[None], grad_input[None], own_qkv.T, own_out)


def solution(mesh):
    return jax.shard_map(
        body,
        mesh=mesh,
        in_specs=(
            P("dp", ("seq", "head"), None),
            P("dp", None),
            P("dp", None, None),
            P(),
            P(),
            P(),
            P("dp", ("seq", "head"), None),
        ),
        out_specs=(
            P("dp", ("seq", "head"), None),
            P("dp", ("seq", "head"), None),
            P(None, "head"),
            P("head", None),
        ),
        check_vma=False,
    )
```

```python
import functools
import math

import jax
import jax.numpy as jnp
from jax import lax
from jax.experimental import pallas as pl
from jax.experimental.pallas import tpu as pltpu
from jax.sharding import PartitionSpec as P

D = 512
HEADS = 8
HD = 64
BLK = 128
NNZ = 9
PER = 8
NB = 64
EPSILON = 1e-05
LOG2E = math.log2(math.e)
MESH = pl.DeviceIdType.MESH
F32 = jnp.float32
BF16 = jnp.bfloat16
CAT = NNZ * BLK

BATCHES = ((0, 1), (1, 2), (3, 2), (5, 2), (7, 1))

(
    Z_BQO, Z_BKV, Z_S3A, Z_S3B, G_ST, G_S1A, G_S1B, G_S4A, G_S4B,
) = range(9)


def dot_nn(a, b):
    return lax.dot_general(a, b, (((1,), (0,)), ((), ())), preferred_element_type=F32)


def dot_nt(a, b):
    return lax.dot_general(a, b, (((1,), (1,)), ((), ())), preferred_element_type=F32)


def place(rel):
    return jnp.where(rel == 0, 0, jnp.where(rel <= 4, 2 * rel - 1, 16 - 2 * rel))


def tile(n):
    return slice(n * BLK, (n + 1) * BLK)


def kernel(
    bias_ref, tok_hbm, gout_hbm, wqkv_hbm, wout_hbm, bins_hbm, pat_hbm,
    out_ref, gtok_ref, fin,
    gkv, gqd, hid, gog, tok, tok_in, gout_in, bins_in, pat_in, wqkv, wout, bins, patv, pat, wcat, wo2, normed_ref, spread_ref,
    ycats, ycat, probs, sd, pd, a2, stcol, strow, stg, deltas, invs, binsf, binst,
    obuf, bqo, bkv, rqo, rkv, dtqo, dtkv,
    wpart, ars, arr, dpx, zbc, att, gp, res, gres,
    ss, rr, ys, yr, zs, zr, xs, xr, ins, sws, swr,
):
    dp = lax.axis_index("dp")
    z = lax.axis_index("seq")
    head = lax.axis_index("head")
    yhi, c = dp // 2, lax.rem(dp, 2)
    x, ylo = head // 2, lax.rem(head, 2)
    r = 2 * x + c
    seqno = 2 * yhi + ylo
    moved = c != ylo
    odd = lax.rem(z, 2) == 1
    factor = 1.0 / math.sqrt(HD)
    c2 = factor * LOG2E

    def mod8(v):
        return lax.rem(v + 16, 8)

    def device(xx, cc):
        return {"dp": 2 * yhi + cc, "head": 2 * xx + ylo}

    partner = {"dp": 2 * yhi + ylo, "head": 2 * x + c}
    sibling = {"dp": 2 * yhi + (1 - c)}

    def member(d):
        dx, dc = d // 2, d % 2
        xx = lax.rem(x + dx, 4)
        cc = c if dc == 0 else 1 - c
        return xx, cc

    def giver(d):
        dx, dc = d // 2, d % 2
        xx = lax.rem(x + 4 - dx, 4)
        cc = c if dc == 0 else 1 - c
        return 2 * xx + cc

    def remote(src, dst, ssem, rsem, dev):
        return pltpu.make_async_remote_copy(
            src_ref=src, dst_ref=dst, send_sem=ssem, recv_sem=rsem,
            device_id=dev, device_id_type=MESH,
        )

    pending = []

    def start(copy):
        copy.start()
        pending.append(copy)
        return copy

    def when(cond, fn):
        pl.when(cond)(fn)

    barrier = pltpu.get_barrier_semaphore()

    def greet(dev):
        pl.semaphore_signal(barrier, inc=1, device_id=dev, device_id_type=MESH)

    for d in range(1, 8):
        greet({"seq": mod8(z + d)})
        greet(device(*member(d)))
    others = []
    for e in range(1, 4):
        yh = yhi if e // 2 == 0 else 1 - yhi
        yl = ylo if e % 2 == 0 else 1 - ylo
        others.append({"dp": 2 * yh + c, "head": 2 * x + yl})
        greet(others[-1])
    when(moved, lambda: greet(partner))

    weights = [
        pltpu.make_async_copy(wqkv_hbm, wqkv, ins.at[0]),
        pltpu.make_async_copy(wout_hbm, wout, ins.at[1]),
    ]
    loads = [
        pltpu.make_async_copy(tok_hbm, tok_in, ins.at[2]),
        pltpu.make_async_copy(gout_hbm, gout_in, ins.at[3]),
        pltpu.make_async_copy(bins_hbm, bins_in, ins.at[4]),
        pltpu.make_async_copy(pat_hbm, pat_in, ins.at[5]),
    ]
    go = [
        remote(tok_in, tok, sws.at[0], swr.at[0], partner),
        remote(gout_in, gog.at[0], sws.at[1], swr.at[1], partner),
    ]
    share = [
        remote(bins_in, bins, sws.at[2], swr.at[2], sibling),
        remote(pat_in, patv, sws.at[5], swr.at[5], sibling),
    ]
    for copy in loads + weights:
        copy.start()
    stays = jnp.logical_not(moved)

    lane = lax.broadcasted_iota(jnp.int32, (BLK, 2 * HD), 1)
    low = lane < HD

    def swap(v):
        return pltpu.roll(v, HD, 1)

    for copy in weights:
        copy.wait()
    pair = pl.multiple_of((z // 2) * 384, 128)
    for q in range(4):
        rows = slice(128 * q, 128 * (q + 1))
        w0 = wqkv[rows, pl.ds(pair, 128)].astype(F32)
        w1 = wqkv[rows, pl.ds(pair + 128, 128)].astype(F32)
        w2 = wqkv[rows, pl.ds(pair + 256, 128)].astype(F32)
        s1 = swap(w1)
        wcat[rows, 0:128] = jnp.where(odd, w2, jnp.where(low, swap(w0), s1)).astype(BF16)
        wcat[rows, 128:256] = jnp.where(low, jnp.where(odd, s1, w0), 0.0).astype(BF16)
    wo_pair = wout[pl.ds(pl.multiple_of((z // 2) * 128, 128), 128), :]
    wo2[0:HD, :] = jnp.zeros((HD, D), BF16)
    wo2[HD:BLK, :] = jnp.where(odd, wo_pair[HD:BLK, :], wo_pair[0:HD, :])

    for copy in loads:
        copy.wait()

    def keep(dst, src):
        def fn():
            dst[...] = src[...]

        when(stays, fn)

    keep(tok, tok_in)
    keep(gog.at[0], gout_in)
    keep(bins, bins_in)
    keep(patv, pat_in)

    pl.semaphore_wait(barrier, 17 + jnp.where(moved, 1, 0))
    when(moved, lambda: go[0].start())
    when(moved, lambda: go[0].wait_recv())

    tokens = tok[...].astype(F32)
    spread = jnp.sqrt(jnp.mean(tokens * tokens, axis=-1, keepdims=True) + EPSILON)
    normed = tokens / spread
    normed_ref[...] = normed
    spread_ref[...] = spread
    hid[0] = normed.astype(BF16)

    rings = (hid, gog)
    table = {}

    def hop(k, way, t, part):
        if way == 0:
            src, dst = (0 if t == 1 else 2 * (t - 1)), (2 * t if t < 4 else 7)
        else:
            src, dst = (0 if t == 1 else 2 * (t - 1) - 1), 2 * t - 1
        rows = pl.ds(64 * part, 64)
        return remote(
            rings[k].at[src, rows], rings[k].at[dst, rows],
            zs.at[k, way, t, part], zr.at[k, way, t, part],
            {"seq": mod8(z + 1) if way == 0 else mod8(z - 1)},
        )

    def first_hop(k):
        for part in (0, 1):
            for way in (0, 1):
                table[k, way, 1, part] = start(hop(k, way, 1, part))

    def next_hop(k, t):
        for part in (0, 1):
            for way in (0, 1):
                table[k, way, t, part].wait_recv()
                if t + 1 < 4 or (t + 1 == 4 and part == way):
                    table[k, way, t + 1, part] = start(hop(k, way, t + 1, part))

    def last_hop(k):
        for way in (0, 1):
            table[k, way, 4, way].wait_recv()

    pools = (gkv, gqd)
    ring_x = {}
    x_right, x_left = lax.rem(x + 1, 4), lax.rem(x + 3, 4)
    x_far = lax.rem(x + 2, 4)

    def xcopy(k, b, kind, owner, dev):
        first, count = BATCHES[b]
        part = pools[k].at[owner, pl.ds(first, count)]
        ring_x[k, b, kind] = start(
            remote(part, part, xs.at[k, b, kind], xr.at[k, b, kind], dev)
        )

    def x_own(k, b):
        xcopy(k, b, 0, r, device(x_right, c))
        xcopy(k, b, 1, r, device(x_left, c))
        xcopy(k, b, 2, r, sibling)

    def x_pass(k, b):
        ring_x[k, b, 0].wait_recv()
        if b in (0, 1, 4):
            xcopy(k, b, 5, 2 * x_left + c, device(x_right, c))
        xcopy(k, b, 3, 2 * x_left + c, sibling)
        ring_x[k, b, 1].wait_recv()
        if b in (2, 3):
            xcopy(k, b, 5, 2 * x_right + c, device(x_left, c))
        xcopy(k, b, 4, 2 * x_right + c, sibling)

    def x_far_pass(k, b):
        ring_x[k, b, 5].wait_recv()
        xcopy(k, b, 6, 2 * x_far + c, sibling)

    def x_end(k):
        for b in range(5):
            for kind in (2, 3, 4, 6):
                ring_x[k, b, kind].wait_recv()

    def project(b):
        first, count = BATCHES[b]
        for p in range(first, first + count):
            t = dot_nn(hid[p], wcat[...]).astype(BF16)
            gkv[r, p] = t[:, 0:128]
            gqd[r, p] = t[:, 128:256]
        x_own(0, b)

    def project_grad(b):
        first, count = BATCHES[b]
        for p in range(first, first + count):
            u = dot_nt(gog[p], wo2[...])
            gqd[r, p] = jnp.where(low, gqd[r, p], u.astype(BF16))
        x_own(1, b)

    first_hop(0)
    when(moved, lambda: go[1].start())
    when(stays, lambda: [copy.start() for copy in share] and None)
    project(0)
    next_hop(0, 1)
    project(1)
    next_hop(0, 2)
    project(2)
    x_pass(0, 0)
    next_hop(0, 3)
    when(moved, lambda: go[1].wait_recv())
    first_hop(1)
    project(3)
    project_grad(0)
    x_pass(0, 1)
    last_hop(0)
    project(4)
    x_far_pass(0, 0)
    x_pass(0, 2)
    x_far_pass(0, 1)
    next_hop(1, 1)
    project_grad(1)
    x_pass(0, 3)
    x_far_pass(0, 2)
    x_pass(0, 4)
    x_pass(1, 0)

    when(moved, lambda: [copy.wait_recv() for copy in share] and None)
    to_scalars = pltpu.make_async_copy(patv, pat, ins.at[8])
    to_scalars.start()
    for q in range(NB):
        binsf[q : q + 1, :] = bins[:, tile(q)].astype(F32)
    binst[...] = jnp.concatenate([binsf[...], jnp.zeros((BLK - NB, BLK), F32)], axis=0).T
    to_scalars.wait()

    x_far_pass(0, 3)
    x_far_pass(0, 4)
    next_hop(1, 2)
    project_grad(2)
    x_pass(1, 1)
    x_end(0)

    bias2 = bias_ref[z] * LOG2E

    def distance(p):
        t = (p + 1) // 2
        return jnp.where(lax.rem(p, 2) == 1, t, 8 - t)

    def own_block(p):
        return 8 * mod8(z + distance(p)) + r

    far = (0, 1, 3, 5, 7, 6, 4, 2)

    def back(kind, src, dst, d):
        return remote(src, dst, ss.at[kind, d], rr.at[kind, d], {"seq": mod8(z + d)})

    def leave(kind, buf, dst, p):
        when(p > 0, lambda: back(kind, buf.at[p], dst.at[z], distance(p)).start())

    def left(kind, buf, dst):
        dst[z] = buf[0]
        copies = [back(kind, buf.at[far[d]], dst.at[z], d) for d in range(1, 8)]
        pending.extend(copies)
        return copies

    def used_block(row, n):
        other = lax.rem(row + pat[n, 0, 0], NB)
        return other, lax.rem(other, 8), place(mod8(other // 8 - z))

    def own_bins(row):
        return jnp.sum(jnp.where(lane == row, binst[...], 0.0), axis=1, keepdims=True)

    stcol[...] = jnp.zeros((BLK, BLK), F32)

    def forward_block(p, carry):
        row = own_block(p)
        for n in range(NNZ):
            _, rn, pn = used_block(row, n)
            ycats[p, tile(n), :] = gkv[rn, pn]
        query = gqd[r, p]
        sd[0:BLK, :] = dot_nt(jnp.where(low, query, jnp.zeros_like(query)), ycats[p])
        bin_col = own_bins(row)
        top = None
        for n in range(NNZ):
            other, _, _ = used_block(row, n)
            bin_row = binsf[pl.ds(other, 1), :]
            v = sd[0:BLK, tile(n)] * c2 + jnp.where(bin_col == bin_row, bias2, 0.0)
            sd[0:BLK, tile(n)] = v
            top = v if top is None else jnp.maximum(top, v)
        m = jnp.max(top, axis=1, keepdims=True)
        total = jnp.zeros((BLK, BLK), F32)
        for n in range(NNZ):
            e = jnp.exp2(sd[0:BLK, tile(n)] - m)
            probs[p, :, tile(n)] = e
            pd[0:BLK, tile(n)] = e.astype(BF16)
            total = total + e
        total = jnp.sum(total, axis=1, keepdims=True)
        inv = 1.0 / total
        obuf[p] = (dot_nn(pd[0:BLK, :], ycats[p]) * inv).astype(BF16)
        invs[p] = inv
        stcol[...] = jnp.where(lane == 2 * p, m + jnp.log2(total), stcol[...])
        return carry

    lax.fori_loop(0, PER, forward_block, 0)
    next_hop(1, 3)
    project_grad(3)

    last_hop(1)
    project_grad(4)

    for p in range(PER):
        both = gqd[r, p].astype(F32) * obuf[p].astype(F32)
        delta = jnp.sum(jnp.where(low, 0.0, both), axis=1, keepdims=True)
        deltas[p] = delta
        stcol[...] = jnp.where(lane == 2 * p + 1, delta, stcol[...])
    strow[...] = stcol[...].T
    mine = stg.at[pl.ds(pl.multiple_of(2 * PER * r, 16), 16)]
    stg[pl.ds(pl.multiple_of(2 * PER * r, 16), 16), :] = strow[0:16, :]

    def group(kind, d, src, dst):
        return start(remote(src, dst, ss.at[kind, d], rr.at[kind, d], device(*member(d))))

    c_st = [group(G_ST, d, mine, mine) for d in range(1, 8)]
    x_far_pass(1, 0)
    x_far_pass(1, 1)
    x_pass(1, 2)
    x_pass(1, 3)
    x_pass(1, 4)

    def query_block(p, carry):
        block = gqd[r, p]
        sd[0:BLK, :] = dot_nt(jnp.where(low, jnp.zeros_like(block), block), ycats[p])
        delta = deltas[p]
        for n in range(NNZ):
            pd[0:BLK, tile(n)] = (
                probs[p, :, tile(n)] * (sd[0:BLK, tile(n)] - delta)
            ).astype(BF16)
        grad = dot_nn(pd[0:BLK, :], ycats[p]) * (invs[p] * factor)
        both = jnp.where(low, grad, obuf[p].astype(F32))
        bqo[p] = both.astype(BF16)
        leave(Z_BQO, bqo, rqo, p)
        dtqo[:, pl.ds(pl.multiple_of(p * BLK, BLK), BLK)] = both.T.astype(BF16)
        return carry

    lax.fori_loop(0, PER, query_block, 0)

    c_bqo = left(Z_BQO, bqo, rqo)
    x_far_pass(1, 2)
    x_far_pass(1, 3)
    x_far_pass(1, 4)

    def stage1(k, part):
        wpart[k] = part
        for q in range(8):
            ars[k, q] = part[16 * q : 16 * (q + 1), :].astype(BF16)
        sent = []
        for d in range(1, 8):
            xx, cc = member(d)
            sent.append(group((G_S1A, G_S1B)[k], d, ars.at[k, 2 * xx + cc], arr.at[k, r]))
        return sent

    def stage2(k, copies):
        total = wpart[k, pl.ds(pl.multiple_of(16 * r, 16), 16), :]
        for d, copy in zip(range(1, 8), copies):
            copy.wait_recv()
            total = total + arr[k, giver(d)].astype(F32)
        dpx[k, seqno] = total.astype(BF16)
        slot = dpx.at[k, seqno]
        return [
            start(remote(slot, slot, ys.at[k, e], yr.at[k, e], others[e - 1]))
            for e in range(1, 4)
        ]

    mine_here = lax.rem(z, 2) == ylo

    def stage3(k, copies):
        for copy in copies:
            copy.wait_recv()
        total = dpx[k, 0].astype(F32)
        for q in range(1, 4):
            total = total + dpx[k, q].astype(F32)

        def spread_out():
            zbc[k, z // 2] = total.astype(BF16)

        slot = zbc.at[k, z // 2]
        kind = (Z_S3A, Z_S3B)[k]
        sent = [
            remote(slot, slot, ss.at[kind, d], rr.at[kind, d], {"seq": mod8(z + d)})
            for d in range(1, 8)
        ]
        when(mine_here, spread_out)
        when(mine_here, lambda: [copy.start() for copy in sent] and None)
        return sent

    def stage4(k, copies):
        for d, copy in zip(range(1, 8), copies):
            when(lax.rem(z + 8 - d, 2) == ylo, lambda: copy.wait_recv())
        fin[k, r] = zbc[k, x]
        sent = []
        for d in range(1, 8):
            xx, _ = member(d)
            sent.append(group((G_S4A, G_S4B)[k], d, zbc.at[k, xx], fin.at[k, r]))
        when(mine_here, lambda: [copy.wait_send() for copy in copies] and None)
        return sent

    hid_all = hid[...].reshape(PER * BLK, D)
    go_all = gog[...].reshape(PER * BLK, D)
    part0 = jnp.concatenate(
        [dot_nn(dtqo[0:HD, :], hid_all), dot_nn(dtqo[HD : 2 * HD, :], go_all)], axis=0
    )
    s1a = stage1(0, part0)
    for copy in c_st:
        copy.wait_recv()
    x_end(1)

    def key_block(p, carry):
        row = own_block(p)
        for n in range(NNZ):
            _, rn, pn = used_block(row, n)
            ycat[tile(n), :] = gqd[rn, pn]
        block = gkv[r, p]
        zero = jnp.zeros_like(block)
        a2[0:BLK, :] = jnp.where(low, block, zero)
        a2[BLK : 2 * BLK, :] = jnp.where(low, zero, block)
        sd[...] = dot_nt(a2[...], ycat[...])
        bin_col = own_bins(row)
        for n in range(NNZ):
            other, rn, pn = used_block(row, n)
            bin_row = binsf[pl.ds(other, 1), :]
            log_row = stg[pl.ds(16 * rn + 2 * pn, 1), :]
            delta_row = stg[pl.ds(16 * rn + 2 * pn + 1, 1), :]
            v = sd[0:BLK, tile(n)] * c2 + jnp.where(bin_col == bin_row, bias2, 0.0)
            e = jnp.exp2(v - log_row)
            pd[0:BLK, tile(n)] = e.astype(BF16)
            pd[BLK : 2 * BLK, tile(n)] = (e * (sd[BLK : 2 * BLK, tile(n)] - delta_row)).astype(BF16)
        g = dot_nn(pd[...], ycat[...])
        both = jnp.where(low, g[BLK : 2 * BLK] * factor, g[0:BLK])
        bkv[p] = both.astype(BF16)
        leave(Z_BKV, bkv, rkv, p)
        dtkv[:, pl.ds(pl.multiple_of(p * BLK, BLK), BLK)] = both.T.astype(BF16)
        return carry

    lax.fori_loop(0, PER, key_block, 0)

    c_bkv = left(Z_BKV, bkv, rkv)
    s1b = stage1(1, dot_nn(dtkv[...], hid[...].reshape(PER * BLK, D)))
    s2a = stage2(0, s1a)

    def deliver(src, dst, k):
        there = remote(src, dst, sws.at[3 + k], swr.at[3 + k], partner)
        keep(dst, src)
        when(moved, lambda: there.start())
        return there

    for copy in c_bqo:
        copy.wait_recv()
    for g in range(HEADS // 2):
        even, uneven = rqo[2 * g].astype(F32), rqo[2 * g + 1].astype(F32)
        att[:, tile(g)] = jnp.where(low, swap(even), uneven).astype(BF16)
    res[...] = dot_nn(att[...], wout[...]).astype(BF16)
    d_out = deliver(res, out_ref, 0)
    s3a = stage3(0, s2a)
    s2b = stage2(1, s1b)
    s4a = stage4(0, s3a)
    s3b = stage3(1, s2b)

    for copy in c_bkv:
        copy.wait_recv()
    for g in range(HEADS // 2):
        qo_even, qo_odd = rqo[2 * g].astype(F32), rqo[2 * g + 1].astype(F32)
        kv_even = swap(rkv[2 * g].astype(F32))
        gp[:, tile(3 * g)] = jnp.where(low, qo_even, kv_even).astype(BF16)
        gp[:, tile(3 * g + 1)] = jnp.where(low, kv_even, swap(qo_odd)).astype(BF16)
        gp[:, tile(3 * g + 2)] = rkv[2 * g + 1]
    s4b = stage4(1, s3b)
    grad_hidden = dot_nt(gp[...], wqkv[...])
    normed = normed_ref[...]
    inner = jnp.mean(grad_hidden * normed, axis=-1, keepdims=True)
    gres[...] = ((grad_hidden - normed * inner) / spread_ref[...]).astype(BF16)
    d_gtok = deliver(gres, gtok_ref, 1)

    for copy in s4a + s4b:
        copy.wait_recv()
    for copy in pending:
        copy.wait_send()
    when(moved, lambda: [copy.wait_send() for copy in go] and None)
    when(stays, lambda: [copy.wait_send() for copy in share] and None)
    for there in (d_out, d_gtok):
        when(moved, lambda: there.wait())


def finish(out_in, gtok_in, fin_ref, out_ref, gtok_ref, gqkv_ref, gwo_ref):
    out_ref[...] = out_in[...]
    gtok_ref[...] = gtok_in[...]
    first = fin_ref[0].reshape(BLK, D).astype(F32)
    second = fin_ref[1].reshape(BLK, D).astype(F32)
    gwo_ref[...] = first[HD : 2 * HD, :]
    gqkv_ref[0:HD, :] = first[0:HD, :]
    gqkv_ref[HD : 3 * HD, :] = second


def body(tokens, bin_ids, pattern, w_qkv, w_out, head_bias, grad_output):
    vmem = pl.BlockSpec(memory_space=pltpu.VMEM)
    smem = pl.BlockSpec(memory_space=pltpu.SMEM)
    hbm = pl.BlockSpec(memory_space=pltpu.HBM)
    dma = pltpu.SemaphoreType.DMA
    half = functools.partial(pltpu.VMEM, dtype=BF16)
    full = functools.partial(pltpu.VMEM, dtype=F32)
    scratch = [
        half((8, 8, BLK, 128)),
        half((8, 8, BLK, 128)),
        half((8, BLK, D)),
        half((8, BLK, D)),
        half((BLK, D)),
        half((BLK, D)),
        half((BLK, D)),
        pltpu.VMEM((1, NB * BLK), jnp.int32),
        pltpu.VMEM((NNZ, 1, NB), jnp.int32),
        half((D, 3 * D)),
        half((D, D)),
        pltpu.VMEM((1, NB * BLK), jnp.int32),
        pltpu.VMEM((NNZ, 1, NB), jnp.int32),
        pltpu.SMEM((NNZ, 1, NB), jnp.int32),
        half((D, 256)),
        half((BLK, D)),
        full((BLK, D)),
        full((BLK, 1)),
        half((PER, CAT, 128)),
        half((CAT, 128)),
        full((PER, BLK, CAT)),
        full((2 * BLK, CAT)),
        half((2 * BLK, CAT)),
        half((2 * BLK, 128)),
        full((BLK, BLK)),
        full((BLK, BLK)),
        full((2 * NB, BLK)),
        full((PER, BLK, 1)),
        full((PER, BLK, 1)),
        full((NB, BLK)),
        full((BLK, BLK)),
        half((8, BLK, 128)),
        half((8, BLK, 128)),
        half((8, BLK, 128)),
        half((8, BLK, 128)),
        half((8, BLK, 128)),
        half((BLK, PER * BLK)),
        half((BLK, PER * BLK)),
        full((2, BLK, D)),
        half((2, 8, 16, D)),
        half((2, 8, 16, D)),
        half((2, 4, 16, D)),
        half((2, 4, 16, D)),
        half((BLK, D)),
        half((BLK, 3 * D)),
        half((BLK, D)),
        half((BLK, D)),
        dma((9, 8)),
        dma((9, 8)),
        dma((2, 4)),
        dma((2, 4)),
        dma((2, 2, 5, 2)),
        dma((2, 2, 5, 2)),
        dma((2, 5, 7)),
        dma((2, 5, 7)),
        dma((9,)),
        dma((6,)),
        dma((6,)),
    ]
    shapes = (
        jax.ShapeDtypeStruct((BLK, D), BF16),
        jax.ShapeDtypeStruct((BLK, D), BF16),
    )
    parts = pl.pallas_call(
        kernel,
        out_shape=shapes + (jax.ShapeDtypeStruct((2, 8, 16, D), BF16),),
        in_specs=[smem, hbm, hbm, hbm, hbm, hbm, hbm],
        out_specs=(vmem, vmem, vmem),
        scratch_shapes=scratch,
        compiler_params=pltpu.CompilerParams(
            collective_id=0, has_side_effects=True, vmem_limit_bytes=62 * 1024 * 1024
        ),
        name="layer",
    )(head_bias, tokens[0], grad_output[0], w_qkv, w_out, bin_ids, pattern.transpose(2, 0, 1))
    result, grad_input, own_qkv, own_out = pl.pallas_call(
        finish,
        out_shape=shapes
        + (
            jax.ShapeDtypeStruct((3 * HD, D), F32),
            jax.ShapeDtypeStruct((HD, D), F32),
        ),
        in_specs=[vmem, vmem, vmem],
        out_specs=(vmem, vmem, vmem, vmem),
        name="finish",
    )(*parts)
    return (result[None], grad_input[None], own_qkv.T, own_out)


def solution(mesh):
    return jax.shard_map(
        body,
        mesh=mesh,
        in_specs=(
            P("dp", ("seq", "head"), None),
            P("dp", None),
            P("dp", None, None),
            P(),
            P(),
            P(),
            P("dp", ("seq", "head"), None),
        ),
        out_specs=(
            P("dp", ("seq", "head"), None),
            P("dp", ("seq", "head"), None),
            P(None, "head"),
            P("head", None),
        ),
        check_vma=False,
    )
```

```python
import functools
import math

import jax
import jax.numpy as jnp
from jax import lax
from jax.experimental import pallas as pl
from jax.experimental.pallas import tpu as pltpu
from jax.sharding import PartitionSpec as P

D = 512
HEADS = 8
HD = 64
BLK = 128
NNZ = 9
PER = 8
NB = 64
EPSILON = 1e-05
LOG2E = math.log2(math.e)
MESH = pl.DeviceIdType.MESH
F32 = jnp.float32
BF16 = jnp.bfloat16
CAT = NNZ * BLK

BATCHES = ((0, 1), (1, 2), (3, 2), (5, 2), (7, 1))

(
    Z_BQO, Z_BKV, Z_S3A, Z_S3B, G_ST, G_S1A, G_S1B, G_S4A, G_S4B,
) = range(9)


def dot_nn(a, b):
    return lax.dot_general(a, b, (((1,), (0,)), ((), ())), preferred_element_type=F32)


def dot_nt(a, b):
    return lax.dot_general(a, b, (((1,), (1,)), ((), ())), preferred_element_type=F32)


def place(rel):
    return jnp.where(rel == 0, 0, jnp.where(rel <= 4, 2 * rel - 1, 16 - 2 * rel))


def tile(n):
    return slice(n * BLK, (n + 1) * BLK)


def kernel(
    bias_ref, tok_hbm, gout_hbm, wqkv_hbm, wout_hbm, bins_hbm, pat_hbm,
    out_ref, gtok_ref, fin,
    gkv, gqd, hid, gog, tok, tok_in, gout_in, bins_in, pat_in, wqkv, wout, bins, patv, pat, wcat, wo2, normed_ref, spread_ref,
    ycats, ycat, probs, sd, pd, a2, stcol, strow, stg, deltas, invs, binsf, binst,
    obuf, bqo, bkv, rqo, rkv, dtqo, dtkv,
    wpart, ars, arr, dpx, zbc, att, gp, res, gres,
    ss, rr, ys, yr, zs, zr, xs, xr, ins, sws, swr,
):
    dp = lax.axis_index("dp")
    z = lax.axis_index("seq")
    head = lax.axis_index("head")
    yhi, c = dp // 2, lax.rem(dp, 2)
    x, ylo = head // 2, lax.rem(head, 2)
    r = 2 * x + c
    seqno = 2 * yhi + ylo
    moved = c != ylo
    odd = lax.rem(z, 2) == 1
    factor = 1.0 / math.sqrt(HD)
    c2 = factor * LOG2E

    def mod8(v):
        return lax.rem(v + 16, 8)

    def device(xx, cc):
        return {"dp": 2 * yhi + cc, "head": 2 * xx + ylo}

    partner = {"dp": 2 * yhi + ylo, "head": 2 * x + c}
    sibling = {"dp": 2 * yhi + (1 - c)}

    def member(d):
        dx, dc = d // 2, d % 2
        xx = lax.rem(x + dx, 4)
        cc = c if dc == 0 else 1 - c
        return xx, cc

    def giver(d):
        dx, dc = d // 2, d % 2
        xx = lax.rem(x + 4 - dx, 4)
        cc = c if dc == 0 else 1 - c
        return 2 * xx + cc

    def remote(src, dst, ssem, rsem, dev):
        return pltpu.make_async_remote_copy(
            src_ref=src, dst_ref=dst, send_sem=ssem, recv_sem=rsem,
            device_id=dev, device_id_type=MESH,
        )

    pending = []

    def start(copy):
        copy.start()
        pending.append(copy)
        return copy

    def when(cond, fn):
        pl.when(cond)(fn)

    barrier = pltpu.get_barrier_semaphore()

    def greet(dev):
        pl.semaphore_signal(barrier, inc=1, device_id=dev, device_id_type=MESH)

    for d in range(1, 8):
        greet({"seq": mod8(z + d)})
        greet(device(*member(d)))
    others = []
    for e in range(1, 4):
        yh = yhi if e // 2 == 0 else 1 - yhi
        yl = ylo if e % 2 == 0 else 1 - ylo
        others.append({"dp": 2 * yh + c, "head": 2 * x + yl})
        greet(others[-1])
    when(moved, lambda: greet(partner))

    weights = [
        pltpu.make_async_copy(wqkv_hbm, wqkv, ins.at[0]),
        pltpu.make_async_copy(wout_hbm, wout, ins.at[1]),
    ]
    loads = [
        pltpu.make_async_copy(tok_hbm, tok_in, ins.at[2]),
        pltpu.make_async_copy(gout_hbm, gout_in, ins.at[3]),
        pltpu.make_async_copy(bins_hbm, bins_in, ins.at[4]),
        pltpu.make_async_copy(pat_hbm, pat_in, ins.at[5]),
    ]
    go = [
        remote(tok_in, tok, sws.at[0], swr.at[0], partner),
        remote(gout_in, gog.at[0], sws.at[1], swr.at[1], partner),
    ]
    share = [
        remote(bins_in, bins, sws.at[2], swr.at[2], sibling),
        remote(pat_in, patv, sws.at[5], swr.at[5], sibling),
    ]
    for copy in loads + weights:
        copy.start()
    stays = jnp.logical_not(moved)

    lane = lax.broadcasted_iota(jnp.int32, (BLK, 2 * HD), 1)
    low = lane < HD

    def swap(v):
        return pltpu.roll(v, HD, 1)

    for copy in weights:
        copy.wait()
    pair = pl.multiple_of((z // 2) * 384, 128)
    for q in range(4):
        rows = slice(128 * q, 128 * (q + 1))
        w0 = wqkv[rows, pl.ds(pair, 128)].astype(F32)
        w1 = wqkv[rows, pl.ds(pair + 128, 128)].astype(F32)
        w2 = wqkv[rows, pl.ds(pair + 256, 128)].astype(F32)
        s1 = swap(w1)
        wcat[rows, 0:128] = jnp.where(odd, w2, jnp.where(low, swap(w0), s1)).astype(BF16)
        wcat[rows, 128:256] = jnp.where(low, jnp.where(odd, s1, w0), 0.0).astype(BF16)
    wo_pair = wout[pl.ds(pl.multiple_of((z // 2) * 128, 128), 128), :]
    wo2[0:HD, :] = jnp.zeros((HD, D), BF16)
    wo2[HD:BLK, :] = jnp.where(odd, wo_pair[HD:BLK, :], wo_pair[0:HD, :])

    for copy in loads:
        copy.wait()

    def keep(dst, src):
        def fn():
            dst[...] = src[...]

        when(stays, fn)

    keep(tok, tok_in)
    keep(gog.at[0], gout_in)
    keep(bins, bins_in)
    keep(patv, pat_in)

    pl.semaphore_wait(barrier, 17 + jnp.where(moved, 1, 0))
    when(moved, lambda: go[0].start())
    when(moved, lambda: go[0].wait_recv())

    tokens = tok[...].astype(F32)
    spread = jnp.sqrt(jnp.mean(tokens * tokens, axis=-1, keepdims=True) + EPSILON)
    normed = tokens / spread
    normed_ref[...] = normed
    spread_ref[...] = spread
    hid[0] = normed.astype(BF16)

    rings = (hid, gog)
    table = {}

    def hop(k, way, t, part):
        if way == 0:
            src, dst = (0 if t == 1 else 2 * (t - 1)), (2 * t if t < 4 else 7)
        else:
            src, dst = (0 if t == 1 else 2 * (t - 1) - 1), 2 * t - 1
        rows = pl.ds(32 * part, 32)
        return remote(
            rings[k].at[src, rows], rings[k].at[dst, rows],
            zs.at[k, way, t, part], zr.at[k, way, t, part],
            {"seq": mod8(z + 1) if way == 0 else mod8(z - 1)},
        )

    orders = ((0, 1, 2, 3), (2, 3, 0, 1))

    def first_hop(k):
        for i in range(4):
            for way in (0, 1):
                part = orders[way][i]
                table[k, way, 1, part] = start(hop(k, way, 1, part))

    def next_hop(k, t, turns=(0, 1, 2, 3)):
        for i in turns:
            for way in (0, 1):
                part = orders[way][i]
                table[k, way, t, part].wait_recv()
                if t + 1 < 4 or i < 2:
                    table[k, way, t + 1, part] = start(hop(k, way, t + 1, part))

    def last_hop(k):
        for i in (0, 1):
            for way in (0, 1):
                table[k, way, 4, orders[way][i]].wait_recv()

    pools = (gkv, gqd)
    ring_x = {}
    x_right, x_left = lax.rem(x + 1, 4), lax.rem(x + 3, 4)
    x_far = lax.rem(x + 2, 4)

    def xcopy(k, b, kind, owner, dev):
        first, count = BATCHES[b]
        part = pools[k].at[owner, pl.ds(first, count)]
        ring_x[k, b, kind] = start(
            remote(part, part, xs.at[k, b, kind], xr.at[k, b, kind], dev)
        )

    def x_own(k, b):
        xcopy(k, b, 0, r, device(x_right, c))
        xcopy(k, b, 1, r, device(x_left, c))
        xcopy(k, b, 2, r, sibling)
        if b >= 2:
            xcopy(k, b, 5, r, device(x_far, c))

    def x_pass(k, b):
        ring_x[k, b, 0].wait_recv()
        if b == 0:
            xcopy(k, b, 5, 2 * x_left + c, device(x_right, c))
        xcopy(k, b, 3, 2 * x_left + c, sibling)
        ring_x[k, b, 1].wait_recv()
        if b == 1:
            xcopy(k, b, 5, 2 * x_right + c, device(x_left, c))
        xcopy(k, b, 4, 2 * x_right + c, sibling)

    def x_far_pass(k, b):
        ring_x[k, b, 5].wait_recv()
        xcopy(k, b, 6, 2 * x_far + c, sibling)

    def x_end(k):
        for b in range(5):
            for kind in (2, 3, 4, 6):
                ring_x[k, b, kind].wait_recv()

    def project(b):
        first, count = BATCHES[b]
        for p in range(first, first + count):
            t = dot_nn(hid[p], wcat[...]).astype(BF16)
            gkv[r, p] = t[:, 0:128]
            gqd[r, p] = t[:, 128:256]
        x_own(0, b)

    def project_grad(b):
        first, count = BATCHES[b]
        for p in range(first, first + count):
            u = dot_nt(gog[p], wo2[...])
            gqd[r, p] = jnp.where(low, gqd[r, p], u.astype(BF16))
        x_own(1, b)

    first_hop(0)
    when(moved, lambda: go[1].start())
    when(stays, lambda: [copy.start() for copy in share] and None)
    project(0)

    when(moved, lambda: [copy.wait_recv() for copy in share] and None)
    to_scalars = pltpu.make_async_copy(patv, pat, ins.at[8])
    to_scalars.start()
    for q in range(NB):
        binsf[q : q + 1, :] = bins[:, tile(q)].astype(F32)
    binst[...] = jnp.concatenate([binsf[...], jnp.zeros((BLK - NB, BLK), F32)], axis=0).T
    to_scalars.wait()

    next_hop(0, 1)
    project(1)
    next_hop(0, 2)
    project(2)
    x_pass(0, 0)
    next_hop(0, 3, (0, 1))
    when(moved, lambda: go[1].wait_recv())
    first_hop(1)
    next_hop(0, 3, (2, 3))
    project(3)
    x_pass(0, 1)
    x_far_pass(0, 0)
    last_hop(0)
    project(4)
    project_grad(0)
    next_hop(1, 1)
    project_grad(1)
    x_pass(0, 2)
    x_far_pass(0, 2)
    x_pass(0, 3)
    x_far_pass(0, 3)
    x_far_pass(0, 1)
    next_hop(1, 2, (0, 1))
    x_pass(0, 4)
    x_far_pass(0, 4)
    next_hop(1, 2, (2, 3))
    project_grad(2)
    x_pass(1, 0)
    x_end(0)

    bias2 = bias_ref[z] * LOG2E

    def distance(p):
        t = (p + 1) // 2
        return jnp.where(lax.rem(p, 2) == 1, t, 8 - t)

    def own_block(p):
        return 8 * mod8(z + distance(p)) + r

    far = (0, 1, 3, 5, 7, 6, 4, 2)

    def back(kind, src, dst, d):
        return remote(src, dst, ss.at[kind, d], rr.at[kind, d], {"seq": mod8(z + d)})

    def leave(kind, buf, dst, p):
        when(p > 0, lambda: back(kind, buf.at[p], dst.at[z], distance(p)).start())

    def left(kind, buf, dst):
        dst[z] = buf[0]
        copies = [back(kind, buf.at[far[d]], dst.at[z], d) for d in range(1, 8)]
        pending.extend(copies)
        return copies

    def used_block(row, n):
        other = lax.rem(row + pat[n, 0, 0], NB)
        return other, lax.rem(other, 8), place(mod8(other // 8 - z))

    def own_bins(row):
        return jnp.sum(jnp.where(lane == row, binst[...], 0.0), axis=1, keepdims=True)

    stcol[...] = jnp.zeros((BLK, BLK), F32)

    def forward_grads():
        for i in (0, 1):
            for way in (0, 1):
                part = orders[way][i]
                hop(1, way, 3, part).wait_recv()
                hop(1, way, 4, part).start()

    def forward_block(p, carry):
        when(p == 2, forward_grads)
        row = own_block(p)
        for n in range(NNZ):
            _, rn, pn = used_block(row, n)
            ycats[p, tile(n), :] = gkv[rn, pn]
        query = gqd[r, p]
        sd[0:BLK, :] = dot_nt(jnp.where(low, query, jnp.zeros_like(query)), ycats[p])
        bin_col = own_bins(row)
        top = None
        for n in range(NNZ):
            other, _, _ = used_block(row, n)
            bin_row = binsf[pl.ds(other, 1), :]
            v = sd[0:BLK, tile(n)] * c2 + jnp.where(bin_col == bin_row, bias2, 0.0)
            sd[0:BLK, tile(n)] = v
            top = v if top is None else jnp.maximum(top, v)
        m = jnp.max(top, axis=1, keepdims=True)
        total = jnp.zeros((BLK, BLK), F32)
        for n in range(NNZ):
            e = jnp.exp2(sd[0:BLK, tile(n)] - m)
            probs[p, :, tile(n)] = e
            pd[0:BLK, tile(n)] = e.astype(BF16)
            total = total + e
        total = jnp.sum(total, axis=1, keepdims=True)
        inv = 1.0 / total
        obuf[p] = (dot_nn(pd[0:BLK, :], ycats[p]) * inv).astype(BF16)
        invs[p] = inv
        stcol[...] = jnp.where(lane == 2 * p, m + jnp.log2(total), stcol[...])
        return carry

    lax.fori_loop(0, PER, forward_block, 0)
    for i in (0, 1):
        for way in (0, 1):
            part = orders[way][i]
            table[1, way, 4, part] = hop(1, way, 4, part)
            pending.append(table[1, way, 4, part])
            table[1, way, 3, orders[way][i + 2]].wait_recv()
    project_grad(3)

    last_hop(1)
    project_grad(4)

    for p in range(PER):
        both = gqd[r, p].astype(F32) * obuf[p].astype(F32)
        delta = jnp.sum(jnp.where(low, 0.0, both), axis=1, keepdims=True)
        deltas[p] = delta
        stcol[...] = jnp.where(lane == 2 * p + 1, delta, stcol[...])
    strow[...] = stcol[...].T
    mine = stg.at[pl.ds(pl.multiple_of(2 * PER * r, 16), 16)]
    stg[pl.ds(pl.multiple_of(2 * PER * r, 16), 16), :] = strow[0:16, :]

    def group(kind, d, src, dst):
        return start(remote(src, dst, ss.at[kind, d], rr.at[kind, d], device(*member(d))))

    c_st = [group(G_ST, d, mine, mine) for d in range(1, 8)]
    x_pass(1, 1)
    x_far_pass(1, 0)
    x_pass(1, 2)
    x_far_pass(1, 2)
    x_far_pass(1, 1)

    def query_block(p, carry):
        block = gqd[r, p]
        sd[0:BLK, :] = dot_nt(jnp.where(low, jnp.zeros_like(block), block), ycats[p])
        delta = deltas[p]
        for n in range(NNZ):
            pd[0:BLK, tile(n)] = (
                probs[p, :, tile(n)] * (sd[0:BLK, tile(n)] - delta)
            ).astype(BF16)
        grad = dot_nn(pd[0:BLK, :], ycats[p]) * (invs[p] * factor)
        both = jnp.where(low, grad, obuf[p].astype(F32))
        bqo[p] = both.astype(BF16)
        leave(Z_BQO, bqo, rqo, p)
        dtqo[:, pl.ds(pl.multiple_of(p * BLK, BLK), BLK)] = both.T.astype(BF16)
        return carry

    lax.fori_loop(0, PER, query_block, 0)

    c_bqo = left(Z_BQO, bqo, rqo)
    x_pass(1, 3)
    x_far_pass(1, 3)
    x_pass(1, 4)
    x_far_pass(1, 4)

    def stage1(k, part):
        wpart[k] = part
        for q in range(8):
            ars[k, q] = part[16 * q : 16 * (q + 1), :].astype(BF16)
        sent = []
        for d in range(1, 8):
            xx, cc = member(d)
            sent.append(group((G_S1A, G_S1B)[k], d, ars.at[k, 2 * xx + cc], arr.at[k, r]))
        return sent

    def stage2(k, copies):
        total = wpart[k, pl.ds(pl.multiple_of(16 * r, 16), 16), :]
        for d, copy in zip(range(1, 8), copies):
            copy.wait_recv()
            total = total + arr[k, giver(d)].astype(F32)
        dpx[k, seqno] = total.astype(BF16)
        slot = dpx.at[k, seqno]
        return [
            start(remote(slot, slot, ys.at[k, e], yr.at[k, e], others[e - 1]))
            for e in range(1, 4)
        ]

    mine_here = lax.rem(z, 2) == ylo

    def stage3(k, copies):
        for copy in copies:
            copy.wait_recv()
        total = dpx[k, 0].astype(F32)
        for q in range(1, 4):
            total = total + dpx[k, q].astype(F32)

        def spread_out():
            zbc[k, z // 2] = total.astype(BF16)

        slot = zbc.at[k, z // 2]
        kind = (Z_S3A, Z_S3B)[k]
        sent = [
            remote(slot, slot, ss.at[kind, d], rr.at[kind, d], {"seq": mod8(z + d)})
            for d in range(1, 8)
        ]
        when(mine_here, spread_out)
        when(mine_here, lambda: [copy.start() for copy in sent] and None)
        return sent

    def stage4(k, copies):
        for d, copy in zip(range(1, 8), copies):
            when(lax.rem(z + 8 - d, 2) == ylo, lambda: copy.wait_recv())
        fin[k, r] = zbc[k, x]
        sent = []
        for d in range(1, 8):
            xx, _ = member(d)
            sent.append(group((G_S4A, G_S4B)[k], d, zbc.at[k, xx], fin.at[k, r]))
        when(mine_here, lambda: [copy.wait_send() for copy in copies] and None)
        return sent

    hid_all = hid[...].reshape(PER * BLK, D)
    go_all = gog[...].reshape(PER * BLK, D)
    part0 = jnp.concatenate(
        [dot_nn(dtqo[0:HD, :], hid_all), dot_nn(dtqo[HD : 2 * HD, :], go_all)], axis=0
    )
    s1a = stage1(0, part0)
    for copy in c_st:
        copy.wait_recv()
    x_end(1)

    def key_block(p, carry):
        row = own_block(p)
        for n in range(NNZ):
            _, rn, pn = used_block(row, n)
            ycat[tile(n), :] = gqd[rn, pn]
        block = gkv[r, p]
        zero = jnp.zeros_like(block)
        a2[0:BLK, :] = jnp.where(low, block, zero)
        a2[BLK : 2 * BLK, :] = jnp.where(low, zero, block)
        sd[...] = dot_nt(a2[...], ycat[...])
        bin_col = own_bins(row)
        for n in range(NNZ):
            other, rn, pn = used_block(row, n)
            bin_row = binsf[pl.ds(other, 1), :]
            log_row = stg[pl.ds(16 * rn + 2 * pn, 1), :]
            delta_row = stg[pl.ds(16 * rn + 2 * pn + 1, 1), :]
            v = sd[0:BLK, tile(n)] * c2 + jnp.where(bin_col == bin_row, bias2, 0.0)
            e = jnp.exp2(v - log_row)
            pd[0:BLK, tile(n)] = e.astype(BF16)
            pd[BLK : 2 * BLK, tile(n)] = (e * (sd[BLK : 2 * BLK, tile(n)] - delta_row)).astype(BF16)
        g = dot_nn(pd[...], ycat[...])
        both = jnp.where(low, g[BLK : 2 * BLK] * factor, g[0:BLK])
        bkv[p] = both.astype(BF16)
        leave(Z_BKV, bkv, rkv, p)
        dtkv[:, pl.ds(pl.multiple_of(p * BLK, BLK), BLK)] = both.T.astype(BF16)
        return carry

    lax.fori_loop(0, PER, key_block, 0)

    c_bkv = left(Z_BKV, bkv, rkv)
    s1b = stage1(1, dot_nn(dtkv[...], hid[...].reshape(PER * BLK, D)))
    s2a = stage2(0, s1a)

    def deliver(src, dst, k):
        there = remote(src, dst, sws.at[3 + k], swr.at[3 + k], partner)
        keep(dst, src)
        when(moved, lambda: there.start())
        return there

    for copy in c_bqo:
        copy.wait_recv()
    for g in range(HEADS // 2):
        even, uneven = rqo[2 * g].astype(F32), rqo[2 * g + 1].astype(F32)
        att[:, tile(g)] = jnp.where(low, swap(even), uneven).astype(BF16)
    res[...] = dot_nn(att[...], wout[...]).astype(BF16)
    d_out = deliver(res, out_ref, 0)
    s2b = stage2(1, s1b)
    s3a = stage3(0, s2a)
    s3b = stage3(1, s2b)
    s4a = stage4(0, s3a)

    for copy in c_bkv:
        copy.wait_recv()
    for g in range(HEADS // 2):
        qo_even, qo_odd = rqo[2 * g].astype(F32), rqo[2 * g + 1].astype(F32)
        kv_even = swap(rkv[2 * g].astype(F32))
        gp[:, tile(3 * g)] = jnp.where(low, qo_even, kv_even).astype(BF16)
        gp[:, tile(3 * g + 1)] = jnp.where(low, kv_even, swap(qo_odd)).astype(BF16)
        gp[:, tile(3 * g + 2)] = rkv[2 * g + 1]
    grad_hidden = dot_nt(gp[...], wqkv[...])
    normed = normed_ref[...]
    inner = jnp.mean(grad_hidden * normed, axis=-1, keepdims=True)
    gres[...] = ((grad_hidden - normed * inner) / spread_ref[...]).astype(BF16)
    d_gtok = deliver(gres, gtok_ref, 1)
    s4b = stage4(1, s3b)

    for copy in s4a + s4b:
        copy.wait_recv()
    for copy in pending:
        copy.wait_send()
    when(moved, lambda: [copy.wait_send() for copy in go] and None)
    when(stays, lambda: [copy.wait_send() for copy in share] and None)
    for there in (d_out, d_gtok):
        when(moved, lambda: there.wait())


def finish(out_in, gtok_in, fin_ref, out_ref, gtok_ref, gqkv_ref, gwo_ref):
    out_ref[...] = out_in[...]
    gtok_ref[...] = gtok_in[...]
    first = fin_ref[0].reshape(BLK, D).astype(F32)
    second = fin_ref[1].reshape(BLK, D).astype(F32)
    gwo_ref[...] = first[HD : 2 * HD, :]
    gqkv_ref[0:HD, :] = first[0:HD, :]
    gqkv_ref[HD : 3 * HD, :] = second


def body(tokens, bin_ids, pattern, w_qkv, w_out, head_bias, grad_output):
    vmem = pl.BlockSpec(memory_space=pltpu.VMEM)
    smem = pl.BlockSpec(memory_space=pltpu.SMEM)
    hbm = pl.BlockSpec(memory_space=pltpu.HBM)
    dma = pltpu.SemaphoreType.DMA
    half = functools.partial(pltpu.VMEM, dtype=BF16)
    full = functools.partial(pltpu.VMEM, dtype=F32)
    scratch = [
        half((8, 8, BLK, 128)),
        half((8, 8, BLK, 128)),
        half((8, BLK, D)),
        half((8, BLK, D)),
        half((BLK, D)),
        half((BLK, D)),
        half((BLK, D)),
        pltpu.VMEM((1, NB * BLK), jnp.int32),
        pltpu.VMEM((NNZ, 1, NB), jnp.int32),
        half((D, 3 * D)),
        half((D, D)),
        pltpu.VMEM((1, NB * BLK), jnp.int32),
        pltpu.VMEM((NNZ, 1, NB), jnp.int32),
        pltpu.SMEM((NNZ, 1, NB), jnp.int32),
        half((D, 256)),
        half((BLK, D)),
        full((BLK, D)),
        full((BLK, 1)),
        half((PER, CAT, 128)),
        half((CAT, 128)),
        full((PER, BLK, CAT)),
        full((2 * BLK, CAT)),
        half((2 * BLK, CAT)),
        half((2 * BLK, 128)),
        full((BLK, BLK)),
        full((BLK, BLK)),
        full((2 * NB, BLK)),
        full((PER, BLK, 1)),
        full((PER, BLK, 1)),
        full((NB, BLK)),
        full((BLK, BLK)),
        half((8, BLK, 128)),
        half((8, BLK, 128)),
        half((8, BLK, 128)),
        half((8, BLK, 128)),
        half((8, BLK, 128)),
        half((BLK, PER * BLK)),
        half((BLK, PER * BLK)),
        full((2, BLK, D)),
        half((2, 8, 16, D)),
        half((2, 8, 16, D)),
        half((2, 4, 16, D)),
        half((2, 4, 16, D)),
        half((BLK, D)),
        half((BLK, 3 * D)),
        half((BLK, D)),
        half((BLK, D)),
        dma((9, 8)),
        dma((9, 8)),
        dma((2, 4)),
        dma((2, 4)),
        dma((2, 2, 5, 4)),
        dma((2, 2, 5, 4)),
        dma((2, 5, 7)),
        dma((2, 5, 7)),
        dma((9,)),
        dma((6,)),
        dma((6,)),
    ]
    shapes = (
        jax.ShapeDtypeStruct((BLK, D), BF16),
        jax.ShapeDtypeStruct((BLK, D), BF16),
    )
    parts = pl.pallas_call(
        kernel,
        out_shape=shapes + (jax.ShapeDtypeStruct((2, 8, 16, D), BF16),),
        in_specs=[smem, hbm, hbm, hbm, hbm, hbm, hbm],
        out_specs=(vmem, vmem, vmem),
        scratch_shapes=scratch,
        compiler_params=pltpu.CompilerParams(
            collective_id=0, has_side_effects=True, vmem_limit_bytes=62 * 1024 * 1024
        ),
        name="layer",
    )(head_bias, tokens[0], grad_output[0], w_qkv, w_out, bin_ids, pattern.transpose(2, 0, 1))
    result, grad_input, own_qkv, own_out = pl.pallas_call(
        finish,
        out_shape=shapes
        + (
            jax.ShapeDtypeStruct((3 * HD, D), F32),
            jax.ShapeDtypeStruct((HD, D), F32),
        ),
        in_specs=[vmem, vmem, vmem],
        out_specs=(vmem, vmem, vmem, vmem),
        name="finish",
    )(*parts)
    return (result[None], grad_input[None], own_qkv.T, own_out)


def solution(mesh):
    return jax.shard_map(
        body,
        mesh=mesh,
        in_specs=(
            P("dp", ("seq", "head"), None),
            P("dp", None),
            P("dp", None, None),
            P(),
            P(),
            P(),
            P("dp", ("seq", "head"), None),
        ),
        out_specs=(
            P("dp", ("seq", "head"), None),
            P("dp", ("seq", "head"), None),
            P(None, "head"),
            P("head", None),
        ),
        check_vma=False,
    )
```

```python
import functools
import math

import jax
import jax.numpy as jnp
from jax import lax
from jax.experimental import pallas as pl
from jax.experimental.pallas import tpu as pltpu
from jax.sharding import PartitionSpec as P

D = 512
HEADS = 8
HD = 64
BLK = 128
NNZ = 9
PER = 8
NB = 64
EPSILON = 1e-05
LOG2E = math.log2(math.e)
MESH = pl.DeviceIdType.MESH
F32 = jnp.float32
BF16 = jnp.bfloat16
CAT = NNZ * BLK

BATCHES = ((0, 1), (1, 2), (3, 2), (5, 2), (7, 1))

(
    Z_BQO, Z_BKV, Z_S3A, Z_S3B, G_ST, G_S1A, G_S1B, G_S4A, G_S4B,
) = range(9)


def dot_nn(a, b):
    return lax.dot_general(a, b, (((1,), (0,)), ((), ())), preferred_element_type=F32)


def dot_nt(a, b):
    return lax.dot_general(a, b, (((1,), (1,)), ((), ())), preferred_element_type=F32)


def place(rel):
    return jnp.where(rel == 0, 0, jnp.where(rel <= 4, 2 * rel - 1, 16 - 2 * rel))


def tile(n):
    return slice(n * BLK, (n + 1) * BLK)


def kernel(
    bias_ref, tok_hbm, gout_hbm, wqkv_hbm, wout_hbm, bins_hbm, pat_hbm,
    out_ref, gtok_ref, fin,
    gkv, gqd, hid, gog, tok, tok_in, gout_in, bins_in, pat_in, wqkv, wout, bins, patv, pat, wcat, wo2, normed_ref, spread_ref,
    ycats, ycat, probs, sd, pd, a2, stcol, strow, stg, deltas, invs, binsf, binst,
    obuf, bqo, bkv, rqo, rkv, dtqo, dtkv,
    wpart, ars, arr, dpx, zbc, att, gp, res, gres,
    ss, rr, ys, yr, zs, zr, xs, xr, ins, sws, swr,
):
    dp = lax.axis_index("dp")
    z = lax.axis_index("seq")
    head = lax.axis_index("head")
    yhi, c = dp // 2, lax.rem(dp, 2)
    x, ylo = head // 2, lax.rem(head, 2)
    r = 2 * x + c
    seqno = 2 * yhi + ylo
    moved = c != ylo
    odd = lax.rem(z, 2) == 1
    factor = 1.0 / math.sqrt(HD)
    c2 = factor * LOG2E

    def mod8(v):
        return lax.rem(v + 16, 8)

    def device(xx, cc):
        return {"dp": 2 * yhi + cc, "head": 2 * xx + ylo}

    partner = {"dp": 2 * yhi + ylo, "head": 2 * x + c}
    sibling = {"dp": 2 * yhi + (1 - c)}

    def member(d):
        dx, dc = d // 2, d % 2
        xx = lax.rem(x + dx, 4)
        cc = c if dc == 0 else 1 - c
        return xx, cc

    def giver(d):
        dx, dc = d // 2, d % 2
        xx = lax.rem(x + 4 - dx, 4)
        cc = c if dc == 0 else 1 - c
        return 2 * xx + cc

    def remote(src, dst, ssem, rsem, dev):
        return pltpu.make_async_remote_copy(
            src_ref=src, dst_ref=dst, send_sem=ssem, recv_sem=rsem,
            device_id=dev, device_id_type=MESH,
        )

    pending = []

    def start(copy):
        copy.start()
        pending.append(copy)
        return copy

    def when(cond, fn):
        pl.when(cond)(fn)

    barrier = pltpu.get_barrier_semaphore()

    def greet(dev):
        pl.semaphore_signal(barrier, inc=1, device_id=dev, device_id_type=MESH)

    for d in range(1, 8):
        greet({"seq": mod8(z + d)})
        greet(device(*member(d)))
    others = []
    for e in range(1, 4):
        yh = yhi if e // 2 == 0 else 1 - yhi
        yl = ylo if e % 2 == 0 else 1 - ylo
        others.append({"dp": 2 * yh + c, "head": 2 * x + yl})
        greet(others[-1])
    when(moved, lambda: greet(partner))

    weights = [
        pltpu.make_async_copy(wqkv_hbm, wqkv, ins.at[0]),
        pltpu.make_async_copy(wout_hbm, wout, ins.at[1]),
    ]
    loads = [
        pltpu.make_async_copy(tok_hbm, tok_in, ins.at[2]),
        pltpu.make_async_copy(gout_hbm, gout_in, ins.at[3]),
        pltpu.make_async_copy(bins_hbm, bins_in, ins.at[4]),
        pltpu.make_async_copy(pat_hbm, pat_in, ins.at[5]),
    ]
    go = [
        remote(tok_in, tok, sws.at[0], swr.at[0], partner),
        remote(gout_in, gog.at[0], sws.at[1], swr.at[1], partner),
    ]
    share = [
        remote(bins_in, bins, sws.at[2], swr.at[2], sibling),
        remote(pat_in, patv, sws.at[5], swr.at[5], sibling),
    ]
    for copy in loads + weights:
        copy.start()
    stays = jnp.logical_not(moved)

    lane = lax.broadcasted_iota(jnp.int32, (BLK, 2 * HD), 1)
    low = lane < HD

    def swap(v):
        return pltpu.roll(v, HD, 1)

    for copy in weights:
        copy.wait()
    pair = pl.multiple_of((z // 2) * 384, 128)
    for q in range(4):
        rows = slice(128 * q, 128 * (q + 1))
        w0 = wqkv[rows, pl.ds(pair, 128)].astype(F32)
        w1 = wqkv[rows, pl.ds(pair + 128, 128)].astype(F32)
        w2 = wqkv[rows, pl.ds(pair + 256, 128)].astype(F32)
        s1 = swap(w1)
        wcat[rows, 0:128] = jnp.where(odd, w2, jnp.where(low, swap(w0), s1)).astype(BF16)
        wcat[rows, 128:256] = jnp.where(low, jnp.where(odd, s1, w0), 0.0).astype(BF16)
    wo_pair = wout[pl.ds(pl.multiple_of((z // 2) * 128, 128), 128), :]
    wo2[0:HD, :] = jnp.zeros((HD, D), BF16)
    wo2[HD:BLK, :] = jnp.where(odd, wo_pair[HD:BLK, :], wo_pair[0:HD, :])

    for copy in loads:
        copy.wait()

    def keep(dst, src):
        def fn():
            dst[...] = src[...]

        when(stays, fn)

    keep(tok, tok_in)
    keep(gog.at[0], gout_in)
    keep(bins, bins_in)
    keep(patv, pat_in)

    pl.semaphore_wait(barrier, 17 + jnp.where(moved, 1, 0))
    when(moved, lambda: go[0].start())
    when(moved, lambda: go[0].wait_send())
    when(moved, lambda: go[1].start())
    when(moved, lambda: go[0].wait_recv())

    tokens = tok[...].astype(F32)
    spread = jnp.sqrt(jnp.mean(tokens * tokens, axis=-1, keepdims=True) + EPSILON)
    normed = tokens / spread
    normed_ref[...] = normed
    spread_ref[...] = spread
    hid[0] = normed.astype(BF16)

    rings = (hid, gog)
    table = {}

    def hop(k, way, t, part):
        if way == 0:
            src, dst = (0 if t == 1 else 2 * (t - 1)), (2 * t if t < 4 else 7)
        else:
            src, dst = (0 if t == 1 else 2 * (t - 1) - 1), 2 * t - 1
        rows = pl.ds(64 * part, 64)
        return remote(
            rings[k].at[src, rows], rings[k].at[dst, rows],
            zs.at[k, way, t, part], zr.at[k, way, t, part],
            {"seq": mod8(z + 1) if way == 0 else mod8(z - 1)},
        )

    def first_hop(k):
        for part in (0, 1):
            for way in (0, 1):
                table[k, way, 1, part] = start(hop(k, way, 1, part))

    def next_hop(k, t):
        for part in (0, 1):
            for way in (0, 1):
                table[k, way, t, part].wait_recv()
                if t + 1 < 4 or part == way:
                    table[k, way, t + 1, part] = start(hop(k, way, t + 1, part))

    def last_hop(k):
        for way in (0, 1):
            table[k, way, 4, way].wait_recv()

    pools = (gkv, gqd)
    ring_x = {}
    x_right, x_left = lax.rem(x + 1, 4), lax.rem(x + 3, 4)
    x_far = lax.rem(x + 2, 4)

    def xcopy(k, b, kind, owner, dev):
        first, count = BATCHES[b]
        part = pools[k].at[owner, pl.ds(first, count)]
        ring_x[k, b, kind] = start(
            remote(part, part, xs.at[k, b, kind], xr.at[k, b, kind], dev)
        )

    def x_own(k, b):
        xcopy(k, b, 0, r, device(x_right, c))
        xcopy(k, b, 1, r, device(x_left, c))
        xcopy(k, b, 2, r, sibling)
        if b >= 2:
            xcopy(k, b, 5, r, device(x_far, c))

    def x_pass(k, b):
        ring_x[k, b, 0].wait_recv()
        if b == 0:
            xcopy(k, b, 5, 2 * x_left + c, device(x_right, c))
        xcopy(k, b, 3, 2 * x_left + c, sibling)
        ring_x[k, b, 1].wait_recv()
        if b == 1:
            xcopy(k, b, 5, 2 * x_right + c, device(x_left, c))
        xcopy(k, b, 4, 2 * x_right + c, sibling)

    def x_far_pass(k, b):
        ring_x[k, b, 5].wait_recv()
        xcopy(k, b, 6, 2 * x_far + c, sibling)

    def x_end(k):
        for b in range(5):
            for kind in (2, 3, 4, 6):
                ring_x[k, b, kind].wait_recv()

    def project(b):
        first, count = BATCHES[b]
        for p in range(first, first + count):
            t = dot_nn(hid[p], wcat[...]).astype(BF16)
            gkv[r, p] = t[:, 0:128]
            gqd[r, p] = t[:, 128:256]
        x_own(0, b)

    def project_grad(b):
        first, count = BATCHES[b]
        for p in range(first, first + count):
            u = dot_nt(gog[p], wo2[...])
            gqd[r, p] = jnp.where(low, gqd[r, p], u.astype(BF16))
        x_own(1, b)

    first_hop(0)
    when(stays, lambda: [copy.start() for copy in share] and None)
    project(0)
    when(moved, lambda: go[1].wait_recv())
    first_hop(1)
    project_grad(0)

    when(moved, lambda: [copy.wait_recv() for copy in share] and None)
    to_scalars = pltpu.make_async_copy(patv, pat, ins.at[8])
    to_scalars.start()
    for q in range(NB):
        binsf[q : q + 1, :] = bins[:, tile(q)].astype(F32)
    binst[...] = jnp.concatenate([binsf[...], jnp.zeros((BLK - NB, BLK), F32)], axis=0).T
    to_scalars.wait()

    next_hop(0, 1)
    project(1)
    x_pass(0, 0)
    next_hop(1, 1)
    project_grad(1)
    x_far_pass(0, 0)
    next_hop(0, 2)
    project(2)
    x_pass(0, 1)
    x_pass(1, 0)
    next_hop(1, 2)
    project_grad(2)
    x_far_pass(0, 1)
    x_pass(1, 1)
    x_far_pass(1, 0)
    next_hop(0, 3)
    project(3)
    x_pass(0, 2)
    x_far_pass(0, 2)
    x_far_pass(1, 1)
    next_hop(1, 3)
    project_grad(3)
    last_hop(0)
    project(4)
    x_pass(1, 2)
    x_far_pass(1, 2)
    x_pass(0, 3)
    x_far_pass(0, 3)
    last_hop(1)
    project_grad(4)
    x_pass(0, 4)
    x_far_pass(0, 4)
    x_pass(1, 3)
    x_far_pass(1, 3)
    x_end(0)

    bias2 = bias_ref[z] * LOG2E

    def distance(p):
        t = (p + 1) // 2
        return jnp.where(lax.rem(p, 2) == 1, t, 8 - t)

    def own_block(p):
        return 8 * mod8(z + distance(p)) + r

    far = (0, 1, 3, 5, 7, 6, 4, 2)

    def back(kind, src, dst, d):
        return remote(src, dst, ss.at[kind, d], rr.at[kind, d], {"seq": mod8(z + d)})

    def leave(kind, buf, dst, p):
        when(p > 0, lambda: back(kind, buf.at[p], dst.at[z], distance(p)).start())

    def left(kind, buf, dst):
        dst[z] = buf[0]
        copies = [back(kind, buf.at[far[d]], dst.at[z], d) for d in range(1, 8)]
        pending.extend(copies)
        return copies

    def used_block(row, n):
        other = lax.rem(row + pat[n, 0, 0], NB)
        return other, lax.rem(other, 8), place(mod8(other // 8 - z))

    def own_bins(row):
        return jnp.sum(jnp.where(lane == row, binst[...], 0.0), axis=1, keepdims=True)

    stcol[...] = jnp.zeros((BLK, BLK), F32)

    def forward_block(p, carry):
        row = own_block(p)
        for n in range(NNZ):
            _, rn, pn = used_block(row, n)
            ycats[p, tile(n), :] = gkv[rn, pn]
        query = gqd[r, p]
        sd[0:BLK, :] = dot_nt(jnp.where(low, query, jnp.zeros_like(query)), ycats[p])
        bin_col = own_bins(row)
        top = None
        for n in range(NNZ):
            other, _, _ = used_block(row, n)
            bin_row = binsf[pl.ds(other, 1), :]
            v = sd[0:BLK, tile(n)] * c2 + jnp.where(bin_col == bin_row, bias2, 0.0)
            sd[0:BLK, tile(n)] = v
            top = v if top is None else jnp.maximum(top, v)
        m = jnp.max(top, axis=1, keepdims=True)
        total = jnp.zeros((BLK, BLK), F32)
        for n in range(NNZ):
            e = jnp.exp2(sd[0:BLK, tile(n)] - m)
            probs[p, :, tile(n)] = e
            pd[0:BLK, tile(n)] = e.astype(BF16)
            total = total + e
        total = jnp.sum(total, axis=1, keepdims=True)
        inv = 1.0 / total
        obuf[p] = (dot_nn(pd[0:BLK, :], ycats[p]) * inv).astype(BF16)
        invs[p] = inv
        stcol[...] = jnp.where(lane == 2 * p, m + jnp.log2(total), stcol[...])
        return carry

    lax.fori_loop(0, PER, forward_block, 0)
    x_pass(1, 4)
    x_far_pass(1, 4)

    for p in range(PER):
        both = gqd[r, p].astype(F32) * obuf[p].astype(F32)
        delta = jnp.sum(jnp.where(low, 0.0, both), axis=1, keepdims=True)
        deltas[p] = delta
        stcol[...] = jnp.where(lane == 2 * p + 1, delta, stcol[...])
    strow[...] = stcol[...].T
    mine = stg.at[pl.ds(pl.multiple_of(2 * PER * r, 16), 16)]
    stg[pl.ds(pl.multiple_of(2 * PER * r, 16), 16), :] = strow[0:16, :]

    def group(kind, d, src, dst):
        return start(remote(src, dst, ss.at[kind, d], rr.at[kind, d], device(*member(d))))

    c_st = [group(G_ST, d, mine, mine) for d in range(1, 8)]

    def query_block(p, carry):
        block = gqd[r, p]
        sd[0:BLK, :] = dot_nt(jnp.where(low, jnp.zeros_like(block), block), ycats[p])
        delta = deltas[p]
        for n in range(NNZ):
            pd[0:BLK, tile(n)] = (
                probs[p, :, tile(n)] * (sd[0:BLK, tile(n)] - delta)
            ).astype(BF16)
        grad = dot_nn(pd[0:BLK, :], ycats[p]) * (invs[p] * factor)
        both = jnp.where(low, grad, obuf[p].astype(F32))
        bqo[p] = both.astype(BF16)
        leave(Z_BQO, bqo, rqo, p)
        dtqo[:, pl.ds(pl.multiple_of(p * BLK, BLK), BLK)] = both.T.astype(BF16)
        return carry

    lax.fori_loop(0, PER, query_block, 0)

    c_bqo = left(Z_BQO, bqo, rqo)

    def stage1(k, part):
        wpart[k] = part
        for q in range(8):
            ars[k, q] = part[16 * q : 16 * (q + 1), :].astype(BF16)
        sent = []
        for d in range(1, 8):
            xx, cc = member(d)
            sent.append(group((G_S1A, G_S1B)[k], d, ars.at[k, 2 * xx + cc], arr.at[k, r]))
        return sent

    def stage2(k, copies):
        total = wpart[k, pl.ds(pl.multiple_of(16 * r, 16), 16), :]
        for d, copy in zip(range(1, 8), copies):
            copy.wait_recv()
            total = total + arr[k, giver(d)].astype(F32)
        dpx[k, seqno] = total.astype(BF16)
        slot = dpx.at[k, seqno]
        return [
            start(remote(slot, slot, ys.at[k, e], yr.at[k, e], others[e - 1]))
            for e in range(1, 4)
        ]

    mine_here = lax.rem(z, 2) == ylo

    def stage3(k, copies):
        for copy in copies:
            copy.wait_recv()
        total = dpx[k, 0].astype(F32)
        for q in range(1, 4):
            total = total + dpx[k, q].astype(F32)

        def spread_out():
            zbc[k, z // 2] = total.astype(BF16)

        slot = zbc.at[k, z // 2]
        kind = (Z_S3A, Z_S3B)[k]
        sent = [
            remote(slot, slot, ss.at[kind, d], rr.at[kind, d], {"seq": mod8(z + d)})
            for d in range(1, 8)
        ]
        when(mine_here, spread_out)
        when(mine_here, lambda: [copy.start() for copy in sent] and None)
        return sent

    def stage4(k, copies):
        for d, copy in zip(range(1, 8), copies):
            when(lax.rem(z + 8 - d, 2) == ylo, lambda: copy.wait_recv())
        fin[k, r] = zbc[k, x]
        sent = []
        for d in range(1, 8):
            xx, _ = member(d)
            sent.append(group((G_S4A, G_S4B)[k], d, zbc.at[k, xx], fin.at[k, r]))
        when(mine_here, lambda: [copy.wait_send() for copy in copies] and None)
        return sent

    hid_all = hid[...].reshape(PER * BLK, D)
    go_all = gog[...].reshape(PER * BLK, D)
    part0 = jnp.concatenate(
        [dot_nn(dtqo[0:HD, :], hid_all), dot_nn(dtqo[HD : 2 * HD, :], go_all)], axis=0
    )
    s1a = stage1(0, part0)
    for copy in c_st:
        copy.wait_recv()
    x_end(1)

    def key_block(p, carry):
        row = own_block(p)
        for n in range(NNZ):
            _, rn, pn = used_block(row, n)
            ycat[tile(n), :] = gqd[rn, pn]
        block = gkv[r, p]
        zero = jnp.zeros_like(block)
        a2[0:BLK, :] = jnp.where(low, block, zero)
        a2[BLK : 2 * BLK, :] = jnp.where(low, zero, block)
        sd[...] = dot_nt(a2[...], ycat[...])
        bin_col = own_bins(row)
        for n in range(NNZ):
            other, rn, pn = used_block(row, n)
            bin_row = binsf[pl.ds(other, 1), :]
            log_row = stg[pl.ds(16 * rn + 2 * pn, 1), :]
            delta_row = stg[pl.ds(16 * rn + 2 * pn + 1, 1), :]
            v = sd[0:BLK, tile(n)] * c2 + jnp.where(bin_col == bin_row, bias2, 0.0)
            e = jnp.exp2(v - log_row)
            pd[0:BLK, tile(n)] = e.astype(BF16)
            pd[BLK : 2 * BLK, tile(n)] = (e * (sd[BLK : 2 * BLK, tile(n)] - delta_row)).astype(BF16)
        g = dot_nn(pd[...], ycat[...])
        both = jnp.where(low, g[BLK : 2 * BLK] * factor, g[0:BLK])
        bkv[p] = both.astype(BF16)
        leave(Z_BKV, bkv, rkv, p)
        dtkv[:, pl.ds(pl.multiple_of(p * BLK, BLK), BLK)] = both.T.astype(BF16)
        return carry

    lax.fori_loop(0, PER, key_block, 0)

    c_bkv = left(Z_BKV, bkv, rkv)
    s1b = stage1(1, dot_nn(dtkv[...], hid[...].reshape(PER * BLK, D)))
    s2a = stage2(0, s1a)

    def deliver(src, dst, k):
        there = remote(src, dst, sws.at[3 + k], swr.at[3 + k], partner)
        keep(dst, src)
        when(moved, lambda: there.start())
        return there

    for copy in c_bqo:
        copy.wait_recv()
    for g in range(HEADS // 2):
        even, uneven = rqo[2 * g].astype(F32), rqo[2 * g + 1].astype(F32)
        att[:, tile(g)] = jnp.where(low, swap(even), uneven).astype(BF16)
    res[...] = dot_nn(att[...], wout[...]).astype(BF16)
    d_out = deliver(res, out_ref, 0)
    s2b = stage2(1, s1b)
    s3a = stage3(0, s2a)
    s3b = stage3(1, s2b)
    s4a = stage4(0, s3a)

    for copy in c_bkv:
        copy.wait_recv()
    for g in range(HEADS // 2):
        qo_even, qo_odd = rqo[2 * g].astype(F32), rqo[2 * g + 1].astype(F32)
        kv_even = swap(rkv[2 * g].astype(F32))
        gp[:, tile(3 * g)] = jnp.where(low, qo_even, kv_even).astype(BF16)
        gp[:, tile(3 * g + 1)] = jnp.where(low, kv_even, swap(qo_odd)).astype(BF16)
        gp[:, tile(3 * g + 2)] = rkv[2 * g + 1]
    grad_hidden = dot_nt(gp[...], wqkv[...])
    normed = normed_ref[...]
    inner = jnp.mean(grad_hidden * normed, axis=-1, keepdims=True)
    gres[...] = ((grad_hidden - normed * inner) / spread_ref[...]).astype(BF16)
    d_gtok = deliver(gres, gtok_ref, 1)
    s4b = stage4(1, s3b)

    for copy in s4a + s4b:
        copy.wait_recv()
    for copy in pending:
        copy.wait_send()
    when(moved, lambda: go[1].wait_send())
    when(stays, lambda: [copy.wait_send() for copy in share] and None)
    for there in (d_out, d_gtok):
        when(moved, lambda: there.wait())


def finish(out_in, gtok_in, fin_ref, out_ref, gtok_ref, gqkv_ref, gwo_ref):
    out_ref[...] = out_in[...]
    gtok_ref[...] = gtok_in[...]
    first = fin_ref[0].reshape(BLK, D).astype(F32)
    second = fin_ref[1].reshape(BLK, D).astype(F32)
    gwo_ref[...] = first[HD : 2 * HD, :]
    gqkv_ref[0:HD, :] = first[0:HD, :]
    gqkv_ref[HD : 3 * HD, :] = second


def body(tokens, bin_ids, pattern, w_qkv, w_out, head_bias, grad_output):
    vmem = pl.BlockSpec(memory_space=pltpu.VMEM)
    smem = pl.BlockSpec(memory_space=pltpu.SMEM)
    hbm = pl.BlockSpec(memory_space=pltpu.HBM)
    dma = pltpu.SemaphoreType.DMA
    half = functools.partial(pltpu.VMEM, dtype=BF16)
    full = functools.partial(pltpu.VMEM, dtype=F32)
    scratch = [
        half((8, 8, BLK, 128)),
        half((8, 8, BLK, 128)),
        half((8, BLK, D)),
        half((8, BLK, D)),
        half((BLK, D)),
        half((BLK, D)),
        half((BLK, D)),
        pltpu.VMEM((1, NB * BLK), jnp.int32),
        pltpu.VMEM((NNZ, 1, NB), jnp.int32),
        half((D, 3 * D)),
        half((D, D)),
        pltpu.VMEM((1, NB * BLK), jnp.int32),
        pltpu.VMEM((NNZ, 1, NB), jnp.int32),
        pltpu.SMEM((NNZ, 1, NB), jnp.int32),
        half((D, 256)),
        half((BLK, D)),
        full((BLK, D)),
        full((BLK, 1)),
        half((PER, CAT, 128)),
        half((CAT, 128)),
        full((PER, BLK, CAT)),
        full((2 * BLK, CAT)),
        half((2 * BLK, CAT)),
        half((2 * BLK, 128)),
        full((BLK, BLK)),
        full((BLK, BLK)),
        full((2 * NB, BLK)),
        full((PER, BLK, 1)),
        full((PER, BLK, 1)),
        full((NB, BLK)),
        full((BLK, BLK)),
        half((8, BLK, 128)),
        half((8, BLK, 128)),
        half((8, BLK, 128)),
        half((8, BLK, 128)),
        half((8, BLK, 128)),
        half((BLK, PER * BLK)),
        half((BLK, PER * BLK)),
        full((2, BLK, D)),
        half((2, 8, 16, D)),
        half((2, 8, 16, D)),
        half((2, 4, 16, D)),
        half((2, 4, 16, D)),
        half((BLK, D)),
        half((BLK, 3 * D)),
        half((BLK, D)),
        half((BLK, D)),
        dma((9, 8)),
        dma((9, 8)),
        dma((2, 4)),
        dma((2, 4)),
        dma((2, 2, 5, 2)),
        dma((2, 2, 5, 2)),
        dma((2, 5, 7)),
        dma((2, 5, 7)),
        dma((9,)),
        dma((6,)),
        dma((6,)),
    ]
    shapes = (
        jax.ShapeDtypeStruct((BLK, D), BF16),
        jax.ShapeDtypeStruct((BLK, D), BF16),
    )
    parts = pl.pallas_call(
        kernel,
        out_shape=shapes + (jax.ShapeDtypeStruct((2, 8, 16, D), BF16),),
        in_specs=[smem, hbm, hbm, hbm, hbm, hbm, hbm],
        out_specs=(vmem, vmem, vmem),
        scratch_shapes=scratch,
        compiler_params=pltpu.CompilerParams(
            collective_id=0, has_side_effects=True, vmem_limit_bytes=62 * 1024 * 1024
        ),
        name="layer",
    )(head_bias, tokens[0], grad_output[0], w_qkv, w_out, bin_ids, pattern.transpose(2, 0, 1))
    result, grad_input, own_qkv, own_out = pl.pallas_call(
        finish,
        out_shape=shapes
        + (
            jax.ShapeDtypeStruct((3 * HD, D), F32),
            jax.ShapeDtypeStruct((HD, D), F32),
        ),
        in_specs=[vmem, vmem, vmem],
        out_specs=(vmem, vmem, vmem, vmem),
        name="finish",
    )(*parts)
    return (result[None], grad_input[None], own_qkv.T, own_out)


def solution(mesh):
    return jax.shard_map(
        body,
        mesh=mesh,
        in_specs=(
            P("dp", ("seq", "head"), None),
            P("dp", None),
            P("dp", None, None),
            P(),
            P(),
            P(),
            P("dp", ("seq", "head"), None),
        ),
        out_specs=(
            P("dp", ("seq", "head"), None),
            P("dp", ("seq", "head"), None),
            P(None, "head"),
            P("head", None),
        ),
        check_vma=False,
    )
```

```python
import functools
import math

import jax
import jax.numpy as jnp
from jax import lax
from jax.experimental import pallas as pl
from jax.experimental.pallas import tpu as pltpu
from jax.sharding import PartitionSpec as P

D = 512
HEADS = 8
HD = 64
BLK = 128
NNZ = 9
PER = 8
NB = 64
EPSILON = 1e-05
LOG2E = math.log2(math.e)
MESH = pl.DeviceIdType.MESH
F32 = jnp.float32
BF16 = jnp.bfloat16
CAT = NNZ * BLK

BATCHES = ((0, 1), (1, 2), (3, 2), (5, 2), (7, 1))

(
    Z_BQO, Z_BKV, Z_S3A, Z_S3B, G_ST, G_S1A, G_S1B, G_S4A, G_S4B,
) = range(9)


def dot_nn(a, b):
    return lax.dot_general(a, b, (((1,), (0,)), ((), ())), preferred_element_type=F32)


def dot_nt(a, b):
    return lax.dot_general(a, b, (((1,), (1,)), ((), ())), preferred_element_type=F32)


def place(rel):
    return jnp.where(rel == 0, 0, jnp.where(rel <= 4, 2 * rel - 1, 16 - 2 * rel))


def tile(n):
    return slice(n * BLK, (n + 1) * BLK)


def kernel(
    bias_ref, tok_hbm, gout_hbm, wqkv_hbm, wout_hbm, bins_hbm, pat_hbm,
    out_ref, gtok_ref, fin,
    gkv, gqd, hid, gog, tok, tok_in, gout_in, bins_in, pat_in, wqkv, wout, bins, patv, pat, wcat, wo2, normed_ref, spread_ref,
    ycats, ycat, probs, sd, pd, a2, stcol, strow, stg, deltas, invs, binsf, binst,
    obuf, bqo, bkv, rqo, rkv, dtqo, dtkv,
    wpart, ars, arr, dpx, zbc, att, gp, res, gres,
    ss, rr, ys, yr, zs, zr, xs, xr, xe, ins, sws, swr,
):
    dp = lax.axis_index("dp")
    z = lax.axis_index("seq")
    head = lax.axis_index("head")
    yhi, c = dp // 2, lax.rem(dp, 2)
    x, ylo = head // 2, lax.rem(head, 2)
    r = 2 * x + c
    seqno = 2 * yhi + ylo
    moved = c != ylo
    odd = lax.rem(z, 2) == 1
    factor = 1.0 / math.sqrt(HD)
    c2 = factor * LOG2E

    def mod8(v):
        return lax.rem(v + 16, 8)

    def device(xx, cc):
        return {"dp": 2 * yhi + cc, "head": 2 * xx + ylo}

    partner = {"dp": 2 * yhi + ylo, "head": 2 * x + c}
    sibling = {"dp": 2 * yhi + (1 - c)}

    def member(d):
        dx, dc = d // 2, d % 2
        xx = lax.rem(x + dx, 4)
        cc = c if dc == 0 else 1 - c
        return xx, cc

    def giver(d):
        dx, dc = d // 2, d % 2
        xx = lax.rem(x + 4 - dx, 4)
        cc = c if dc == 0 else 1 - c
        return 2 * xx + cc

    def remote(src, dst, ssem, rsem, dev):
        return pltpu.make_async_remote_copy(
            src_ref=src, dst_ref=dst, send_sem=ssem, recv_sem=rsem,
            device_id=dev, device_id_type=MESH,
        )

    def start(copy):
        copy.start()
        return copy

    def wait_bytes(ref, sem):
        pltpu.make_async_copy(ref, ref, sem).wait()

    def when(cond, fn):
        pl.when(cond)(fn)

    barrier = pltpu.get_barrier_semaphore()

    def greet(dev):
        pl.semaphore_signal(barrier, inc=1, device_id=dev, device_id_type=MESH)

    for d in range(1, 8):
        greet({"seq": mod8(z + d)})
        greet(device(*member(d)))
    others = []
    for e in range(1, 4):
        yh = yhi if e // 2 == 0 else 1 - yhi
        yl = ylo if e % 2 == 0 else 1 - ylo
        others.append({"dp": 2 * yh + c, "head": 2 * x + yl})
        greet(others[-1])
    when(moved, lambda: greet(partner))

    weights = [
        pltpu.make_async_copy(wqkv_hbm, wqkv, ins.at[0]),
        pltpu.make_async_copy(wout_hbm, wout, ins.at[1]),
    ]
    loads = [
        pltpu.make_async_copy(tok_hbm, tok_in, ins.at[2]),
        pltpu.make_async_copy(gout_hbm, gout_in, ins.at[3]),
        pltpu.make_async_copy(bins_hbm, bins_in, ins.at[4]),
        pltpu.make_async_copy(pat_hbm, pat_in, ins.at[5]),
    ]
    go = [
        remote(tok_in, tok, sws.at[0], swr.at[0], partner),
        remote(gout_in, gog.at[0], sws.at[1], swr.at[1], partner),
    ]
    share = [
        remote(bins_in, bins, sws.at[2], swr.at[2], sibling),
        remote(pat_in, patv, sws.at[5], swr.at[5], sibling),
    ]
    for copy in loads + weights:
        copy.start()
    stays = jnp.logical_not(moved)

    lane = lax.broadcasted_iota(jnp.int32, (BLK, 2 * HD), 1)
    low = lane < HD

    def swap(v):
        return pltpu.roll(v, HD, 1)

    for copy in weights:
        copy.wait()
    pair = pl.multiple_of((z // 2) * 384, 128)
    for q in range(4):
        rows = slice(128 * q, 128 * (q + 1))
        w0 = wqkv[rows, pl.ds(pair, 128)].astype(F32)
        w1 = wqkv[rows, pl.ds(pair + 128, 128)].astype(F32)
        w2 = wqkv[rows, pl.ds(pair + 256, 128)].astype(F32)
        s1 = swap(w1)
        wcat[rows, 0:128] = jnp.where(odd, w2, jnp.where(low, swap(w0), s1)).astype(BF16)
        wcat[rows, 128:256] = jnp.where(low, jnp.where(odd, s1, w0), 0.0).astype(BF16)
    wo_pair = wout[pl.ds(pl.multiple_of((z // 2) * 128, 128), 128), :]
    wo2[0:HD, :] = jnp.zeros((HD, D), BF16)
    wo2[HD:BLK, :] = jnp.where(odd, wo_pair[HD:BLK, :], wo_pair[0:HD, :])

    for copy in loads:
        copy.wait()

    def keep(dst, src):
        def fn():
            dst[...] = src[...]

        when(stays, fn)

    keep(tok, tok_in)
    keep(gog.at[0], gout_in)
    keep(bins, bins_in)
    keep(patv, pat_in)

    pl.semaphore_wait(barrier, 17 + jnp.where(moved, 1, 0))
    when(moved, lambda: go[0].start())
    when(moved, lambda: go[0].wait_send())
    when(moved, lambda: go[1].start())
    when(moved, lambda: go[0].wait_recv())

    tokens = tok[...].astype(F32)
    spread = jnp.sqrt(jnp.mean(tokens * tokens, axis=-1, keepdims=True) + EPSILON)
    normed = tokens / spread
    normed_ref[...] = normed
    spread_ref[...] = spread
    hid[0] = normed.astype(BF16)

    rings = (hid, gog)
    table = {}

    def hop(k, way, t, part):
        if way == 0:
            src, dst = (0 if t == 1 else 2 * (t - 1)), (2 * t if t < 4 else 7)
        else:
            src, dst = (0 if t == 1 else 2 * (t - 1) - 1), 2 * t - 1
        rows = pl.ds(64 * part, 64)
        return remote(
            rings[k].at[src, rows], rings[k].at[dst, rows],
            zs.at[k], zr.at[k, way, t - 1, part],
            {"seq": mod8(z + 1) if way == 0 else mod8(z - 1)},
        )

    def first_hop(k):
        for part in (0, 1):
            for way in (0, 1):
                table[k, way, 1, part] = start(hop(k, way, 1, part))

    def next_hop(k, t):
        for part in (0, 1):
            for way in (0, 1):
                table[k, way, t, part].wait_recv()
                if t + 1 < 4 or part == way:
                    table[k, way, t + 1, part] = start(hop(k, way, t + 1, part))

    def last_hop(k):
        for way in (0, 1):
            table[k, way, 4, way].wait_recv()

    pools = (gkv, gqd)
    ring_x = {}
    x_right, x_left = lax.rem(x + 1, 4), lax.rem(x + 3, 4)
    x_far = lax.rem(x + 2, 4)

    gates = {0: 0, 1: 1, 5: 2}

    def xcopy(k, b, kind, owner, dev):
        first, count = BATCHES[b]
        part = pools[k].at[owner, pl.ds(first, count)]
        rsem = xr.at[k, b, gates[kind]] if kind in gates else xe.at[k]
        ring_x[k, b, kind] = start(remote(part, part, xs.at[k], rsem, dev))

    def x_own(k, b):
        xcopy(k, b, 0, r, device(x_right, c))
        xcopy(k, b, 1, r, device(x_left, c))
        xcopy(k, b, 2, r, sibling)
        if b >= 2:
            xcopy(k, b, 5, r, device(x_far, c))

    def x_pass(k, b):
        ring_x[k, b, 0].wait_recv()
        if b == 0:
            xcopy(k, b, 5, 2 * x_left + c, device(x_right, c))
        xcopy(k, b, 3, 2 * x_left + c, sibling)
        ring_x[k, b, 1].wait_recv()
        if b == 1:
            xcopy(k, b, 5, 2 * x_right + c, device(x_left, c))
        xcopy(k, b, 4, 2 * x_right + c, sibling)

    def x_far_pass(k, b):
        ring_x[k, b, 5].wait_recv()
        xcopy(k, b, 6, 2 * x_far + c, sibling)

    def x_end(k):
        wait_bytes(pools[k].at[pl.ds(0, 4)], xe.at[k])

    def project(b):
        first, count = BATCHES[b]
        for p in range(first, first + count):
            t = dot_nn(hid[p], wcat[...]).astype(BF16)
            gkv[r, p] = t[:, 0:128]
            gqd[r, p] = t[:, 128:256]
        x_own(0, b)

    def project_grad(b):
        first, count = BATCHES[b]
        for p in range(first, first + count):
            u = dot_nt(gog[p], wo2[...])
            gqd[r, p] = jnp.where(low, gqd[r, p], u.astype(BF16))
        x_own(1, b)

    first_hop(0)
    when(stays, lambda: [copy.start() for copy in share] and None)
    project(0)
    when(moved, lambda: go[1].wait_recv())
    first_hop(1)
    project_grad(0)

    when(moved, lambda: [copy.wait_recv() for copy in share] and None)
    to_scalars = pltpu.make_async_copy(patv, pat, ins.at[8])
    to_scalars.start()
    for q in range(NB):
        binsf[q : q + 1, :] = bins[:, tile(q)].astype(F32)
    binst[...] = jnp.concatenate([binsf[...], jnp.zeros((BLK - NB, BLK), F32)], axis=0).T
    to_scalars.wait()

    next_hop(0, 1)
    project(1)
    x_pass(0, 0)
    next_hop(1, 1)
    project_grad(1)
    x_far_pass(0, 0)
    next_hop(0, 2)
    project(2)
    x_pass(0, 1)
    x_pass(1, 0)
    next_hop(1, 2)
    project_grad(2)
    x_far_pass(0, 1)
    x_pass(1, 1)
    x_far_pass(1, 0)
    next_hop(0, 3)
    project(3)
    x_pass(0, 2)
    x_far_pass(0, 2)
    x_far_pass(1, 1)
    next_hop(1, 3)
    project_grad(3)
    last_hop(0)
    project(4)
    x_pass(1, 2)
    x_far_pass(1, 2)
    x_pass(0, 3)
    x_far_pass(0, 3)
    last_hop(1)
    project_grad(4)
    x_pass(0, 4)
    x_far_pass(0, 4)
    x_pass(1, 3)
    x_far_pass(1, 3)
    x_end(0)

    bias2 = bias_ref[z] * LOG2E

    def distance(p):
        t = (p + 1) // 2
        return jnp.where(lax.rem(p, 2) == 1, t, 8 - t)

    def own_block(p):
        return 8 * mod8(z + distance(p)) + r

    def back(kind, src, dst, d):
        return remote(src, dst, ss.at[kind], rr.at[kind], {"seq": mod8(z + d)})

    def leave(kind, buf, dst, p):
        when(p > 0, lambda: back(kind, buf.at[p], dst.at[z], distance(p)).start())

    def used_block(row, n):
        other = lax.rem(row + pat[n, 0, 0], NB)
        return other, lax.rem(other, 8), place(mod8(other // 8 - z))

    def own_bins(row):
        return jnp.sum(jnp.where(lane == row, binst[...], 0.0), axis=1, keepdims=True)

    stcol[...] = jnp.zeros((BLK, BLK), F32)

    def forward_block(p, carry):
        row = own_block(p)
        for n in range(NNZ):
            _, rn, pn = used_block(row, n)
            ycats[p, tile(n), :] = gkv[rn, pn]
        query = gqd[r, p]
        sd[0:BLK, :] = dot_nt(jnp.where(low, query, jnp.zeros_like(query)), ycats[p])
        bin_col = own_bins(row)
        top = None
        for n in range(NNZ):
            other, _, _ = used_block(row, n)
            bin_row = binsf[pl.ds(other, 1), :]
            v = sd[0:BLK, tile(n)] * c2 + jnp.where(bin_col == bin_row, bias2, 0.0)
            sd[0:BLK, tile(n)] = v
            top = v if top is None else jnp.maximum(top, v)
        m = jnp.max(top, axis=1, keepdims=True)
        total = jnp.zeros((BLK, BLK), F32)
        for n in range(NNZ):
            e = jnp.exp2(sd[0:BLK, tile(n)] - m)
            probs[p, :, tile(n)] = e
            pd[0:BLK, tile(n)] = e.astype(BF16)
            total = total + e
        total = jnp.sum(total, axis=1, keepdims=True)
        inv = 1.0 / total
        obuf[p] = (dot_nn(pd[0:BLK, :], ycats[p]) * inv).astype(BF16)
        invs[p] = inv
        stcol[...] = jnp.where(lane == 2 * p, m + jnp.log2(total), stcol[...])
        return carry

    lax.fori_loop(0, PER, forward_block, 0)
    x_pass(1, 4)
    x_far_pass(1, 4)

    for p in range(PER):
        both = gqd[r, p].astype(F32) * obuf[p].astype(F32)
        delta = jnp.sum(jnp.where(low, 0.0, both), axis=1, keepdims=True)
        deltas[p] = delta
        stcol[...] = jnp.where(lane == 2 * p + 1, delta, stcol[...])
    strow[...] = stcol[...].T
    mine = stg.at[pl.ds(pl.multiple_of(2 * PER * r, 16), 16)]
    stg[pl.ds(pl.multiple_of(2 * PER * r, 16), 16), :] = strow[0:16, :]

    def group(kind, d, src, dst):
        start(remote(src, dst, ss.at[kind], rr.at[kind], device(*member(d))))

    for d in range(1, 8):
        group(G_ST, d, mine, mine)

    def query_block(p, carry):
        block = gqd[r, p]
        sd[0:BLK, :] = dot_nt(jnp.where(low, jnp.zeros_like(block), block), ycats[p])
        delta = deltas[p]
        for n in range(NNZ):
            pd[0:BLK, tile(n)] = (
                probs[p, :, tile(n)] * (sd[0:BLK, tile(n)] - delta)
            ).astype(BF16)
        grad = dot_nn(pd[0:BLK, :], ycats[p]) * (invs[p] * factor)
        both = jnp.where(low, grad, obuf[p].astype(F32))
        bqo[p] = both.astype(BF16)
        leave(Z_BQO, bqo, rqo, p)
        dtqo[:, pl.ds(pl.multiple_of(p * BLK, BLK), BLK)] = both.T.astype(BF16)
        return carry

    lax.fori_loop(0, PER, query_block, 0)

    rqo[z] = bqo[0]

    def stage1(k, part):
        wpart[k] = part
        for q in range(8):
            ars[k, q] = part[16 * q : 16 * (q + 1), :].astype(BF16)
        for d in range(1, 8):
            xx, cc = member(d)
            group((G_S1A, G_S1B)[k], d, ars.at[k, 2 * xx + cc], arr.at[k, r])

    def stage2(k):
        wait_bytes(arr.at[k, pl.ds(0, 7)], rr.at[(G_S1A, G_S1B)[k]])
        total = wpart[k, pl.ds(pl.multiple_of(16 * r, 16), 16), :]
        for d in range(1, 8):
            total = total + arr[k, giver(d)].astype(F32)
        dpx[k, seqno] = total.astype(BF16)
        slot = dpx.at[k, seqno]
        for e in range(1, 4):
            start(remote(slot, slot, ys.at[k], yr.at[k], others[e - 1]))

    mine_here = lax.rem(z, 2) == ylo
    not_here = jnp.logical_not(mine_here)

    def stage3(k):
        wait_bytes(dpx.at[k, pl.ds(0, 3)], yr.at[k])
        total = dpx[k, 0].astype(F32)
        for q in range(1, 4):
            total = total + dpx[k, q].astype(F32)
        slot = zbc.at[k, z // 2]
        kind = (Z_S3A, Z_S3B)[k]

        def spread_out():
            zbc[k, z // 2] = total.astype(BF16)
            for d in range(1, 8):
                remote(slot, slot, ss.at[kind], rr.at[kind], {"seq": mod8(z + d)}).start()

        when(mine_here, spread_out)

    def stage4(k):
        kind = (Z_S3A, Z_S3B)[k]
        when(mine_here, lambda: wait_bytes(zbc.at[k, pl.ds(0, 3)], rr.at[kind]))
        when(not_here, lambda: wait_bytes(zbc.at[k, pl.ds(0, 4)], rr.at[kind]))
        fin[k, r] = zbc[k, x]
        for d in range(1, 8):
            xx, _ = member(d)
            group((G_S4A, G_S4B)[k], d, zbc.at[k, xx], fin.at[k, r])

    hid_all = hid[...].reshape(PER * BLK, D)
    go_all = gog[...].reshape(PER * BLK, D)
    part0 = jnp.concatenate(
        [dot_nn(dtqo[0:HD, :], hid_all), dot_nn(dtqo[HD : 2 * HD, :], go_all)], axis=0
    )
    stage1(0, part0)
    wait_bytes(stg.at[pl.ds(0, 7 * 16)], rr.at[G_ST])
    x_end(1)

    def key_block(p, carry):
        row = own_block(p)
        for n in range(NNZ):
            _, rn, pn = used_block(row, n)
            ycat[tile(n), :] = gqd[rn, pn]
        block = gkv[r, p]
        zero = jnp.zeros_like(block)
        a2[0:BLK, :] = jnp.where(low, block, zero)
        a2[BLK : 2 * BLK, :] = jnp.where(low, zero, block)
        sd[...] = dot_nt(a2[...], ycat[...])
        bin_col = own_bins(row)
        for n in range(NNZ):
            other, rn, pn = used_block(row, n)
            bin_row = binsf[pl.ds(other, 1), :]
            log_row = stg[pl.ds(16 * rn + 2 * pn, 1), :]
            delta_row = stg[pl.ds(16 * rn + 2 * pn + 1, 1), :]
            v = sd[0:BLK, tile(n)] * c2 + jnp.where(bin_col == bin_row, bias2, 0.0)
            e = jnp.exp2(v - log_row)
            pd[0:BLK, tile(n)] = e.astype(BF16)
            pd[BLK : 2 * BLK, tile(n)] = (e * (sd[BLK : 2 * BLK, tile(n)] - delta_row)).astype(BF16)
        g = dot_nn(pd[...], ycat[...])
        both = jnp.where(low, g[BLK : 2 * BLK] * factor, g[0:BLK])
        bkv[p] = both.astype(BF16)
        leave(Z_BKV, bkv, rkv, p)
        dtkv[:, pl.ds(pl.multiple_of(p * BLK, BLK), BLK)] = both.T.astype(BF16)
        return carry

    lax.fori_loop(0, PER, key_block, 0)

    rkv[z] = bkv[0]
    stage1(1, dot_nn(dtkv[...], hid[...].reshape(PER * BLK, D)))
    stage2(0)

    def deliver(src, dst, k):
        there = remote(src, dst, sws.at[3 + k], swr.at[3 + k], partner)
        keep(dst, src)
        when(moved, lambda: there.start())
        return there

    wait_bytes(rqo.at[pl.ds(0, 7)], rr.at[Z_BQO])
    for g in range(HEADS // 2):
        even, uneven = rqo[2 * g].astype(F32), rqo[2 * g + 1].astype(F32)
        att[:, tile(g)] = jnp.where(low, swap(even), uneven).astype(BF16)
    res[...] = dot_nn(att[...], wout[...]).astype(BF16)
    d_out = deliver(res, out_ref, 0)
    stage2(1)
    stage3(0)
    stage3(1)
    stage4(0)

    wait_bytes(rkv.at[pl.ds(0, 7)], rr.at[Z_BKV])
    for g in range(HEADS // 2):
        qo_even, qo_odd = rqo[2 * g].astype(F32), rqo[2 * g + 1].astype(F32)
        kv_even = swap(rkv[2 * g].astype(F32))
        gp[:, tile(3 * g)] = jnp.where(low, qo_even, kv_even).astype(BF16)
        gp[:, tile(3 * g + 1)] = jnp.where(low, kv_even, swap(qo_odd)).astype(BF16)
        gp[:, tile(3 * g + 2)] = rkv[2 * g + 1]
    grad_hidden = dot_nt(gp[...], wqkv[...])
    normed = normed_ref[...]
    inner = jnp.mean(grad_hidden * normed, axis=-1, keepdims=True)
    gres[...] = ((grad_hidden - normed * inner) / spread_ref[...]).astype(BF16)
    d_gtok = deliver(gres, gtok_ref, 1)
    stage4(1)

    for k in (0, 1):
        wait_bytes(fin.at[k, pl.ds(0, 7)], rr.at[(G_S4A, G_S4B)[k]])
    for k in (0, 1):
        wait_bytes(rings[k].at[pl.ds(0, 7)], zs.at[k])
        wait_bytes(pools[k].at[pl.ds(0, 7)], xs.at[k])
        wait_bytes(dpx.at[k, pl.ds(0, 3)], ys.at[k])
        wait_bytes(arr.at[k, pl.ds(0, 7)], ss.at[(G_S1A, G_S1B)[k]])
        wait_bytes(arr.at[k, pl.ds(0, 7)], ss.at[(G_S4A, G_S4B)[k]])
    wait_bytes(rqo.at[pl.ds(0, 7)], ss.at[Z_BQO])
    wait_bytes(rkv.at[pl.ds(0, 7)], ss.at[Z_BKV])
    wait_bytes(stg.at[pl.ds(0, 7 * 16)], ss.at[G_ST])

    def spread_sent():
        for kind in (Z_S3A, Z_S3B):
            wait_bytes(arr.at[0, pl.ds(0, 7)], ss.at[kind])

    when(mine_here, spread_sent)
    when(moved, lambda: go[1].wait_send())
    when(stays, lambda: [copy.wait_send() for copy in share] and None)
    for there in (d_out, d_gtok):
        when(moved, lambda: there.wait())


def finish(out_in, gtok_in, fin_ref, out_ref, gtok_ref, gqkv_ref, gwo_ref):
    out_ref[...] = out_in[...]
    gtok_ref[...] = gtok_in[...]
    first = fin_ref[0].reshape(BLK, D).astype(F32)
    second = fin_ref[1].reshape(BLK, D).astype(F32)
    gwo_ref[...] = first[HD : 2 * HD, :]
    gqkv_ref[0:HD, :] = first[0:HD, :]
    gqkv_ref[HD : 3 * HD, :] = second


def body(tokens, bin_ids, pattern, w_qkv, w_out, head_bias, grad_output):
    vmem = pl.BlockSpec(memory_space=pltpu.VMEM)
    smem = pl.BlockSpec(memory_space=pltpu.SMEM)
    hbm = pl.BlockSpec(memory_space=pltpu.HBM)
    dma = pltpu.SemaphoreType.DMA
    half = functools.partial(pltpu.VMEM, dtype=BF16)
    full = functools.partial(pltpu.VMEM, dtype=F32)
    scratch = [
        half((8, 8, BLK, 128)),
        half((8, 8, BLK, 128)),
        half((8, BLK, D)),
        half((8, BLK, D)),
        half((BLK, D)),
        half((BLK, D)),
        half((BLK, D)),
        pltpu.VMEM((1, NB * BLK), jnp.int32),
        pltpu.VMEM((NNZ, 1, NB), jnp.int32),
        half((D, 3 * D)),
        half((D, D)),
        pltpu.VMEM((1, NB * BLK), jnp.int32),
        pltpu.VMEM((NNZ, 1, NB), jnp.int32),
        pltpu.SMEM((NNZ, 1, NB), jnp.int32),
        half((D, 256)),
        half((BLK, D)),
        full((BLK, D)),
        full((BLK, 1)),
        half((PER, CAT, 128)),
        half((CAT, 128)),
        full((PER, BLK, CAT)),
        full((2 * BLK, CAT)),
        half((2 * BLK, CAT)),
        half((2 * BLK, 128)),
        full((BLK, BLK)),
        full((BLK, BLK)),
        full((2 * NB, BLK)),
        full((PER, BLK, 1)),
        full((PER, BLK, 1)),
        full((NB, BLK)),
        full((BLK, BLK)),
        half((8, BLK, 128)),
        half((8, BLK, 128)),
        half((8, BLK, 128)),
        half((8, BLK, 128)),
        half((8, BLK, 128)),
        half((BLK, PER * BLK)),
        half((BLK, PER * BLK)),
        full((2, BLK, D)),
        half((2, 8, 16, D)),
        half((2, 8, 16, D)),
        half((2, 4, 16, D)),
        half((2, 4, 16, D)),
        half((BLK, D)),
        half((BLK, 3 * D)),
        half((BLK, D)),
        half((BLK, D)),
        dma((9,)),
        dma((9,)),
        dma((2,)),
        dma((2,)),
        dma((2,)),
        dma((2, 2, 4, 2)),
        dma((2,)),
        dma((2, 5, 3)),
        dma((2,)),
        dma((9,)),
        dma((6,)),
        dma((6,)),
    ]
    shapes = (
        jax.ShapeDtypeStruct((BLK, D), BF16),
        jax.ShapeDtypeStruct((BLK, D), BF16),
    )
    parts = pl.pallas_call(
        kernel,
        out_shape=shapes + (jax.ShapeDtypeStruct((2, 8, 16, D), BF16),),
        in_specs=[smem, hbm, hbm, hbm, hbm, hbm, hbm],
        out_specs=(vmem, vmem, vmem),
        scratch_shapes=scratch,
        compiler_params=pltpu.CompilerParams(
            collective_id=0, has_side_effects=True, vmem_limit_bytes=62 * 1024 * 1024
        ),
        name="layer",
    )(head_bias, tokens[0], grad_output[0], w_qkv, w_out, bin_ids, pattern.transpose(2, 0, 1))
    result, grad_input, own_qkv, own_out = pl.pallas_call(
        finish,
        out_shape=shapes
        + (
            jax.ShapeDtypeStruct((3 * HD, D), F32),
            jax.ShapeDtypeStruct((HD, D), F32),
        ),
        in_specs=[vmem, vmem, vmem],
        out_specs=(vmem, vmem, vmem, vmem),
        name="finish",
    )(*parts)
    return (result[None], grad_input[None], own_qkv.T, own_out)


def solution(mesh):
    return jax.shard_map(
        body,
        mesh=mesh,
        in_specs=(
            P("dp", ("seq", "head"), None),
            P("dp", None),
            P("dp", None, None),
            P(),
            P(),
            P(),
            P("dp", ("seq", "head"), None),
        ),
        out_specs=(
            P("dp", ("seq", "head"), None),
            P("dp", ("seq", "head"), None),
            P(None, "head"),
            P("head", None),
        ),
        check_vma=False,
    )
```

```python
import functools
import math

import jax
import jax.numpy as jnp
from jax import lax
from jax.experimental import pallas as pl
from jax.experimental.pallas import tpu as pltpu
from jax.sharding import PartitionSpec as P

D = 512
HEADS = 8
HD = 64
BLK = 128
NNZ = 9
PER = 8
NB = 64
EPSILON = 1e-05
LOG2E = math.log2(math.e)
MESH = pl.DeviceIdType.MESH
F32 = jnp.float32
BF16 = jnp.bfloat16
CAT = NNZ * BLK

BATCHES = ((0, 1), (1, 2), (3, 2), (5, 2), (7, 1))

(
    Z_BQO, Z_BKV, Z_S3A, Z_S3B, G_ST, G_S1A, G_S1B, G_S4A, G_S4B,
) = range(9)


def dot_nn(a, b):
    return lax.dot_general(a, b, (((1,), (0,)), ((), ())), preferred_element_type=F32)


def dot_nt(a, b):
    return lax.dot_general(a, b, (((1,), (1,)), ((), ())), preferred_element_type=F32)


def place(rel):
    return jnp.where(rel == 0, 0, jnp.where(rel <= 4, 2 * rel - 1, 16 - 2 * rel))


def tile(n):
    return slice(n * BLK, (n + 1) * BLK)


def kernel(
    bias_ref, tok_hbm, gout_hbm, wqkv_hbm, wout_hbm, bins_hbm, pat_hbm,
    out_ref, gtok_ref, fin,
    gkv, gqd, hid, gog, tok, tok_in, gout_in, bins_in, pat_in, wqkv, wout, bins, patv, pat, wcat, wo2, normed_ref, spread_ref,
    ycats, ycat, probs, sd, pd, a2, stcol, strow, stg, deltas, invs, binsf, binst,
    obuf, bqo, bkv, rqo, rkv, dtqo, dtkv,
    wpart, ars, arr, dpx, zbc, att, gp, res, gres,
    ss, rr, ys, yr, zs, zr, xs, xr, xe, ins, sws, swr,
):
    dp = lax.axis_index("dp")
    z = lax.axis_index("seq")
    head = lax.axis_index("head")
    yhi, c = dp // 2, lax.rem(dp, 2)
    x, ylo = head // 2, lax.rem(head, 2)
    r = 2 * x + c
    seqno = 2 * yhi + ylo
    moved = c != ylo
    odd = lax.rem(z, 2) == 1
    factor = 1.0 / math.sqrt(HD)
    c2 = factor * LOG2E

    def mod8(v):
        return lax.rem(v + 16, 8)

    def device(xx, cc):
        return {"dp": 2 * yhi + cc, "head": 2 * xx + ylo}

    partner = {"dp": 2 * yhi + ylo, "head": 2 * x + c}
    sibling = {"dp": 2 * yhi + (1 - c)}

    def member(d):
        dx, dc = d // 2, d % 2
        xx = lax.rem(x + dx, 4)
        cc = c if dc == 0 else 1 - c
        return xx, cc

    def giver(d):
        dx, dc = d // 2, d % 2
        xx = lax.rem(x + 4 - dx, 4)
        cc = c if dc == 0 else 1 - c
        return 2 * xx + cc

    def remote(src, dst, ssem, rsem, dev):
        return pltpu.make_async_remote_copy(
            src_ref=src, dst_ref=dst, send_sem=ssem, recv_sem=rsem,
            device_id=dev, device_id_type=MESH,
        )

    def start(copy):
        copy.start()
        return copy

    def wait_bytes(ref, sem):
        pltpu.make_async_copy(ref, ref, sem).wait()

    def when(cond, fn):
        pl.when(cond)(fn)

    barrier = pltpu.get_barrier_semaphore()

    def greet(dev):
        pl.semaphore_signal(barrier, inc=1, device_id=dev, device_id_type=MESH)

    for d in (1, 7):
        greet({"seq": mod8(z + d)})
    for d in (1, 2, 3):
        greet(device(lax.rem(x + d, 4), c))
    greet(sibling)
    others = []
    for e in range(1, 4):
        yh = yhi if e // 2 == 0 else 1 - yhi
        yl = ylo if e % 2 == 0 else 1 - ylo
        others.append({"dp": 2 * yh + c, "head": 2 * x + yl})
        greet(others[-1])
    when(moved, lambda: greet(partner))

    weights = [
        pltpu.make_async_copy(wqkv_hbm, wqkv, ins.at[0]),
        pltpu.make_async_copy(wout_hbm, wout, ins.at[1]),
    ]
    loads = [
        pltpu.make_async_copy(tok_hbm, tok_in, ins.at[2]),
        pltpu.make_async_copy(gout_hbm, gout_in, ins.at[3]),
        pltpu.make_async_copy(bins_hbm, bins_in, ins.at[4]),
        pltpu.make_async_copy(pat_hbm, pat_in, ins.at[5]),
    ]
    go = [
        remote(tok_in, tok, sws.at[0], swr.at[0], partner),
        remote(gout_in, gog.at[0], sws.at[1], swr.at[1], partner),
    ]
    share = [
        remote(bins_in, bins, sws.at[2], swr.at[2], sibling),
        remote(pat_in, patv, sws.at[5], swr.at[5], sibling),
    ]
    for copy in loads + weights:
        copy.start()
    stays = jnp.logical_not(moved)

    lane = lax.broadcasted_iota(jnp.int32, (BLK, 2 * HD), 1)
    low = lane < HD

    def swap(v):
        return pltpu.roll(v, HD, 1)

    for copy in weights:
        copy.wait()
    pair = pl.multiple_of((z // 2) * 384, 128)
    for q in range(4):
        rows = slice(128 * q, 128 * (q + 1))
        w0 = wqkv[rows, pl.ds(pair, 128)].astype(F32)
        w1 = wqkv[rows, pl.ds(pair + 128, 128)].astype(F32)
        w2 = wqkv[rows, pl.ds(pair + 256, 128)].astype(F32)
        s1 = swap(w1)
        wcat[rows, 0:128] = jnp.where(odd, w2, jnp.where(low, swap(w0), s1)).astype(BF16)
        wcat[rows, 128:256] = jnp.where(low, jnp.where(odd, s1, w0), 0.0).astype(BF16)
    wo_pair = wout[pl.ds(pl.multiple_of((z // 2) * 128, 128), 128), :]
    wo2[0:HD, :] = jnp.zeros((HD, D), BF16)
    wo2[HD:BLK, :] = jnp.where(odd, wo_pair[HD:BLK, :], wo_pair[0:HD, :])

    for copy in loads:
        copy.wait()

    def keep(dst, src):
        def fn():
            dst[...] = src[...]

        when(stays, fn)

    keep(tok, tok_in)
    keep(gog.at[0], gout_in)
    keep(bins, bins_in)
    keep(patv, pat_in)

    pl.semaphore_wait(barrier, 9 + jnp.where(moved, 1, 0))
    when(moved, lambda: go[0].start())
    when(moved, lambda: go[0].wait_send())
    when(moved, lambda: go[1].start())
    when(moved, lambda: go[0].wait_recv())

    tokens = tok[...].astype(F32)
    spread = jnp.sqrt(jnp.mean(tokens * tokens, axis=-1, keepdims=True) + EPSILON)
    normed = tokens / spread
    normed_ref[...] = normed
    spread_ref[...] = spread
    hid[0] = normed.astype(BF16)

    rings = (hid, gog)
    table = {}

    def hop(k, way, t, part):
        if way == 0:
            src, dst = (0 if t == 1 else 2 * (t - 1)), (2 * t if t < 4 else 7)
        else:
            src, dst = (0 if t == 1 else 2 * (t - 1) - 1), 2 * t - 1
        rows = pl.ds(64 * part, 64)
        return remote(
            rings[k].at[src, rows], rings[k].at[dst, rows],
            zs.at[k], zr.at[k, way, t - 1, part],
            {"seq": mod8(z + 1) if way == 0 else mod8(z - 1)},
        )

    def first_hop(k):
        for part in (0, 1):
            for way in (0, 1):
                table[k, way, 1, part] = start(hop(k, way, 1, part))

    def next_hop(k, t):
        for part in (0, 1):
            for way in (0, 1):
                table[k, way, t, part].wait_recv()
                if t + 1 < 4 or part == way:
                    table[k, way, t + 1, part] = start(hop(k, way, t + 1, part))

    def last_hop(k):
        for way in (0, 1):
            table[k, way, 4, way].wait_recv()

    pools = (gkv, gqd)
    ring_x = {}
    x_right, x_left = lax.rem(x + 1, 4), lax.rem(x + 3, 4)
    x_far = lax.rem(x + 2, 4)

    gates = {0: 0, 1: 1, 5: 2}

    def xcopy(k, b, kind, owner, dev):
        first, count = BATCHES[b]
        part = pools[k].at[owner, pl.ds(first, count)]
        rsem = xr.at[k, b, gates[kind]] if kind in gates else xe.at[k]
        ring_x[k, b, kind] = start(remote(part, part, xs.at[k], rsem, dev))

    def x_own(k, b):
        xcopy(k, b, 0, r, device(x_right, c))
        xcopy(k, b, 1, r, device(x_left, c))
        xcopy(k, b, 2, r, sibling)
        if b >= 2:
            xcopy(k, b, 5, r, device(x_far, c))

    def x_pass(k, b):
        ring_x[k, b, 0].wait_recv()
        if b == 0:
            xcopy(k, b, 5, 2 * x_left + c, device(x_right, c))
        xcopy(k, b, 3, 2 * x_left + c, sibling)
        ring_x[k, b, 1].wait_recv()
        if b == 1:
            xcopy(k, b, 5, 2 * x_right + c, device(x_left, c))
        xcopy(k, b, 4, 2 * x_right + c, sibling)

    def x_far_pass(k, b):
        ring_x[k, b, 5].wait_recv()
        xcopy(k, b, 6, 2 * x_far + c, sibling)

    def x_end(k):
        wait_bytes(pools[k].at[pl.ds(0, 4)], xe.at[k])

    def project(b):
        first, count = BATCHES[b]
        for p in range(first, first + count):
            t = dot_nn(hid[p], wcat[...]).astype(BF16)
            gkv[r, p] = t[:, 0:128]
            gqd[r, p] = t[:, 128:256]
        x_own(0, b)

    def project_grad(b):
        first, count = BATCHES[b]
        for p in range(first, first + count):
            u = dot_nt(gog[p], wo2[...])
            gqd[r, p] = jnp.where(low, gqd[r, p], u.astype(BF16))
        x_own(1, b)

    first_hop(0)
    when(stays, lambda: [copy.start() for copy in share] and None)
    project(0)
    when(moved, lambda: go[1].wait_recv())
    first_hop(1)
    project_grad(0)

    when(moved, lambda: [copy.wait_recv() for copy in share] and None)
    to_scalars = pltpu.make_async_copy(patv, pat, ins.at[8])
    to_scalars.start()
    for q in range(NB):
        binsf[q : q + 1, :] = bins[:, tile(q)].astype(F32)
    binst[...] = jnp.concatenate([binsf[...], jnp.zeros((BLK - NB, BLK), F32)], axis=0).T
    to_scalars.wait()

    next_hop(0, 1)
    project(1)
    x_pass(0, 0)
    next_hop(1, 1)
    project_grad(1)
    x_far_pass(0, 0)
    next_hop(0, 2)
    project(2)
    x_pass(0, 1)
    x_pass(1, 0)
    next_hop(1, 2)
    project_grad(2)
    x_far_pass(0, 1)
    x_pass(1, 1)
    x_far_pass(1, 0)
    next_hop(0, 3)
    project(3)
    x_pass(0, 2)
    x_far_pass(0, 2)
    x_far_pass(1, 1)
    next_hop(1, 3)
    project_grad(3)
    last_hop(0)
    project(4)
    x_pass(1, 2)
    x_far_pass(1, 2)
    x_pass(0, 3)
    x_far_pass(0, 3)
    last_hop(1)
    project_grad(4)
    x_pass(0, 4)
    x_far_pass(0, 4)
    x_pass(1, 3)
    x_far_pass(1, 3)
    x_end(0)

    bias2 = bias_ref[z] * LOG2E

    def distance(p):
        t = (p + 1) // 2
        return jnp.where(lax.rem(p, 2) == 1, t, 8 - t)

    def own_block(p):
        return 8 * mod8(z + distance(p)) + r

    def back(kind, src, dst, d):
        return remote(src, dst, ss.at[kind], rr.at[kind], {"seq": mod8(z + d)})

    def leave(kind, buf, dst, p):
        when(p > 0, lambda: back(kind, buf.at[p], dst.at[z], distance(p)).start())

    def used_block(row, n):
        other = lax.rem(row + pat[n, 0, 0], NB)
        return other, lax.rem(other, 8), place(mod8(other // 8 - z))

    def own_bins(row):
        return jnp.sum(jnp.where(lane == row, binst[...], 0.0), axis=1, keepdims=True)

    stcol[...] = jnp.zeros((BLK, BLK), F32)

    def forward_block(p, carry):
        row = own_block(p)
        for n in range(NNZ):
            _, rn, pn = used_block(row, n)
            ycats[p, tile(n), :] = gkv[rn, pn]
        query = gqd[r, p]
        sd[0:BLK, :] = dot_nt(jnp.where(low, query, jnp.zeros_like(query)), ycats[p])
        bin_col = own_bins(row)
        top = None
        for n in range(NNZ):
            other, _, _ = used_block(row, n)
            bin_row = binsf[pl.ds(other, 1), :]
            v = sd[0:BLK, tile(n)] * c2 + jnp.where(bin_col == bin_row, bias2, 0.0)
            sd[0:BLK, tile(n)] = v
            top = v if top is None else jnp.maximum(top, v)
        m = jnp.max(top, axis=1, keepdims=True)
        total = jnp.zeros((BLK, BLK), F32)
        for n in range(NNZ):
            e = jnp.exp2(sd[0:BLK, tile(n)] - m)
            probs[p, :, tile(n)] = e
            pd[0:BLK, tile(n)] = e.astype(BF16)
            total = total + e
        total = jnp.sum(total, axis=1, keepdims=True)
        inv = 1.0 / total
        obuf[p] = (dot_nn(pd[0:BLK, :], ycats[p]) * inv).astype(BF16)
        invs[p] = inv
        stcol[...] = jnp.where(lane == 2 * p, m + jnp.log2(total), stcol[...])
        return carry

    lax.fori_loop(0, PER, forward_block, 0)
    x_pass(1, 4)
    x_far_pass(1, 4)

    for p in range(PER):
        both = gqd[r, p].astype(F32) * obuf[p].astype(F32)
        delta = jnp.sum(jnp.where(low, 0.0, both), axis=1, keepdims=True)
        deltas[p] = delta
        stcol[...] = jnp.where(lane == 2 * p + 1, delta, stcol[...])
    strow[...] = stcol[...].T
    mine = stg.at[pl.ds(pl.multiple_of(2 * PER * r, 16), 16)]
    stg[pl.ds(pl.multiple_of(2 * PER * r, 16), 16), :] = strow[0:16, :]

    def group(kind, d, src, dst):
        start(remote(src, dst, ss.at[kind], rr.at[kind], device(*member(d))))

    for d in range(1, 8):
        group(G_ST, d, mine, mine)

    def query_block(p, carry):
        block = gqd[r, p]
        sd[0:BLK, :] = dot_nt(jnp.where(low, jnp.zeros_like(block), block), ycats[p])
        delta = deltas[p]
        for n in range(NNZ):
            pd[0:BLK, tile(n)] = (
                probs[p, :, tile(n)] * (sd[0:BLK, tile(n)] - delta)
            ).astype(BF16)
        grad = dot_nn(pd[0:BLK, :], ycats[p]) * (invs[p] * factor)
        both = jnp.where(low, grad, obuf[p].astype(F32))
        bqo[p] = both.astype(BF16)
        leave(Z_BQO, bqo, rqo, p)
        dtqo[:, pl.ds(pl.multiple_of(p * BLK, BLK), BLK)] = both.T.astype(BF16)
        return carry

    lax.fori_loop(0, PER, query_block, 0)

    rqo[z] = bqo[0]

    def stage1(k, part):
        wpart[k] = part
        for q in range(8):
            ars[k, q] = part[16 * q : 16 * (q + 1), :].astype(BF16)
        for d in range(1, 8):
            xx, cc = member(d)
            group((G_S1A, G_S1B)[k], d, ars.at[k, 2 * xx + cc], arr.at[k, r])

    def stage2(k):
        wait_bytes(arr.at[k, pl.ds(0, 7)], rr.at[(G_S1A, G_S1B)[k]])
        total = wpart[k, pl.ds(pl.multiple_of(16 * r, 16), 16), :]
        for d in range(1, 8):
            total = total + arr[k, giver(d)].astype(F32)
        dpx[k, seqno] = total.astype(BF16)
        slot = dpx.at[k, seqno]
        for e in range(1, 4):
            start(remote(slot, slot, ys.at[k], yr.at[k], others[e - 1]))

    mine_here = lax.rem(z, 2) == ylo
    not_here = jnp.logical_not(mine_here)

    def stage3(k):
        wait_bytes(dpx.at[k, pl.ds(0, 3)], yr.at[k])
        total = dpx[k, 0].astype(F32)
        for q in range(1, 4):
            total = total + dpx[k, q].astype(F32)
        slot = zbc.at[k, z // 2]
        kind = (Z_S3A, Z_S3B)[k]

        def spread_out():
            zbc[k, z // 2] = total.astype(BF16)
            for d in range(1, 8):
                remote(slot, slot, ss.at[kind], rr.at[kind], {"seq": mod8(z + d)}).start()

        when(mine_here, spread_out)

    def stage4(k):
        kind = (Z_S3A, Z_S3B)[k]
        when(mine_here, lambda: wait_bytes(zbc.at[k, pl.ds(0, 3)], rr.at[kind]))
        when(not_here, lambda: wait_bytes(zbc.at[k, pl.ds(0, 4)], rr.at[kind]))
        fin[k, r] = zbc[k, x]
        for d in range(1, 8):
            xx, _ = member(d)
            group((G_S4A, G_S4B)[k], d, zbc.at[k, xx], fin.at[k, r])

    hid_all = hid[...].reshape(PER * BLK, D)
    go_all = gog[...].reshape(PER * BLK, D)
    part0 = jnp.concatenate(
        [dot_nn(dtqo[0:HD, :], hid_all), dot_nn(dtqo[HD : 2 * HD, :], go_all)], axis=0
    )
    stage1(0, part0)
    wait_bytes(stg.at[pl.ds(0, 7 * 16)], rr.at[G_ST])
    x_end(1)

    def key_block(p, carry):
        row = own_block(p)
        for n in range(NNZ):
            _, rn, pn = used_block(row, n)
            ycat[tile(n), :] = gqd[rn, pn]
        block = gkv[r, p]
        zero = jnp.zeros_like(block)
        a2[0:BLK, :] = jnp.where(low, block, zero)
        a2[BLK : 2 * BLK, :] = jnp.where(low, zero, block)
        sd[...] = dot_nt(a2[...], ycat[...])
        bin_col = own_bins(row)
        for n in range(NNZ):
            other, rn, pn = used_block(row, n)
            bin_row = binsf[pl.ds(other, 1), :]
            log_row = stg[pl.ds(16 * rn + 2 * pn, 1), :]
            delta_row = stg[pl.ds(16 * rn + 2 * pn + 1, 1), :]
            v = sd[0:BLK, tile(n)] * c2 + jnp.where(bin_col == bin_row, bias2, 0.0)
            e = jnp.exp2(v - log_row)
            pd[0:BLK, tile(n)] = e.astype(BF16)
            pd[BLK : 2 * BLK, tile(n)] = (e * (sd[BLK : 2 * BLK, tile(n)] - delta_row)).astype(BF16)
        g = dot_nn(pd[...], ycat[...])
        both = jnp.where(low, g[BLK : 2 * BLK] * factor, g[0:BLK])
        bkv[p] = both.astype(BF16)
        leave(Z_BKV, bkv, rkv, p)
        dtkv[:, pl.ds(pl.multiple_of(p * BLK, BLK), BLK)] = both.T.astype(BF16)
        return carry

    lax.fori_loop(0, PER, key_block, 0)

    rkv[z] = bkv[0]
    stage1(1, dot_nn(dtkv[...], hid[...].reshape(PER * BLK, D)))
    stage2(0)

    def deliver(src, dst, k):
        there = remote(src, dst, sws.at[3 + k], swr.at[3 + k], partner)
        keep(dst, src)
        when(moved, lambda: there.start())
        return there

    wait_bytes(rqo.at[pl.ds(0, 7)], rr.at[Z_BQO])
    for g in range(HEADS // 2):
        even, uneven = rqo[2 * g].astype(F32), rqo[2 * g + 1].astype(F32)
        att[:, tile(g)] = jnp.where(low, swap(even), uneven).astype(BF16)
    res[...] = dot_nn(att[...], wout[...]).astype(BF16)
    d_out = deliver(res, out_ref, 0)
    stage2(1)
    stage3(0)
    stage3(1)
    stage4(0)

    wait_bytes(rkv.at[pl.ds(0, 7)], rr.at[Z_BKV])
    for g in range(HEADS // 2):
        qo_even, qo_odd = rqo[2 * g].astype(F32), rqo[2 * g + 1].astype(F32)
        kv_even = swap(rkv[2 * g].astype(F32))
        gp[:, tile(3 * g)] = jnp.where(low, qo_even, kv_even).astype(BF16)
        gp[:, tile(3 * g + 1)] = jnp.where(low, kv_even, swap(qo_odd)).astype(BF16)
        gp[:, tile(3 * g + 2)] = rkv[2 * g + 1]
    grad_hidden = dot_nt(gp[...], wqkv[...])
    normed = normed_ref[...]
    inner = jnp.mean(grad_hidden * normed, axis=-1, keepdims=True)
    gres[...] = ((grad_hidden - normed * inner) / spread_ref[...]).astype(BF16)
    d_gtok = deliver(gres, gtok_ref, 1)
    stage4(1)

    for k in (0, 1):
        wait_bytes(fin.at[k, pl.ds(0, 7)], rr.at[(G_S4A, G_S4B)[k]])
    for k in (0, 1):
        wait_bytes(rings[k].at[pl.ds(0, 7)], zs.at[k])
        wait_bytes(pools[k].at[pl.ds(0, 7)], xs.at[k])
        wait_bytes(dpx.at[k, pl.ds(0, 3)], ys.at[k])
        wait_bytes(arr.at[k, pl.ds(0, 7)], ss.at[(G_S1A, G_S1B)[k]])
        wait_bytes(arr.at[k, pl.ds(0, 7)], ss.at[(G_S4A, G_S4B)[k]])
    wait_bytes(rqo.at[pl.ds(0, 7)], ss.at[Z_BQO])
    wait_bytes(rkv.at[pl.ds(0, 7)], ss.at[Z_BKV])
    wait_bytes(stg.at[pl.ds(0, 7 * 16)], ss.at[G_ST])

    def spread_sent():
        for kind in (Z_S3A, Z_S3B):
            wait_bytes(arr.at[0, pl.ds(0, 7)], ss.at[kind])

    when(mine_here, spread_sent)
    when(moved, lambda: go[1].wait_send())
    when(stays, lambda: [copy.wait_send() for copy in share] and None)
    for there in (d_out, d_gtok):
        when(moved, lambda: there.wait())


def finish(out_in, gtok_in, fin_ref, out_ref, gtok_ref, gqkv_ref, gwo_ref):
    out_ref[...] = out_in[...]
    gtok_ref[...] = gtok_in[...]
    first = fin_ref[0].reshape(BLK, D).astype(F32)
    second = fin_ref[1].reshape(BLK, D).astype(F32)
    gwo_ref[...] = first[HD : 2 * HD, :]
    gqkv_ref[0:HD, :] = first[0:HD, :]
    gqkv_ref[HD : 3 * HD, :] = second


def body(tokens, bin_ids, pattern, w_qkv, w_out, head_bias, grad_output):
    vmem = pl.BlockSpec(memory_space=pltpu.VMEM)
    smem = pl.BlockSpec(memory_space=pltpu.SMEM)
    hbm = pl.BlockSpec(memory_space=pltpu.HBM)
    dma = pltpu.SemaphoreType.DMA
    half = functools.partial(pltpu.VMEM, dtype=BF16)
    full = functools.partial(pltpu.VMEM, dtype=F32)
    scratch = [
        half((8, 8, BLK, 128)),
        half((8, 8, BLK, 128)),
        half((8, BLK, D)),
        half((8, BLK, D)),
        half((BLK, D)),
        half((BLK, D)),
        half((BLK, D)),
        pltpu.VMEM((1, NB * BLK), jnp.int32),
        pltpu.VMEM((NNZ, 1, NB), jnp.int32),
        half((D, 3 * D)),
        half((D, D)),
        pltpu.VMEM((1, NB * BLK), jnp.int32),
        pltpu.VMEM((NNZ, 1, NB), jnp.int32),
        pltpu.SMEM((NNZ, 1, NB), jnp.int32),
        half((D, 256)),
        half((BLK, D)),
        full((BLK, D)),
        full((BLK, 1)),
        half((PER, CAT, 128)),
        half((CAT, 128)),
        full((PER, BLK, CAT)),
        full((2 * BLK, CAT)),
        half((2 * BLK, CAT)),
        half((2 * BLK, 128)),
        full((BLK, BLK)),
        full((BLK, BLK)),
        full((2 * NB, BLK)),
        full((PER, BLK, 1)),
        full((PER, BLK, 1)),
        full((NB, BLK)),
        full((BLK, BLK)),
        half((8, BLK, 128)),
        half((8, BLK, 128)),
        half((8, BLK, 128)),
        half((8, BLK, 128)),
        half((8, BLK, 128)),
        half((BLK, PER * BLK)),
        half((BLK, PER * BLK)),
        full((2, BLK, D)),
        half((2, 8, 16, D)),
        half((2, 8, 16, D)),
        half((2, 4, 16, D)),
        half((2, 4, 16, D)),
        half((BLK, D)),
        half((BLK, 3 * D)),
        half((BLK, D)),
        half((BLK, D)),
        dma((9,)),
        dma((9,)),
        dma((2,)),
        dma((2,)),
        dma((2,)),
        dma((2, 2, 4, 2)),
        dma((2,)),
        dma((2, 5, 3)),
        dma((2,)),
        dma((9,)),
        dma((6,)),
        dma((6,)),
    ]
    shapes = (
        jax.ShapeDtypeStruct((BLK, D), BF16),
        jax.ShapeDtypeStruct((BLK, D), BF16),
    )
    parts = pl.pallas_call(
        kernel,
        out_shape=shapes + (jax.ShapeDtypeStruct((2, 8, 16, D), BF16),),
        in_specs=[smem, hbm, hbm, hbm, hbm, hbm, hbm],
        out_specs=(vmem, vmem, vmem),
        scratch_shapes=scratch,
        compiler_params=pltpu.CompilerParams(
            collective_id=0, has_side_effects=True, vmem_limit_bytes=62 * 1024 * 1024
        ),
        name="layer",
    )(head_bias, tokens[0], grad_output[0], w_qkv, w_out, bin_ids, pattern.transpose(2, 0, 1))
    result, grad_input, own_qkv, own_out = pl.pallas_call(
        finish,
        out_shape=shapes
        + (
            jax.ShapeDtypeStruct((3 * HD, D), F32),
            jax.ShapeDtypeStruct((HD, D), F32),
        ),
        in_specs=[vmem, vmem, vmem],
        out_specs=(vmem, vmem, vmem, vmem),
        name="finish",
    )(*parts)
    return (result[None], grad_input[None], own_qkv.T, own_out)


def solution(mesh):
    return jax.shard_map(
        body,
        mesh=mesh,
        in_specs=(
            P("dp", ("seq", "head"), None),
            P("dp", None),
            P("dp", None, None),
            P(),
            P(),
            P(),
            P("dp", ("seq", "head"), None),
        ),
        out_specs=(
            P("dp", ("seq", "head"), None),
            P("dp", ("seq", "head"), None),
            P(None, "head"),
            P("head", None),
        ),
        check_vma=False,
    )
```

```python
import functools
import math

import jax
import jax.numpy as jnp
from jax import lax
from jax.experimental import pallas as pl
from jax.experimental.pallas import tpu as pltpu
from jax.sharding import PartitionSpec as P

D = 512
HEADS = 8
HD = 64
BLK = 128
NNZ = 9
PER = 8
NB = 64
EPSILON = 1e-05
LOG2E = math.log2(math.e)
MESH = pl.DeviceIdType.MESH
F32 = jnp.float32
BF16 = jnp.bfloat16
CAT = NNZ * BLK

BATCHES = ((0, 1), (1, 2), (3, 2), (5, 2), (7, 1))

(
    Z_BQO, Z_BKV, Z_S3A, Z_S3B, G_ST, G_S1A, G_S1B, G_S4A, G_S4B,
) = range(9)


def dot_nn(a, b):
    return lax.dot_general(a, b, (((1,), (0,)), ((), ())), preferred_element_type=F32)


def dot_nt(a, b):
    return lax.dot_general(a, b, (((1,), (1,)), ((), ())), preferred_element_type=F32)


def place(rel):
    return jnp.where(rel == 0, 0, jnp.where(rel <= 4, 2 * rel - 1, 16 - 2 * rel))


def tile(n):
    return slice(n * BLK, (n + 1) * BLK)


def kernel(
    bias_ref, tok_hbm, gout_hbm, wqkv_hbm, wout_hbm, bins_hbm, pat_hbm,
    out_ref, gtok_ref, fin,
    gkv, gqd, hid, gog, tok, tok_in, gout_in, bins_in, pat_in, wqkv, wout, bins, patv, pat, wcat, wo2, normed_ref, spread_ref,
    ycats, ycat, probs, sd, pd, a2, stcol, strow, stg, deltas, invs, binsf, binst,
    obuf, bqo, bkv, rqo, rkv, dtqo, dtkv,
    wpart, ars, arr, dpx, zbc, att, gp, res, gres,
    ss, rr, ys, yr, zs, zr, xs, xr, xe, ins, sws, swr,
):
    dp = lax.axis_index("dp")
    z = lax.axis_index("seq")
    head = lax.axis_index("head")
    yhi, c = dp // 2, lax.rem(dp, 2)
    x, ylo = head // 2, lax.rem(head, 2)
    r = 2 * x + c
    seqno = 2 * yhi + ylo
    moved = c != ylo
    odd = lax.rem(z, 2) == 1
    factor = 1.0 / math.sqrt(HD)
    c2 = factor * LOG2E

    def mod8(v):
        return lax.rem(v + 16, 8)

    def device(xx, cc):
        return {"dp": 2 * yhi + cc, "head": 2 * xx + ylo}

    partner = {"dp": 2 * yhi + ylo, "head": 2 * x + c}
    sibling = {"dp": 2 * yhi + (1 - c)}

    def member(d):
        dx, dc = d // 2, d % 2
        xx = lax.rem(x + dx, 4)
        cc = c if dc == 0 else 1 - c
        return xx, cc

    def giver(d):
        dx, dc = d // 2, d % 2
        xx = lax.rem(x + 4 - dx, 4)
        cc = c if dc == 0 else 1 - c
        return 2 * xx + cc

    def remote(src, dst, ssem, rsem, dev):
        return pltpu.make_async_remote_copy(
            src_ref=src, dst_ref=dst, send_sem=ssem, recv_sem=rsem,
            device_id=dev, device_id_type=MESH,
        )

    def start(copy):
        copy.start()
        return copy

    def wait_bytes(ref, sem):
        pltpu.make_async_copy(ref, ref, sem).wait()

    def when(cond, fn):
        pl.when(cond)(fn)

    barrier = pltpu.get_barrier_semaphore()

    def greet(dev):
        pl.semaphore_signal(barrier, inc=1, device_id=dev, device_id_type=MESH)

    for d in (1, 7):
        greet({"seq": mod8(z + d)})
    for d in (1, 2, 3):
        greet(device(lax.rem(x + d, 4), c))
        greet(device(lax.rem(x + d, 4), 1 - c))
    greet(sibling)
    others = []
    for e in range(1, 4):
        yh = yhi if e // 2 == 0 else 1 - yhi
        yl = ylo if e % 2 == 0 else 1 - ylo
        others.append({"dp": 2 * yh + c, "head": 2 * x + yl})
        greet(others[-1])
    when(moved, lambda: greet(partner))

    weights = [
        pltpu.make_async_copy(wqkv_hbm, wqkv, ins.at[0]),
        pltpu.make_async_copy(wout_hbm, wout, ins.at[1]),
    ]
    loads = [
        pltpu.make_async_copy(tok_hbm, tok_in, ins.at[2]),
        pltpu.make_async_copy(gout_hbm, gout_in, ins.at[3]),
        pltpu.make_async_copy(bins_hbm, bins_in, ins.at[4]),
        pltpu.make_async_copy(pat_hbm, pat_in, ins.at[5]),
    ]
    halves = [pl.ds(0, 64), pl.ds(64, 64)]
    go_tok = [
        remote(tok_in.at[rows], tok.at[rows], sws.at[sem], swr.at[sem], partner)
        for rows, sem in zip(halves, (0, 6))
    ]
    go_grad = remote(gout_in, gog.at[0], sws.at[1], swr.at[1], partner)
    share = [
        remote(bins_in, bins, sws.at[2], swr.at[2], sibling),
        remote(pat_in, patv, sws.at[5], swr.at[5], sibling),
    ]
    for copy in loads + weights:
        copy.start()
    stays = jnp.logical_not(moved)

    lane = lax.broadcasted_iota(jnp.int32, (BLK, 2 * HD), 1)
    low = lane < HD

    def swap(v):
        return pltpu.roll(v, HD, 1)

    for copy in weights:
        copy.wait()
    pair = pl.multiple_of((z // 2) * 384, 128)
    for q in range(4):
        rows = slice(128 * q, 128 * (q + 1))
        w0 = wqkv[rows, pl.ds(pair, 128)].astype(F32)
        w1 = wqkv[rows, pl.ds(pair + 128, 128)].astype(F32)
        w2 = wqkv[rows, pl.ds(pair + 256, 128)].astype(F32)
        s1 = swap(w1)
        wcat[rows, 0:128] = jnp.where(odd, w2, jnp.where(low, swap(w0), s1)).astype(BF16)
        wcat[rows, 128:256] = jnp.where(low, jnp.where(odd, s1, w0), 0.0).astype(BF16)
    wo_pair = wout[pl.ds(pl.multiple_of((z // 2) * 128, 128), 128), :]
    wo2[0:HD, :] = jnp.zeros((HD, D), BF16)
    wo2[HD:BLK, :] = jnp.where(odd, wo_pair[HD:BLK, :], wo_pair[0:HD, :])

    for copy in loads:
        copy.wait()

    def keep(dst, src):
        def fn():
            dst[...] = src[...]

        when(stays, fn)

    keep(tok, tok_in)
    keep(gog.at[0], gout_in)
    keep(bins, bins_in)
    keep(patv, pat_in)

    pl.semaphore_wait(barrier, 12 + jnp.where(moved, 1, 0))

    def exchange():
        for copy in go_tok:
            copy.start()
            copy.wait_send()
        go_grad.start()

    when(moved, exchange)

    rings = (hid, gog)
    table = {}

    def hop(k, way, t, part):
        if way == 0:
            src, dst = (0 if t == 1 else 2 * (t - 1)), (2 * t if t < 4 else 7)
        else:
            src, dst = (0 if t == 1 else 2 * (t - 1) - 1), 2 * t - 1
        rows = pl.ds(64 * part, 64)
        return remote(
            rings[k].at[src, rows], rings[k].at[dst, rows],
            zs.at[k], zr.at[k, way, t - 1, part],
            {"seq": mod8(z + 1) if way == 0 else mod8(z - 1)},
        )

    def first_hop(k):
        for part in (0, 1):
            for way in (0, 1):
                table[k, way, 1, part] = start(hop(k, way, 1, part))

    def next_hop(k, t):
        for part in (0, 1):
            for way in (0, 1):
                table[k, way, t, part].wait_recv()
                if t + 1 < 4 or part == way:
                    table[k, way, t + 1, part] = start(hop(k, way, t + 1, part))

    def last_hop(k):
        for way in (0, 1):
            table[k, way, 4, way].wait_recv()

    pools = (gkv, gqd)
    ring_x = {}
    x_right, x_left = lax.rem(x + 1, 4), lax.rem(x + 3, 4)
    x_far = lax.rem(x + 2, 4)

    gates = {0: 0, 1: 1, 5: 2}

    def xcopy(k, b, kind, owner, dev):
        first, count = BATCHES[b]
        part = pools[k].at[owner, pl.ds(first, count)]
        rsem = xr.at[k, b, gates[kind]] if kind in gates else xe.at[k]
        ring_x[k, b, kind] = start(remote(part, part, xs.at[k], rsem, dev))

    def x_own(k, b):
        xcopy(k, b, 0, r, device(x_right, c))
        xcopy(k, b, 1, r, device(x_left, c))
        xcopy(k, b, 2, r, sibling)
        if b >= 2:
            xcopy(k, b, 5, r, device(x_far, c))
        if b == 4:
            xcopy(k, b, 3, r, device(x_right, 1 - c))
            xcopy(k, b, 4, r, device(x_left, 1 - c))
            xcopy(k, b, 6, r, device(x_far, 1 - c))

    def x_pass(k, b):
        ring_x[k, b, 0].wait_recv()
        if b == 0:
            xcopy(k, b, 5, 2 * x_left + c, device(x_right, c))
        if b < 4:
            xcopy(k, b, 3, 2 * x_left + c, sibling)
        ring_x[k, b, 1].wait_recv()
        if b == 1:
            xcopy(k, b, 5, 2 * x_right + c, device(x_left, c))
        if b < 4:
            xcopy(k, b, 4, 2 * x_right + c, sibling)

    def x_far_pass(k, b):
        ring_x[k, b, 5].wait_recv()
        if b < 4:
            xcopy(k, b, 6, 2 * x_far + c, sibling)

    def x_end(k):
        wait_bytes(pools[k].at[pl.ds(0, 4)], xe.at[k])

    def project(b):
        first, count = BATCHES[b]
        for p in range(first, first + count):
            t = dot_nn(hid[p], wcat[...]).astype(BF16)
            gkv[r, p] = t[:, 0:128]
            gqd[r, p] = t[:, 128:256]
        x_own(0, b)

    def project_grad(b):
        first, count = BATCHES[b]
        for p in range(first, first + count):
            u = dot_nt(gog[p], wo2[...])
            gqd[r, p] = jnp.where(low, gqd[r, p], u.astype(BF16))
        x_own(1, b)

    for part, rows in enumerate(halves):
        when(moved, lambda: go_tok[part].wait_recv())
        tokens = tok[rows, :].astype(F32)
        spread = jnp.sqrt(jnp.mean(tokens * tokens, axis=-1, keepdims=True) + EPSILON)
        normed = tokens / spread
        normed_ref[rows, :] = normed
        spread_ref[rows, :] = spread
        hid[0, rows, :] = normed.astype(BF16)
        for way in (0, 1):
            table[0, way, 1, part] = start(hop(0, way, 1, part))
    when(stays, lambda: [copy.start() for copy in share] and None)
    project(0)
    when(moved, lambda: go_grad.wait_recv())
    first_hop(1)
    project_grad(0)

    when(moved, lambda: [copy.wait_recv() for copy in share] and None)
    to_scalars = pltpu.make_async_copy(patv, pat, ins.at[8])
    to_scalars.start()
    for q in range(NB):
        binsf[q : q + 1, :] = bins[:, tile(q)].astype(F32)
    binst[...] = jnp.concatenate([binsf[...], jnp.zeros((BLK - NB, BLK), F32)], axis=0).T
    to_scalars.wait()

    next_hop(0, 1)
    project(1)
    x_pass(0, 0)
    next_hop(1, 1)
    project_grad(1)
    x_far_pass(0, 0)
    next_hop(0, 2)
    project(2)
    x_pass(0, 1)
    x_pass(1, 0)
    next_hop(1, 2)
    project_grad(2)
    x_far_pass(0, 1)
    x_pass(1, 1)
    x_far_pass(1, 0)
    next_hop(0, 3)
    project(3)
    x_pass(0, 2)
    x_far_pass(0, 2)
    x_far_pass(1, 1)
    next_hop(1, 3)
    project_grad(3)
    last_hop(0)
    project(4)
    x_pass(1, 2)
    x_far_pass(1, 2)
    x_pass(0, 3)
    x_far_pass(0, 3)
    last_hop(1)
    project_grad(4)
    x_pass(0, 4)
    x_far_pass(0, 4)
    x_pass(1, 3)
    x_far_pass(1, 3)
    x_end(0)

    bias2 = bias_ref[z] * LOG2E

    def distance(p):
        t = (p + 1) // 2
        return jnp.where(lax.rem(p, 2) == 1, t, 8 - t)

    def own_block(p):
        return 8 * mod8(z + distance(p)) + r

    def back(kind, src, dst, d):
        return remote(src, dst, ss.at[kind], rr.at[kind], {"seq": mod8(z + d)})

    def leave(kind, buf, dst, p):
        when(p > 0, lambda: back(kind, buf.at[p], dst.at[z], distance(p)).start())

    def used_block(row, n):
        other = lax.rem(row + pat[n, 0, 0], NB)
        return other, lax.rem(other, 8), place(mod8(other // 8 - z))

    def own_bins(row):
        return jnp.sum(jnp.where(lane == row, binst[...], 0.0), axis=1, keepdims=True)

    stcol[...] = jnp.zeros((BLK, BLK), F32)

    def forward_block(p, carry):
        row = own_block(p)
        for n in range(NNZ):
            _, rn, pn = used_block(row, n)
            ycats[p, tile(n), :] = gkv[rn, pn]
        query = gqd[r, p]
        sd[0:BLK, :] = dot_nt(jnp.where(low, query, jnp.zeros_like(query)), ycats[p])
        bin_col = own_bins(row)
        top = None
        for n in range(NNZ):
            other, _, _ = used_block(row, n)
            bin_row = binsf[pl.ds(other, 1), :]
            v = sd[0:BLK, tile(n)] * c2 + jnp.where(bin_col == bin_row, bias2, 0.0)
            sd[0:BLK, tile(n)] = v
            top = v if top is None else jnp.maximum(top, v)
        m = jnp.max(top, axis=1, keepdims=True)
        total = jnp.zeros((BLK, BLK), F32)
        for n in range(NNZ):
            e = jnp.exp2(sd[0:BLK, tile(n)] - m)
            probs[p, :, tile(n)] = e
            pd[0:BLK, tile(n)] = e.astype(BF16)
            total = total + e
        total = jnp.sum(total, axis=1, keepdims=True)
        inv = 1.0 / total
        obuf[p] = (dot_nn(pd[0:BLK, :], ycats[p]) * inv).astype(BF16)
        invs[p] = inv
        stcol[...] = jnp.where(lane == 2 * p, m + jnp.log2(total), stcol[...])
        return carry

    lax.fori_loop(0, PER, forward_block, 0)
    x_pass(1, 4)
    x_far_pass(1, 4)

    for p in range(PER):
        both = gqd[r, p].astype(F32) * obuf[p].astype(F32)
        delta = jnp.sum(jnp.where(low, 0.0, both), axis=1, keepdims=True)
        deltas[p] = delta
        stcol[...] = jnp.where(lane == 2 * p + 1, delta, stcol[...])
    strow[...] = stcol[...].T
    mine = stg.at[pl.ds(pl.multiple_of(2 * PER * r, 16), 16)]
    stg[pl.ds(pl.multiple_of(2 * PER * r, 16), 16), :] = strow[0:16, :]

    def group(kind, d, src, dst):
        start(remote(src, dst, ss.at[kind], rr.at[kind], device(*member(d))))

    for d in range(1, 8):
        group(G_ST, d, mine, mine)

    def query_block(p, carry):
        block = gqd[r, p]
        sd[0:BLK, :] = dot_nt(jnp.where(low, jnp.zeros_like(block), block), ycats[p])
        delta = deltas[p]
        for n in range(NNZ):
            pd[0:BLK, tile(n)] = (
                probs[p, :, tile(n)] * (sd[0:BLK, tile(n)] - delta)
            ).astype(BF16)
        grad = dot_nn(pd[0:BLK, :], ycats[p]) * (invs[p] * factor)
        both = jnp.where(low, grad, obuf[p].astype(F32))
        bqo[p] = both.astype(BF16)
        leave(Z_BQO, bqo, rqo, p)
        dtqo[:, pl.ds(pl.multiple_of(p * BLK, BLK), BLK)] = both.T.astype(BF16)
        return carry

    lax.fori_loop(0, PER, query_block, 0)

    rqo[z] = bqo[0]

    def stage1(k, part):
        wpart[k] = part
        for q in range(8):
            ars[k, q] = part[16 * q : 16 * (q + 1), :].astype(BF16)
        for d in range(1, 8):
            xx, cc = member(d)
            group((G_S1A, G_S1B)[k], d, ars.at[k, 2 * xx + cc], arr.at[k, r])

    def stage2(k):
        wait_bytes(arr.at[k, pl.ds(0, 7)], rr.at[(G_S1A, G_S1B)[k]])
        total = wpart[k, pl.ds(pl.multiple_of(16 * r, 16), 16), :]
        for d in range(1, 8):
            total = total + arr[k, giver(d)].astype(F32)
        dpx[k, seqno] = total.astype(BF16)
        slot = dpx.at[k, seqno]
        for e in range(1, 4):
            start(remote(slot, slot, ys.at[k], yr.at[k], others[e - 1]))

    mine_here = lax.rem(z, 2) == ylo
    not_here = jnp.logical_not(mine_here)

    def stage3(k):
        wait_bytes(dpx.at[k, pl.ds(0, 3)], yr.at[k])
        total = dpx[k, 0].astype(F32)
        for q in range(1, 4):
            total = total + dpx[k, q].astype(F32)
        slot = zbc.at[k, z // 2]
        kind = (Z_S3A, Z_S3B)[k]

        def spread_out():
            zbc[k, z // 2] = total.astype(BF16)
            for d in range(1, 8):
                remote(slot, slot, ss.at[kind], rr.at[kind], {"seq": mod8(z + d)}).start()

        when(mine_here, spread_out)

    def stage4(k):
        kind = (Z_S3A, Z_S3B)[k]
        when(mine_here, lambda: wait_bytes(zbc.at[k, pl.ds(0, 3)], rr.at[kind]))
        when(not_here, lambda: wait_bytes(zbc.at[k, pl.ds(0, 4)], rr.at[kind]))
        fin[k, r] = zbc[k, x]
        for d in range(1, 8):
            xx, _ = member(d)
            group((G_S4A, G_S4B)[k], d, zbc.at[k, xx], fin.at[k, r])

    hid_all = hid[...].reshape(PER * BLK, D)
    go_all = gog[...].reshape(PER * BLK, D)
    part0 = jnp.concatenate(
        [dot_nn(dtqo[0:HD, :], hid_all), dot_nn(dtqo[HD : 2 * HD, :], go_all)], axis=0
    )
    stage1(0, part0)
    wait_bytes(stg.at[pl.ds(0, 7 * 16)], rr.at[G_ST])
    x_end(1)

    def key_block(p, carry):
        row = own_block(p)
        for n in range(NNZ):
            _, rn, pn = used_block(row, n)
            ycat[tile(n), :] = gqd[rn, pn]
        block = gkv[r, p]
        zero = jnp.zeros_like(block)
        a2[0:BLK, :] = jnp.where(low, block, zero)
        a2[BLK : 2 * BLK, :] = jnp.where(low, zero, block)
        sd[...] = dot_nt(a2[...], ycat[...])
        bin_col = own_bins(row)
        for n in range(NNZ):
            other, rn, pn = used_block(row, n)
            bin_row = binsf[pl.ds(other, 1), :]
            log_row = stg[pl.ds(16 * rn + 2 * pn, 1), :]
            delta_row = stg[pl.ds(16 * rn + 2 * pn + 1, 1), :]
            v = sd[0:BLK, tile(n)] * c2 + jnp.where(bin_col == bin_row, bias2, 0.0)
            e = jnp.exp2(v - log_row)
            pd[0:BLK, tile(n)] = e.astype(BF16)
            pd[BLK : 2 * BLK, tile(n)] = (e * (sd[BLK : 2 * BLK, tile(n)] - delta_row)).astype(BF16)
        g = dot_nn(pd[...], ycat[...])
        both = jnp.where(low, g[BLK : 2 * BLK] * factor, g[0:BLK])
        bkv[p] = both.astype(BF16)
        leave(Z_BKV, bkv, rkv, p)
        dtkv[:, pl.ds(pl.multiple_of(p * BLK, BLK), BLK)] = both.T.astype(BF16)
        return carry

    lax.fori_loop(0, PER, key_block, 0)

    rkv[z] = bkv[0]
    stage1(1, dot_nn(dtkv[...], hid[...].reshape(PER * BLK, D)))
    stage2(0)

    def deliver(src, dst, k):
        there = remote(src, dst, sws.at[3 + k], swr.at[3 + k], partner)
        keep(dst, src)
        when(moved, lambda: there.start())
        return there

    wait_bytes(rqo.at[pl.ds(0, 7)], rr.at[Z_BQO])
    for g in range(HEADS // 2):
        even, uneven = rqo[2 * g].astype(F32), rqo[2 * g + 1].astype(F32)
        att[:, tile(g)] = jnp.where(low, swap(even), uneven).astype(BF16)
    res[...] = dot_nn(att[...], wout[...]).astype(BF16)
    d_out = deliver(res, out_ref, 0)
    stage2(1)
    stage3(0)
    stage3(1)
    stage4(0)

    wait_bytes(rkv.at[pl.ds(0, 7)], rr.at[Z_BKV])
    for g in range(HEADS // 2):
        qo_even, qo_odd = rqo[2 * g].astype(F32), rqo[2 * g + 1].astype(F32)
        kv_even = swap(rkv[2 * g].astype(F32))
        gp[:, tile(3 * g)] = jnp.where(low, qo_even, kv_even).astype(BF16)
        gp[:, tile(3 * g + 1)] = jnp.where(low, kv_even, swap(qo_odd)).astype(BF16)
        gp[:, tile(3 * g + 2)] = rkv[2 * g + 1]
    grad_hidden = dot_nt(gp[...], wqkv[...])
    normed = normed_ref[...]
    inner = jnp.mean(grad_hidden * normed, axis=-1, keepdims=True)
    gres[...] = ((grad_hidden - normed * inner) / spread_ref[...]).astype(BF16)
    d_gtok = deliver(gres, gtok_ref, 1)
    stage4(1)

    for k in (0, 1):
        wait_bytes(fin.at[k, pl.ds(0, 7)], rr.at[(G_S4A, G_S4B)[k]])
    for k in (0, 1):
        wait_bytes(rings[k].at[pl.ds(0, 7)], zs.at[k])
        wait_bytes(pools[k].at[pl.ds(0, 7)], xs.at[k])
        wait_bytes(dpx.at[k, pl.ds(0, 3)], ys.at[k])
        wait_bytes(arr.at[k, pl.ds(0, 7)], ss.at[(G_S1A, G_S1B)[k]])
        wait_bytes(arr.at[k, pl.ds(0, 7)], ss.at[(G_S4A, G_S4B)[k]])
    wait_bytes(rqo.at[pl.ds(0, 7)], ss.at[Z_BQO])
    wait_bytes(rkv.at[pl.ds(0, 7)], ss.at[Z_BKV])
    wait_bytes(stg.at[pl.ds(0, 7 * 16)], ss.at[G_ST])

    def spread_sent():
        for kind in (Z_S3A, Z_S3B):
            wait_bytes(arr.at[0, pl.ds(0, 7)], ss.at[kind])

    when(mine_here, spread_sent)
    when(moved, lambda: go_grad.wait_send())
    when(stays, lambda: [copy.wait_send() for copy in share] and None)
    for there in (d_out, d_gtok):
        when(moved, lambda: there.wait())


def finish(out_in, gtok_in, fin_ref, out_ref, gtok_ref, gqkv_ref, gwo_ref):
    out_ref[...] = out_in[...]
    gtok_ref[...] = gtok_in[...]
    first = fin_ref[0].reshape(BLK, D).astype(F32)
    second = fin_ref[1].reshape(BLK, D).astype(F32)
    gwo_ref[...] = first[HD : 2 * HD, :]
    gqkv_ref[0:HD, :] = first[0:HD, :]
    gqkv_ref[HD : 3 * HD, :] = second


def body(tokens, bin_ids, pattern, w_qkv, w_out, head_bias, grad_output):
    vmem = pl.BlockSpec(memory_space=pltpu.VMEM)
    smem = pl.BlockSpec(memory_space=pltpu.SMEM)
    hbm = pl.BlockSpec(memory_space=pltpu.HBM)
    dma = pltpu.SemaphoreType.DMA
    half = functools.partial(pltpu.VMEM, dtype=BF16)
    full = functools.partial(pltpu.VMEM, dtype=F32)
    scratch = [
        half((8, 8, BLK, 128)),
        half((8, 8, BLK, 128)),
        half((8, BLK, D)),
        half((8, BLK, D)),
        half((BLK, D)),
        half((BLK, D)),
        half((BLK, D)),
        pltpu.VMEM((1, NB * BLK), jnp.int32),
        pltpu.VMEM((NNZ, 1, NB), jnp.int32),
        half((D, 3 * D)),
        half((D, D)),
        pltpu.VMEM((1, NB * BLK), jnp.int32),
        pltpu.VMEM((NNZ, 1, NB), jnp.int32),
        pltpu.SMEM((NNZ, 1, NB), jnp.int32),
        half((D, 256)),
        half((BLK, D)),
        full((BLK, D)),
        full((BLK, 1)),
        half((PER, CAT, 128)),
        half((CAT, 128)),
        full((PER, BLK, CAT)),
        full((2 * BLK, CAT)),
        half((2 * BLK, CAT)),
        half((2 * BLK, 128)),
        full((BLK, BLK)),
        full((BLK, BLK)),
        full((2 * NB, BLK)),
        full((PER, BLK, 1)),
        full((PER, BLK, 1)),
        full((NB, BLK)),
        full((BLK, BLK)),
        half((8, BLK, 128)),
        half((8, BLK, 128)),
        half((8, BLK, 128)),
        half((8, BLK, 128)),
        half((8, BLK, 128)),
        half((BLK, PER * BLK)),
        half((BLK, PER * BLK)),
        full((2, BLK, D)),
        half((2, 8, 16, D)),
        half((2, 8, 16, D)),
        half((2, 4, 16, D)),
        half((2, 4, 16, D)),
        half((BLK, D)),
        half((BLK, 3 * D)),
        half((BLK, D)),
        half((BLK, D)),
        dma((9,)),
        dma((9,)),
        dma((2,)),
        dma((2,)),
        dma((2,)),
        dma((2, 2, 4, 2)),
        dma((2,)),
        dma((2, 5, 3)),
        dma((2,)),
        dma((9,)),
        dma((7,)),
        dma((7,)),
    ]
    shapes = (
        jax.ShapeDtypeStruct((BLK, D), BF16),
        jax.ShapeDtypeStruct((BLK, D), BF16),
    )
    parts = pl.pallas_call(
        kernel,
        out_shape=shapes + (jax.ShapeDtypeStruct((2, 8, 16, D), BF16),),
        in_specs=[smem, hbm, hbm, hbm, hbm, hbm, hbm],
        out_specs=(vmem, vmem, vmem),
        scratch_shapes=scratch,
        compiler_params=pltpu.CompilerParams(
            collective_id=0, has_side_effects=True, vmem_limit_bytes=62 * 1024 * 1024
        ),
        name="layer",
    )(head_bias, tokens[0], grad_output[0], w_qkv, w_out, bin_ids, pattern.transpose(2, 0, 1))
    result, grad_input, own_qkv, own_out = pl.pallas_call(
        finish,
        out_shape=shapes
        + (
            jax.ShapeDtypeStruct((3 * HD, D), F32),
            jax.ShapeDtypeStruct((HD, D), F32),
        ),
        in_specs=[vmem, vmem, vmem],
        out_specs=(vmem, vmem, vmem, vmem),
        name="finish",
    )(*parts)
    return (result[None], grad_input[None], own_qkv.T, own_out)


def solution(mesh):
    return jax.shard_map(
        body,
        mesh=mesh,
        in_specs=(
            P("dp", ("seq", "head"), None),
            P("dp", None),
            P("dp", None, None),
            P(),
            P(),
            P(),
            P("dp", ("seq", "head"), None),
        ),
        out_specs=(
            P("dp", ("seq", "head"), None),
            P("dp", ("seq", "head"), None),
            P(None, "head"),
            P("head", None),
        ),
        check_vma=False,
    )
```

```python
import functools
import math

import jax
import jax.numpy as jnp
from jax import lax
from jax.experimental import pallas as pl
from jax.experimental.pallas import tpu as pltpu
from jax.sharding import PartitionSpec as P

D = 512
HEADS = 8
HD = 64
BLK = 128
NNZ = 9
PER = 8
NB = 64
EPSILON = 1e-05
LOG2E = math.log2(math.e)
MESH = pl.DeviceIdType.MESH
F32 = jnp.float32
BF16 = jnp.bfloat16
CAT = NNZ * BLK

BATCHES = ((0, 1), (1, 2), (3, 2), (5, 2), (7, 1))

(
    Z_BQO, Z_BKV, Z_S3A, Z_S3B, G_ST, G_S1A, G_S1B, G_S4A, G_S4B,
) = range(9)


def dot_nn(a, b):
    return lax.dot_general(a, b, (((1,), (0,)), ((), ())), preferred_element_type=F32)


def dot_nt(a, b):
    return lax.dot_general(a, b, (((1,), (1,)), ((), ())), preferred_element_type=F32)


def place(rel):
    return jnp.where(rel == 0, 0, jnp.where(rel <= 4, 2 * rel - 1, 16 - 2 * rel))


def tile(n):
    return slice(n * BLK, (n + 1) * BLK)


def kernel(
    bias_ref, tok_hbm, gout_hbm, wqkv_hbm, wout_hbm, bins_hbm, pat_hbm,
    out_ref, gtok_ref, fin,
    gkv, gqd, hid, gog, tok, tok_in, gout_in, bins_in, pat_in, wqkv, wout, bins, patv, pat, wcat, wo2, normed_ref, spread_ref,
    ycats, ycat, probs, sd, pd, a2, stcol, strow, stg, deltas, invs, binsf, binst,
    obuf, bqo, bkv, rqo, rkv, dtqo, dtkv,
    wpart, ars, arr, dpx, zbc, att, gp, res, gres,
    ss, rr, ys, yr, zs, zr, xs, xr, xe, ins, sws, swr,
):
    dp = lax.axis_index("dp")
    z = lax.axis_index("seq")
    head = lax.axis_index("head")
    yhi, c = dp // 2, lax.rem(dp, 2)
    x, ylo = head // 2, lax.rem(head, 2)
    r = 2 * x + c
    seqno = 2 * yhi + ylo
    moved = c != ylo
    odd = lax.rem(z, 2) == 1
    factor = 1.0 / math.sqrt(HD)
    c2 = factor * LOG2E

    def mod8(v):
        return lax.rem(v + 16, 8)

    def device(xx, cc):
        return {"dp": 2 * yhi + cc, "head": 2 * xx + ylo}

    partner = {"dp": 2 * yhi + ylo, "head": 2 * x + c}
    sibling = {"dp": 2 * yhi + (1 - c)}

    def member(d):
        dx, dc = d // 2, d % 2
        xx = lax.rem(x + dx, 4)
        cc = c if dc == 0 else 1 - c
        return xx, cc

    def giver(d):
        dx, dc = d // 2, d % 2
        xx = lax.rem(x + 4 - dx, 4)
        cc = c if dc == 0 else 1 - c
        return 2 * xx + cc

    def remote(src, dst, ssem, rsem, dev):
        return pltpu.make_async_remote_copy(
            src_ref=src, dst_ref=dst, send_sem=ssem, recv_sem=rsem,
            device_id=dev, device_id_type=MESH,
        )

    def start(copy):
        copy.start()
        return copy

    def wait_bytes(ref, sem):
        pltpu.make_async_copy(ref, ref, sem).wait()

    def when(cond, fn):
        pl.when(cond)(fn)

    barrier = pltpu.get_barrier_semaphore()

    def greet(dev):
        pl.semaphore_signal(barrier, inc=1, device_id=dev, device_id_type=MESH)

    for d in (1, 7):
        greet({"seq": mod8(z + d)})
    for d in (1, 2, 3):
        greet(device(lax.rem(x + d, 4), c))
    greet(sibling)
    others = []
    for e in range(1, 4):
        yh = yhi if e // 2 == 0 else 1 - yhi
        yl = ylo if e % 2 == 0 else 1 - ylo
        others.append({"dp": 2 * yh + c, "head": 2 * x + yl})
        greet(others[-1])
    when(moved, lambda: greet(partner))

    weights = [
        pltpu.make_async_copy(wqkv_hbm, wqkv, ins.at[0]),
        pltpu.make_async_copy(wout_hbm, wout, ins.at[1]),
    ]
    loads = [
        pltpu.make_async_copy(tok_hbm, tok_in, ins.at[2]),
        pltpu.make_async_copy(gout_hbm, gout_in, ins.at[3]),
        pltpu.make_async_copy(bins_hbm, bins_in, ins.at[4]),
        pltpu.make_async_copy(pat_hbm, pat_in, ins.at[5]),
    ]
    go = [
        remote(tok_in, tok, sws.at[0], swr.at[0], partner),
        remote(gout_in, gog.at[0], sws.at[1], swr.at[1], partner),
    ]
    share = [
        remote(bins_in, bins, sws.at[2], swr.at[2], sibling),
        remote(pat_in, patv, sws.at[5], swr.at[5], sibling),
    ]
    for copy in loads + weights:
        copy.start()
    stays = jnp.logical_not(moved)

    lane = lax.broadcasted_iota(jnp.int32, (BLK, 2 * HD), 1)
    low = lane < HD

    def swap(v):
        return pltpu.roll(v, HD, 1)

    for copy in weights:
        copy.wait()
    pair = pl.multiple_of((z // 2) * 384, 128)
    for q in range(4):
        rows = slice(128 * q, 128 * (q + 1))
        w0 = wqkv[rows, pl.ds(pair, 128)].astype(F32)
        w1 = wqkv[rows, pl.ds(pair + 128, 128)].astype(F32)
        w2 = wqkv[rows, pl.ds(pair + 256, 128)].astype(F32)
        s1 = swap(w1)
        wcat[rows, 0:128] = jnp.where(odd, w2, jnp.where(low, swap(w0), s1)).astype(BF16)
        wcat[rows, 128:256] = jnp.where(low, jnp.where(odd, s1, w0), 0.0).astype(BF16)
    wo_pair = wout[pl.ds(pl.multiple_of((z // 2) * 128, 128), 128), :]
    wo2[0:HD, :] = jnp.zeros((HD, D), BF16)
    wo2[HD:BLK, :] = jnp.where(odd, wo_pair[HD:BLK, :], wo_pair[0:HD, :])

    for copy in loads:
        copy.wait()

    def keep(dst, src):
        def fn():
            dst[...] = src[...]

        when(stays, fn)

    keep(tok, tok_in)
    keep(gog.at[0], gout_in)
    keep(bins, bins_in)
    keep(patv, pat_in)

    pl.semaphore_wait(barrier, 9 + jnp.where(moved, 1, 0))
    when(moved, lambda: go[0].start())
    when(moved, lambda: go[0].wait_send())
    when(moved, lambda: go[1].start())
    when(moved, lambda: go[0].wait_recv())

    tokens = tok[...].astype(F32)
    spread = jnp.sqrt(jnp.mean(tokens * tokens, axis=-1, keepdims=True) + EPSILON)
    normed = tokens / spread
    normed_ref[...] = normed
    spread_ref[...] = spread
    hid[0] = normed.astype(BF16)

    rings = (hid, gog)
    table = {}

    def hop(k, way, t, part):
        if way == 0:
            src, dst = (0 if t == 1 else 2 * (t - 1)), (2 * t if t < 4 else 7)
        else:
            src, dst = (0 if t == 1 else 2 * (t - 1) - 1), 2 * t - 1
        rows = pl.ds(64 * part, 64)
        return remote(
            rings[k].at[src, rows], rings[k].at[dst, rows],
            zs.at[k], zr.at[k, way, t - 1, part],
            {"seq": mod8(z + 1) if way == 0 else mod8(z - 1)},
        )

    def first_hop(k):
        for part in (0, 1):
            for way in (0, 1):
                table[k, way, 1, part] = start(hop(k, way, 1, part))

    def next_hop(k, t):
        for part in (0, 1):
            for way in (0, 1):
                table[k, way, t, part].wait_recv()
                if t + 1 < 4 or part == way:
                    table[k, way, t + 1, part] = start(hop(k, way, t + 1, part))

    def last_hop(k):
        for way in (0, 1):
            table[k, way, 4, way].wait_recv()

    pools = (gkv, gqd)
    ring_x = {}
    x_right, x_left = lax.rem(x + 1, 4), lax.rem(x + 3, 4)
    x_far = lax.rem(x + 2, 4)

    gates = {0: 0, 1: 1, 5: 2}

    def xcopy(k, b, kind, owner, dev):
        first, count = BATCHES[b]
        part = pools[k].at[owner, pl.ds(first, count)]
        rsem = xr.at[k, b, gates[kind]] if kind in gates else xe.at[k]
        ring_x[k, b, kind] = start(remote(part, part, xs.at[k], rsem, dev))

    def x_own(k, b):
        xcopy(k, b, 0, r, device(x_right, c))
        xcopy(k, b, 1, r, device(x_left, c))
        xcopy(k, b, 2, r, sibling)
        xcopy(k, b, 5, r, device(x_far, c))

    def x_pass(k, b):
        ring_x[k, b, 0].wait_recv()
        xcopy(k, b, 3, 2 * x_left + c, sibling)
        ring_x[k, b, 1].wait_recv()
        xcopy(k, b, 4, 2 * x_right + c, sibling)

    def x_far_pass(k, b):
        ring_x[k, b, 5].wait_recv()
        xcopy(k, b, 6, 2 * x_far + c, sibling)

    def x_end(k):
        wait_bytes(pools[k].at[pl.ds(0, 4)], xe.at[k])

    def project(b):
        first, count = BATCHES[b]
        for p in range(first, first + count):
            t = dot_nn(hid[p], wcat[...]).astype(BF16)
            gkv[r, p] = t[:, 0:128]
            gqd[r, p] = t[:, 128:256]
        x_own(0, b)

    def project_grad(b):
        first, count = BATCHES[b]
        for p in range(first, first + count):
            u = dot_nt(gog[p], wo2[...])
            gqd[r, p] = jnp.where(low, gqd[r, p], u.astype(BF16))
        x_own(1, b)

    first_hop(0)
    when(stays, lambda: [copy.start() for copy in share] and None)
    project(0)
    when(moved, lambda: go[1].wait_recv())
    first_hop(1)
    project_grad(0)

    when(moved, lambda: [copy.wait_recv() for copy in share] and None)
    to_scalars = pltpu.make_async_copy(patv, pat, ins.at[8])
    to_scalars.start()
    for q in range(NB):
        binsf[q : q + 1, :] = bins[:, tile(q)].astype(F32)
    binst[...] = jnp.concatenate([binsf[...], jnp.zeros((BLK - NB, BLK), F32)], axis=0).T
    to_scalars.wait()

    next_hop(0, 1)
    project(1)
    x_pass(0, 0)
    next_hop(1, 1)
    project_grad(1)
    x_far_pass(0, 0)
    next_hop(0, 2)
    project(2)
    x_pass(0, 1)
    x_pass(1, 0)
    next_hop(1, 2)
    project_grad(2)
    x_far_pass(0, 1)
    x_pass(1, 1)
    x_far_pass(1, 0)
    next_hop(0, 3)
    project(3)
    x_pass(0, 2)
    x_far_pass(0, 2)
    x_far_pass(1, 1)
    next_hop(1, 3)
    project_grad(3)
    last_hop(0)
    project(4)
    x_pass(1, 2)
    x_far_pass(1, 2)
    x_pass(0, 3)
    x_far_pass(0, 3)
    last_hop(1)
    project_grad(4)
    x_pass(0, 4)
    x_far_pass(0, 4)
    x_pass(1, 3)
    x_far_pass(1, 3)
    x_end(0)

    bias2 = bias_ref[z] * LOG2E

    def distance(p):
        t = (p + 1) // 2
        return jnp.where(lax.rem(p, 2) == 1, t, 8 - t)

    def own_block(p):
        return 8 * mod8(z + distance(p)) + r

    def back(kind, src, dst, d):
        return remote(src, dst, ss.at[kind], rr.at[kind], {"seq": mod8(z + d)})

    def leave(kind, buf, dst, p):
        when(p > 0, lambda: back(kind, buf.at[p], dst.at[z], distance(p)).start())

    def used_block(row, n):
        other = lax.rem(row + pat[n, 0, 0], NB)
        return other, lax.rem(other, 8), place(mod8(other // 8 - z))

    def own_bins(row):
        return jnp.sum(jnp.where(lane == row, binst[...], 0.0), axis=1, keepdims=True)

    stcol[...] = jnp.zeros((BLK, BLK), F32)

    def forward_block(p, carry):
        row = own_block(p)
        for n in range(NNZ):
            _, rn, pn = used_block(row, n)
            ycats[p, tile(n), :] = gkv[rn, pn]
        query = gqd[r, p]
        sd[0:BLK, :] = dot_nt(jnp.where(low, query, jnp.zeros_like(query)), ycats[p])
        bin_col = own_bins(row)
        top = None
        for n in range(NNZ):
            other, _, _ = used_block(row, n)
            bin_row = binsf[pl.ds(other, 1), :]
            v = sd[0:BLK, tile(n)] * c2 + jnp.where(bin_col == bin_row, bias2, 0.0)
            sd[0:BLK, tile(n)] = v
            top = v if top is None else jnp.maximum(top, v)
        m = jnp.max(top, axis=1, keepdims=True)
        total = jnp.zeros((BLK, BLK), F32)
        for n in range(NNZ):
            e = jnp.exp2(sd[0:BLK, tile(n)] - m)
            probs[p, :, tile(n)] = e
            pd[0:BLK, tile(n)] = e.astype(BF16)
            total = total + e
        total = jnp.sum(total, axis=1, keepdims=True)
        inv = 1.0 / total
        obuf[p] = (dot_nn(pd[0:BLK, :], ycats[p]) * inv).astype(BF16)
        invs[p] = inv
        stcol[...] = jnp.where(lane == 2 * p, m + jnp.log2(total), stcol[...])
        return carry

    lax.fori_loop(0, PER, forward_block, 0)
    x_pass(1, 4)
    x_far_pass(1, 4)

    for p in range(PER):
        both = gqd[r, p].astype(F32) * obuf[p].astype(F32)
        delta = jnp.sum(jnp.where(low, 0.0, both), axis=1, keepdims=True)
        deltas[p] = delta
        stcol[...] = jnp.where(lane == 2 * p + 1, delta, stcol[...])
    strow[...] = stcol[...].T
    mine = stg.at[pl.ds(pl.multiple_of(2 * PER * r, 16), 16)]
    stg[pl.ds(pl.multiple_of(2 * PER * r, 16), 16), :] = strow[0:16, :]

    def group(kind, d, src, dst):
        start(remote(src, dst, ss.at[kind], rr.at[kind], device(*member(d))))

    for d in range(1, 8):
        group(G_ST, d, mine, mine)

    def query_block(p, carry):
        block = gqd[r, p]
        sd[0:BLK, :] = dot_nt(jnp.where(low, jnp.zeros_like(block), block), ycats[p])
        delta = deltas[p]
        for n in range(NNZ):
            pd[0:BLK, tile(n)] = (
                probs[p, :, tile(n)] * (sd[0:BLK, tile(n)] - delta)
            ).astype(BF16)
        grad = dot_nn(pd[0:BLK, :], ycats[p]) * (invs[p] * factor)
        both = jnp.where(low, grad, obuf[p].astype(F32))
        bqo[p] = both.astype(BF16)
        leave(Z_BQO, bqo, rqo, p)
        dtqo[:, pl.ds(pl.multiple_of(p * BLK, BLK), BLK)] = both.T.astype(BF16)
        return carry

    lax.fori_loop(0, PER, query_block, 0)

    rqo[z] = bqo[0]

    def stage1(k, part):
        wpart[k] = part
        for q in range(8):
            ars[k, q] = part[16 * q : 16 * (q + 1), :].astype(BF16)
        for d in range(1, 8):
            xx, cc = member(d)
            group((G_S1A, G_S1B)[k], d, ars.at[k, 2 * xx + cc], arr.at[k, r])

    def stage2(k):
        wait_bytes(arr.at[k, pl.ds(0, 7)], rr.at[(G_S1A, G_S1B)[k]])
        total = wpart[k, pl.ds(pl.multiple_of(16 * r, 16), 16), :]
        for d in range(1, 8):
            total = total + arr[k, giver(d)].astype(F32)
        dpx[k, seqno] = total.astype(BF16)
        slot = dpx.at[k, seqno]
        for e in range(1, 4):
            start(remote(slot, slot, ys.at[k], yr.at[k], others[e - 1]))

    mine_here = lax.rem(z, 2) == ylo
    not_here = jnp.logical_not(mine_here)

    def stage3(k):
        wait_bytes(dpx.at[k, pl.ds(0, 3)], yr.at[k])
        total = dpx[k, 0].astype(F32)
        for q in range(1, 4):
            total = total + dpx[k, q].astype(F32)
        slot = zbc.at[k, z // 2]
        kind = (Z_S3A, Z_S3B)[k]

        def spread_out():
            zbc[k, z // 2] = total.astype(BF16)
            for d in range(1, 8):
                remote(slot, slot, ss.at[kind], rr.at[kind], {"seq": mod8(z + d)}).start()

        when(mine_here, spread_out)

    def stage4(k):
        kind = (Z_S3A, Z_S3B)[k]
        when(mine_here, lambda: wait_bytes(zbc.at[k, pl.ds(0, 3)], rr.at[kind]))
        when(not_here, lambda: wait_bytes(zbc.at[k, pl.ds(0, 4)], rr.at[kind]))
        fin[k, r] = zbc[k, x]
        for d in range(1, 8):
            xx, _ = member(d)
            group((G_S4A, G_S4B)[k], d, zbc.at[k, xx], fin.at[k, r])

    hid_all = hid[...].reshape(PER * BLK, D)
    go_all = gog[...].reshape(PER * BLK, D)
    part0 = jnp.concatenate(
        [dot_nn(dtqo[0:HD, :], hid_all), dot_nn(dtqo[HD : 2 * HD, :], go_all)], axis=0
    )
    stage1(0, part0)
    wait_bytes(stg.at[pl.ds(0, 7 * 16)], rr.at[G_ST])
    x_end(1)

    def key_block(p, carry):
        row = own_block(p)
        for n in range(NNZ):
            _, rn, pn = used_block(row, n)
            ycat[tile(n), :] = gqd[rn, pn]
        block = gkv[r, p]
        zero = jnp.zeros_like(block)
        a2[0:BLK, :] = jnp.where(low, block, zero)
        a2[BLK : 2 * BLK, :] = jnp.where(low, zero, block)
        sd[...] = dot_nt(a2[...], ycat[...])
        bin_col = own_bins(row)
        for n in range(NNZ):
            other, rn, pn = used_block(row, n)
            bin_row = binsf[pl.ds(other, 1), :]
            log_row = stg[pl.ds(16 * rn + 2 * pn, 1), :]
            delta_row = stg[pl.ds(16 * rn + 2 * pn + 1, 1), :]
            v = sd[0:BLK, tile(n)] * c2 + jnp.where(bin_col == bin_row, bias2, 0.0)
            e = jnp.exp2(v - log_row)
            pd[0:BLK, tile(n)] = e.astype(BF16)
            pd[BLK : 2 * BLK, tile(n)] = (e * (sd[BLK : 2 * BLK, tile(n)] - delta_row)).astype(BF16)
        g = dot_nn(pd[...], ycat[...])
        both = jnp.where(low, g[BLK : 2 * BLK] * factor, g[0:BLK])
        bkv[p] = both.astype(BF16)
        leave(Z_BKV, bkv, rkv, p)
        dtkv[:, pl.ds(pl.multiple_of(p * BLK, BLK), BLK)] = both.T.astype(BF16)
        return carry

    lax.fori_loop(0, PER, key_block, 0)

    rkv[z] = bkv[0]
    stage1(1, dot_nn(dtkv[...], hid[...].reshape(PER * BLK, D)))
    stage2(0)

    def deliver(src, dst, k):
        there = remote(src, dst, sws.at[3 + k], swr.at[3 + k], partner)
        keep(dst, src)
        when(moved, lambda: there.start())
        return there

    wait_bytes(rqo.at[pl.ds(0, 7)], rr.at[Z_BQO])
    for g in range(HEADS // 2):
        even, uneven = rqo[2 * g].astype(F32), rqo[2 * g + 1].astype(F32)
        att[:, tile(g)] = jnp.where(low, swap(even), uneven).astype(BF16)
    res[...] = dot_nn(att[...], wout[...]).astype(BF16)
    d_out = deliver(res, out_ref, 0)
    stage2(1)
    stage3(0)
    stage3(1)
    stage4(0)

    wait_bytes(rkv.at[pl.ds(0, 7)], rr.at[Z_BKV])
    for g in range(HEADS // 2):
        qo_even, qo_odd = rqo[2 * g].astype(F32), rqo[2 * g + 1].astype(F32)
        kv_even = swap(rkv[2 * g].astype(F32))
        gp[:, tile(3 * g)] = jnp.where(low, qo_even, kv_even).astype(BF16)
        gp[:, tile(3 * g + 1)] = jnp.where(low, kv_even, swap(qo_odd)).astype(BF16)
        gp[:, tile(3 * g + 2)] = rkv[2 * g + 1]
    grad_hidden = dot_nt(gp[...], wqkv[...])
    normed = normed_ref[...]
    inner = jnp.mean(grad_hidden * normed, axis=-1, keepdims=True)
    gres[...] = ((grad_hidden - normed * inner) / spread_ref[...]).astype(BF16)
    d_gtok = deliver(gres, gtok_ref, 1)
    stage4(1)

    for k in (0, 1):
        wait_bytes(fin.at[k, pl.ds(0, 7)], rr.at[(G_S4A, G_S4B)[k]])
    for k in (0, 1):
        wait_bytes(rings[k].at[pl.ds(0, 7)], zs.at[k])
        wait_bytes(pools[k].at[pl.ds(0, 7)], xs.at[k])
        wait_bytes(dpx.at[k, pl.ds(0, 3)], ys.at[k])
        wait_bytes(arr.at[k, pl.ds(0, 7)], ss.at[(G_S1A, G_S1B)[k]])
        wait_bytes(arr.at[k, pl.ds(0, 7)], ss.at[(G_S4A, G_S4B)[k]])
    wait_bytes(rqo.at[pl.ds(0, 7)], ss.at[Z_BQO])
    wait_bytes(rkv.at[pl.ds(0, 7)], ss.at[Z_BKV])
    wait_bytes(stg.at[pl.ds(0, 7 * 16)], ss.at[G_ST])

    def spread_sent():
        for kind in (Z_S3A, Z_S3B):
            wait_bytes(arr.at[0, pl.ds(0, 7)], ss.at[kind])

    when(mine_here, spread_sent)
    when(moved, lambda: go[1].wait_send())
    when(stays, lambda: [copy.wait_send() for copy in share] and None)
    for there in (d_out, d_gtok):
        when(moved, lambda: there.wait())


def finish(out_in, gtok_in, fin_ref, out_ref, gtok_ref, gqkv_ref, gwo_ref):
    out_ref[...] = out_in[...]
    gtok_ref[...] = gtok_in[...]
    first = fin_ref[0].reshape(BLK, D).astype(F32)
    second = fin_ref[1].reshape(BLK, D).astype(F32)
    gwo_ref[...] = first[HD : 2 * HD, :]
    gqkv_ref[0:HD, :] = first[0:HD, :]
    gqkv_ref[HD : 3 * HD, :] = second


def body(tokens, bin_ids, pattern, w_qkv, w_out, head_bias, grad_output):
    vmem = pl.BlockSpec(memory_space=pltpu.VMEM)
    smem = pl.BlockSpec(memory_space=pltpu.SMEM)
    hbm = pl.BlockSpec(memory_space=pltpu.HBM)
    dma = pltpu.SemaphoreType.DMA
    half = functools.partial(pltpu.VMEM, dtype=BF16)
    full = functools.partial(pltpu.VMEM, dtype=F32)
    scratch = [
        half((8, 8, BLK, 128)),
        half((8, 8, BLK, 128)),
        half((8, BLK, D)),
        half((8, BLK, D)),
        half((BLK, D)),
        half((BLK, D)),
        half((BLK, D)),
        pltpu.VMEM((1, NB * BLK), jnp.int32),
        pltpu.VMEM((NNZ, 1, NB), jnp.int32),
        half((D, 3 * D)),
        half((D, D)),
        pltpu.VMEM((1, NB * BLK), jnp.int32),
        pltpu.VMEM((NNZ, 1, NB), jnp.int32),
        pltpu.SMEM((NNZ, 1, NB), jnp.int32),
        half((D, 256)),
        half((BLK, D)),
        full((BLK, D)),
        full((BLK, 1)),
        half((PER, CAT, 128)),
        half((CAT, 128)),
        full((PER, BLK, CAT)),
        full((2 * BLK, CAT)),
        half((2 * BLK, CAT)),
        half((2 * BLK, 128)),
        full((BLK, BLK)),
        full((BLK, BLK)),
        full((2 * NB, BLK)),
        full((PER, BLK, 1)),
        full((PER, BLK, 1)),
        full((NB, BLK)),
        full((BLK, BLK)),
        half((8, BLK, 128)),
        half((8, BLK, 128)),
        half((8, BLK, 128)),
        half((8, BLK, 128)),
        half((8, BLK, 128)),
        half((BLK, PER * BLK)),
        half((BLK, PER * BLK)),
        full((2, BLK, D)),
        half((2, 8, 16, D)),
        half((2, 8, 16, D)),
        half((2, 4, 16, D)),
        half((2, 4, 16, D)),
        half((BLK, D)),
        half((BLK, 3 * D)),
        half((BLK, D)),
        half((BLK, D)),
        dma((9,)),
        dma((9,)),
        dma((2,)),
        dma((2,)),
        dma((2,)),
        dma((2, 2, 4, 2)),
        dma((2,)),
        dma((2, 5, 3)),
        dma((2,)),
        dma((9,)),
        dma((6,)),
        dma((6,)),
    ]
    shapes = (
        jax.ShapeDtypeStruct((BLK, D), BF16),
        jax.ShapeDtypeStruct((BLK, D), BF16),
    )
    parts = pl.pallas_call(
        kernel,
        out_shape=shapes + (jax.ShapeDtypeStruct((2, 8, 16, D), BF16),),
        in_specs=[smem, hbm, hbm, hbm, hbm, hbm, hbm],
        out_specs=(vmem, vmem, vmem),
        scratch_shapes=scratch,
        compiler_params=pltpu.CompilerParams(
            collective_id=0, has_side_effects=True, vmem_limit_bytes=62 * 1024 * 1024
        ),
        name="layer",
    )(head_bias, tokens[0], grad_output[0], w_qkv, w_out, bin_ids, pattern.transpose(2, 0, 1))
    result, grad_input, own_qkv, own_out = pl.pallas_call(
        finish,
        out_shape=shapes
        + (
            jax.ShapeDtypeStruct((3 * HD, D), F32),
            jax.ShapeDtypeStruct((HD, D), F32),
        ),
        in_specs=[vmem, vmem, vmem],
        out_specs=(vmem, vmem, vmem, vmem),
        name="finish",
    )(*parts)
    return (result[None], grad_input[None], own_qkv.T, own_out)


def solution(mesh):
    return jax.shard_map(
        body,
        mesh=mesh,
        in_specs=(
            P("dp", ("seq", "head"), None),
            P("dp", None),
            P("dp", None, None),
            P(),
            P(),
            P(),
            P("dp", ("seq", "head"), None),
        ),
        out_specs=(
            P("dp", ("seq", "head"), None),
            P("dp", ("seq", "head"), None),
            P(None, "head"),
            P("head", None),
        ),
        check_vma=False,
    )
```
